256 devices in a mesh: segment: 8 (over y, core), row: 2 (over x_hi), dp: 16 (over z, x_lo).
Axes of the slice: x: 4 (x_hi: 2, x_lo: 2; x = x_hi * 2 + x_lo), y: 4, z: 8, core: 2. Of those that a mesh axis runs over, the one named last changes fastest.
Arguments:
- fresh: float32 [2, 16, 16, 16, 256], P(None, 'dp', 'row'), may hold values from -6 to 6
- target: float32 [1, 16, 16, 16, 256], P(None, 'dp', 'row'), may hold values from -6 to 6
- carried: float32 [8, 16, 16, 16, 256], P('segment', 'dp', 'row'), may hold values from -6 to 6
- returning: float32 [8, 2, 16, 16, 16, 256], P('segment', None, 'dp', 'row'), may hold values from -6 to 6
- weights: float32 [8, 2, 2, 1152, 128], P('segment'), may hold values from -0.09375 to 0.09375
- section_blocks: int32 [8], P('segment'), may hold values from 1 to 2, as said below
Outputs:
- grad_weights: float32 [8, 2, 2, 1152, 128], P('segment', None, None, ('row', 'dp'))
- leaving: float32 [8, 16, 16, 16, 256], P('segment', 'dp', 'row')
- sent_back: float32 [8, 2, 16, 16, 16, 256], P('segment', None, 'dp', 'row')
The draws below stay inside these ranges and needn't reach their ends.
Inputs may be any that keep to these rules, and one draw needn't show every extreme that they name: `section_blocks`: each section holds one or two blocks; some section holds two and some one.
All inputs are finite; a program needn't handle non-finite values.
Results may differ from the reference program's by a relative error of at most 0.00012.
Values sent between devices are 32-bit elements; how exact they have to be, the bound alone decides.
No kernel may reach another device: no remote copies, remote signals or barrier semaphores. Data moves between devices by JAX's collectives and lax.ppermute only.
A program may use at most 64 MiB of HBM per device.

```python
import math
import jax
import jax.numpy as jnp
from jax import lax

C = 128
BLK = 2
TICKS = 2
WD = 16
BATCH = 16
HEIGHT = 16
N_SEGMENT = 8


def draw_section_blocks(key, part):
    first_key, second_key = jax.random.split(jax.random.fold_in(key, 7))
    counts = 1 + jax.random.randint(first_key, (N_SEGMENT,), 0, 2)
    ordering = jax.random.permutation(second_key, N_SEGMENT)
    counts = counts.at[ordering[0]].set(2).at[ordering[1]].set(1)
    return counts.astype(jnp.int32)


def levels(key, dims, pieces, least, top_value):
    factor_of = 1.0
    for position, shards_of in pieces:
        heights = jax.random.uniform(jax.random.fold_in(jax.random.fold_in(key, 6), position), (shards_of,), jnp.float32, least / len(pieces), top_value / len(pieces))
        factor_of = factor_of * jnp.repeat(jnp.exp(heights), dims[position] // shards_of).reshape((-1,) + (1,) * (len(dims) - 1 - position))
    return factor_of


def gaussian(key, shape, width, bound, cuts=(), kind=jnp.bfloat16):
    result = jax.random.normal(key, shape, jnp.float32) * width
    if len(cuts) > 0:
        result = levels(key, shape, cuts, -0.22, 0.18) * result
    return jnp.clip(result, min=-bound, max=bound).astype(kind)


def setup_inputs(seed: int = 0) -> dict:
    keys = jax.random.split(jax.random.key(seed), 7)
    fresh = gaussian(keys[0], (TICKS, BATCH, HEIGHT, WD, 2 * C), 1.0, 6.0, ((1, 16), (2, 2)), jnp.float32)
    target = gaussian(keys[1], (TICKS - 1, BATCH, HEIGHT, WD, 2 * C), 1.0, 6.0, ((1, 16), (2, 2)), jnp.float32)
    carried = gaussian(keys[2], (N_SEGMENT, BATCH, HEIGHT, WD, 2 * C), 1.0, 6.0, ((0, 8), (1, 16), (2, 2)), jnp.float32)
    returning = gaussian(keys[3], (N_SEGMENT, 2, BATCH, HEIGHT, WD, 2 * C), 1.0, 6.0, ((0, 8), (2, 16), (3, 2)), jnp.float32)
    weights = gaussian(keys[4], (N_SEGMENT, BLK, 2, 9 * C, C), (36 * C) ** -0.5, 0.09375, ((0, 8),), jnp.float32)
    section_blocks = draw_section_blocks(jax.random.fold_in(keys[6], 71), 0)
    return dict(fresh=fresh, target=target, carried=carried, returning=returning, weights=weights, section_blocks=section_blocks)


HIGHEST = lax.Precision.HIGHEST

def convolve(source, kernel):
    chans = kernel.shape[1]
    return lax.conv_general_dilated(source, kernel.reshape(3, 3, chans, chans), (1, 1), 'SAME', dimension_numbers=('NHWC', 'HWIO', 'NHWC'), precision=HIGHEST)

def branch(source, kernel):
    return convolve(jax.nn.silu(source), kernel)

def forward_block(state, first_kernel, second_kernel):
    chans = first_kernel.shape[1]
    upper_half = state[..., :chans] + branch(state[..., chans:], first_kernel)
    lower_half = state[..., chans:] + branch(upper_half, second_kernel)
    return jnp.concatenate([upper_half, lower_half], axis=-1)

def backward_block(outputs, grads, first_kernel, second_kernel):
    chans = first_kernel.shape[1]
    upper_half, lower_half = (outputs[..., :chans], outputs[..., chans:])
    grad_upper, grad_lower = (grads[..., :chans], grads[..., chans:])
    rebuilt, pull_second = jax.vjp(branch, upper_half, second_kernel)
    lower_in = lower_half - rebuilt
    added_grad, grad_second = pull_second(grad_lower)
    grad_upper = grad_upper + added_grad
    rebuilt, pull_first = jax.vjp(branch, lower_in, first_kernel)
    upper_in = upper_half - rebuilt
    added_grad, grad_first = pull_first(grad_upper)
    grad_lower = grad_lower + added_grad
    return (jnp.concatenate([upper_in, lower_in], axis=-1), jnp.concatenate([grad_upper, grad_lower], axis=-1), grad_first, grad_second)

def reference(fresh, target, carried, returning, weights, section_blocks):
    inputs = [carried[segment_id] for segment_id in range(N_SEGMENT)]
    pairs = [(returning[segment_id, 0], returning[segment_id, 1]) for segment_id in range(N_SEGMENT)]
    running = [jnp.zeros((BLK, 2, 9 * C, C), jnp.float32) for segment_id in range(N_SEGMENT)]
    produced = []
    sent = []
    for window_tick in range(TICKS):
        produced = []
        sent = []
        for segment_id in range(N_SEGMENT):
            doubled = section_blocks[segment_id] == 2
            factor = doubled.astype(jnp.float32)
            source = fresh[window_tick] if segment_id == 0 else inputs[segment_id]
            once = forward_block(source, weights[segment_id, 0, 0], weights[segment_id, 0, 1])
            twice = forward_block(once, weights[segment_id, 1, 0], weights[segment_id, 1, 1])
            produced.append(jnp.where(doubled, twice, once))
            outputs, grads = pairs[segment_id]
            back_in, back_grad, first_one, second_one = backward_block(outputs, grads, weights[segment_id, 1, 0], weights[segment_id, 1, 1])
            outputs = jnp.where(doubled, back_in, outputs)
            grads = jnp.where(doubled, back_grad, grads)
            back_in, back_grad, first_zero, second_zero = backward_block(outputs, grads, weights[segment_id, 0, 0], weights[segment_id, 0, 1])
            tick_grads = jnp.stack([jnp.stack([first_zero, second_zero]), jnp.stack([first_one, second_one]) * factor])
            running[segment_id] = running[segment_id] + tick_grads
            sent.append((back_in, back_grad))
        if window_tick < TICKS - 1:
            inputs = [produced[0]] + produced[:-1]
            last_out = produced[-1]
            pairs = sent[1:] + [(last_out, last_out - target[window_tick])]
    grad_weights = jnp.stack(running) / math.sqrt(TICKS * BATCH * HEIGHT * WD)
    leaving = jnp.stack(produced)
    sent_back = jnp.stack([jnp.stack([pair_in, pair_grad]) for pair_in, pair_grad in sent])
    return (grad_weights, leaving, sent_back)
```

```python
import functools
import math

import jax
import jax.numpy as jnp
from jax import lax
from jax.experimental import pallas as pl
from jax.experimental.pallas import tpu as pltpu
from jax.sharding import PartitionSpec as P

F32 = jnp.float32
BF16 = jnp.bfloat16
C = 128
TAPS = 9
DEPTH = TAPS * C
WD = 16
OWN = 8
HALF = 4
FULL = 16
WINDOW = 12
VIEW = OWN + 2
PACK = (VIEW + OWN) * WD
MEGA = 1 << 20


def params(mib):
    return pltpu.CompilerParams(vmem_limit_bytes=mib * MEGA)


def cost(flops, nbytes):
    return pl.CostEstimate(flops=flops, bytes_accessed=nbytes, transcendentals=0)


def whole(memory_space=pltpu.VMEM):
    return pl.BlockSpec(memory_space=memory_space)


def call(body, out_shape, scratch, args, mib, flops, smem=()):
    in_specs = [whole(pltpu.SMEM if i in smem else pltpu.VMEM) for i in range(len(args))]
    outs = [jax.ShapeDtypeStruct(shape, F32) for shape in out_shape]
    nbytes = sum(4 * math.prod(shape) for shape in out_shape)
    return pl.pallas_call(
        body,
        out_shape=outs,
        in_specs=in_specs,
        out_specs=[whole() for _ in outs],
        scratch_shapes=scratch,
        compiler_params=params(mib),
        cost_estimate=cost(flops, nbytes),
    )(*args)


def rows(start, count):
    return pl.ds(pl.multiple_of(start * WD, HALF * WD), count * WD)


def hi_lo(value):
    high = value.astype(BF16)
    return high, (value - high.astype(F32)).astype(BF16)


def shifted(value):
    count = value.shape[0]
    column = lax.broadcasted_iota(jnp.int32, value.shape, 0) % WD
    left = jnp.where(column == 0, 0.0, pltpu.roll(value, 1, 0))
    right = jnp.where(column == WD - 1, 0.0, pltpu.roll(value, count - 1, 0))
    return left, value, right


def fill_patches(value, high_ref, low_ref):
    count = value.shape[0]
    for tap, moved in enumerate(shifted(value)):
        high, low = hi_lo(moved)
        high_ref[WD : WD + count, tap * C : (tap + 1) * C] = high
        low_ref[WD : WD + count, tap * C : (tap + 1) * C] = low


def clear_rim(ref, count):
    rim = jnp.zeros((WD,) + tuple(ref.shape[1:]), ref.dtype)
    ref[0:WD] = rim
    ref[WD + count : 2 * WD + count] = rim


def gathered(ref, count):
    return jnp.concatenate([ref[d * WD : d * WD + count, :] for d in range(3)], axis=1)


def conv(high_ref, low_ref, kernel_ref, slot, count):
    both = jnp.dot(gathered(high_ref, count), kernel_ref[slot], preferred_element_type=F32)
    rest = jnp.dot(
        gathered(low_ref, count), kernel_ref[slot, :, 0:C], preferred_element_type=F32
    )
    return both[:, :C] + (both[:, C:] + rest)


def logistic(value):
    return 1.0 / (1.0 + jnp.exp(-value))


def prepare_body(weight_ref, plain_ref, turned_ref):
    for tap in range(TAPS):
        block = weight_ref[0, tap * C : (tap + 1) * C, :]
        high, low = hi_lo(block)
        plain_ref[0, tap * C : (tap + 1) * C, 0:C] = high
        plain_ref[0, tap * C : (tap + 1) * C, C:] = low
        high, low = hi_lo(block.T)
        back = TAPS - 1 - tap
        turned_ref[0, back * C : (back + 1) * C, 0:C] = high
        turned_ref[0, back * C : (back + 1) * C, C:] = low


def prepare(weights):
    slots = weights.shape[0]
    shape = jax.ShapeDtypeStruct((slots, DEPTH, 2 * C), BF16)
    return pl.pallas_call(
        prepare_body,
        out_shape=[shape, shape],
        grid=(slots,),
        in_specs=[pl.BlockSpec((1, DEPTH, C), lambda i: (i, 0, 0))],
        out_specs=[pl.BlockSpec((1, DEPTH, 2 * C), lambda i: (i, 0, 0))] * 2,
        compiler_params=params(16),
        cost_estimate=cost(slots * DEPTH * C * 8, slots * DEPTH * C * 12),
    )(weights)


def pack_body(fresh_ref, carried_ref, target_ref, out_ref):
    first = lax.axis_index("segment") == 0
    start = HALF * (1 - lax.axis_index("row"))

    @pl.when(first)
    def _():
        out_ref[0 : OWN * WD] = fresh_ref[0]

    @pl.when(jnp.logical_not(first))
    def _():
        out_ref[0 : OWN * WD] = carried_ref[...]

    out_ref[OWN * WD : WINDOW * WD] = target_ref[rows(start, HALF)]
    out_ref[WINDOW * WD :] = fresh_ref[1, rows(start, HALF)]


def put_halves(ref, index, where, value):
    ref[0, where] = value[:, :C]
    ref[1, where] = value[:, C:]


def forward_loop(state_ref, high_ref, low_ref, kernel_ref, blocks_ref, count):
    clear_rim(high_ref, count)
    clear_rim(low_ref, count)

    def step(slot, carry):
        half = slot % 2
        source = state_ref[1 - half]
        fill_patches(source * logistic(source), high_ref, low_ref)
        state_ref[half] = state_ref[half] + conv(high_ref, low_ref, kernel_ref, slot, count)
        return carry

    lax.fori_loop(0, 2 * blocks_ref[0], step, 0)


def forward_full_body(blocks_ref, own_ref, other_ref, kernel_ref, out_ref, state, high, low):
    row = lax.axis_index("row")
    put_halves(state, 0, rows(OWN * row, OWN), own_ref[...])
    put_halves(state, 0, rows(OWN * (1 - row), OWN), other_ref[0 : OWN * WD])
    forward_loop(state, high, low, kernel_ref, blocks_ref, FULL * WD)
    part = rows(HALF * row, WINDOW)
    out_ref[:, :C] = state[0, part]
    out_ref[:, C:] = state[1, part]


def forward_window_body(
    blocks_ref, came_ref, fresh_ref, other_ref, kernel_ref, out_ref, state, high, low
):
    row = lax.axis_index("row")
    first = lax.axis_index("segment") == 0

    @pl.when(first)
    def _():
        put_halves(state, 0, rows(HALF * row, OWN), fresh_ref[1])
        put_halves(state, 0, rows(OWN * (1 - row), HALF), other_ref[WINDOW * WD :])

    @pl.when(jnp.logical_not(first))
    def _():
        put_halves(state, 0, pl.ds(0, WINDOW * WD), came_ref[...])

    forward_loop(state, high, low, kernel_ref, blocks_ref, WINDOW * WD)
    part = rows(HALF * row, OWN)
    out_ref[:, :C] = state[0, part]
    out_ref[:, C:] = state[1, part]


def backward_loop(
    state, slope_in, plain_ref, turned_ref, blocks_ref, pads, picked, own, count
):
    source_high, source_low, grad_high, grad_low, source_pad = pads
    for ref in pads:
        clear_rim(ref, count)

    @pl.when(blocks_ref[0] < 2)
    def _():
        picked[2] = jnp.zeros((PACK, C), F32)
        picked[3] = jnp.zeros((PACK, C), F32)

    top = 2 * blocks_ref[0] - 1

    def step(turn, carry):
        slot = top - turn
        half = slot % 2
        source = state[1 - half]
        grad = slope_in[half]
        gate = logistic(source)
        field = source * gate
        source_pad[WD : WD + count] = field
        fill_patches(field, source_high, source_low)
        fill_patches(grad, grad_high, grad_low)
        picked[slot, 0 : VIEW * WD] = source_pad[rows(own, VIEW)]
        picked[slot, VIEW * WD :] = slope_in[half, rows(own, OWN)]
        state[half] = state[half] - conv(source_high, source_low, plain_ref, slot, count)
        slope = gate * (1.0 + source * (1.0 - gate))
        slope_in[1 - half] = slope_in[1 - half] + slope * conv(
            grad_high, grad_low, turned_ref, slot, count
        )
        return carry

    lax.fori_loop(0, top + 1, step, 0)


def crossing(row):
    return 2 * row + lax.axis_index("dp") % 2


def hand_out(picked, refs):
    place = crossing(lax.axis_index("row"))
    for by, ref in enumerate(refs):
        ref[...] = picked[(place + by) % 4]


def backward_full_body(
    blocks_ref, own_ref, other_ref, plain_ref, turned_ref, out_ref, *rest
):
    outs, (state, grads, picked), pads = rest[:4], rest[4:7], rest[7:]
    row = lax.axis_index("row")
    for ref, index in ((state, 0), (grads, 1)):
        put_halves(ref, 0, rows(OWN * row, OWN), own_ref[index])
        put_halves(ref, 0, rows(OWN * (1 - row), OWN), other_ref[index])
    backward_loop(
        state, grads, plain_ref, turned_ref, blocks_ref, pads, picked, OWN * row, FULL * WD
    )
    part = rows(HALF * row, WINDOW)
    for ref, index in ((state, 0), (grads, 1)):
        out_ref[index, :, :C] = ref[0, part]
        out_ref[index, :, C:] = ref[1, part]
    hand_out(picked, outs)


def backward_window_body(
    blocks_ref,
    came_ref,
    made_ref,
    target_ref,
    other_ref,
    plain_ref,
    turned_ref,
    out_ref,
    *rest,
):
    outs, (state, grads, picked), pads = rest[:4], rest[4:7], rest[7:]
    row = lax.axis_index("row")
    final = lax.axis_index("segment") == lax.axis_size("segment") - 1

    @pl.when(final)
    def _():
        put_halves(grads, 0, rows(HALF * row, OWN), target_ref[...])
        put_halves(grads, 0, rows(OWN * (1 - row), HALF), other_ref[OWN * WD : WINDOW * WD])
        for half in range(2):
            made = made_ref[:, half * C : (half + 1) * C]
            state[half] = made
            grads[half] = made - grads[half]

    @pl.when(jnp.logical_not(final))
    def _():
        put_halves(state, 0, pl.ds(0, WINDOW * WD), came_ref[0])
        put_halves(grads, 0, pl.ds(0, WINDOW * WD), came_ref[1])

    backward_loop(
        state, grads, plain_ref, turned_ref, blocks_ref, pads, picked, HALF * row, WINDOW * WD
    )
    part = rows(HALF * row, OWN)
    for ref, index in ((state, 0), (grads, 1)):
        out_ref[index, :, :C] = ref[0, part]
        out_ref[index, :, C:] = ref[1, part]
    hand_out(picked, outs)


def forward_scratch(count):
    return [
        pltpu.VMEM((2, count, C), F32),
        pltpu.VMEM((count + 2 * WD, 3 * C), BF16),
        pltpu.VMEM((count + 2 * WD, 3 * C), BF16),
    ]


def backward_scratch(count):
    padded = pltpu.VMEM((count + 2 * WD, 3 * C), BF16)
    return [
        pltpu.VMEM((2, count, C), F32),
        pltpu.VMEM((2, count, C), F32),
        pltpu.VMEM((4, PACK, C), F32),
        padded,
        padded,
        padded,
        padded,
        pltpu.VMEM((count + 2 * WD, C), F32),
    ]


def kernel_grad(parts, high_ref, low_ref, turned_ref):
    for index, part in enumerate(parts):
        at = slice(index * OWN * WD, (index + 1) * OWN * WD)
        for tap, moved in enumerate(shifted(part[0 : VIEW * WD])):
            high, low = hi_lo(moved)
            for drop in range(3):
                lanes = slice((3 * drop + tap) * C, (3 * drop + tap + 1) * C)
                high_ref[at, lanes] = high[drop * WD : (drop + OWN) * WD]
                low_ref[at, lanes] = low[drop * WD : (drop + OWN) * WD]
        high, low = hi_lo(part[VIEW * WD :].T)
        turned_ref[0:C, at] = high
        turned_ref[C:, at] = low
    both = jnp.dot(turned_ref[...], high_ref[...], preferred_element_type=F32)
    rest = jnp.dot(turned_ref[0:C], low_ref[...], preferred_element_type=F32)
    return both[:C] + (both[C:] + rest)


def early_grad_body(*refs):
    parts, out_ref, scratch = refs[:4], refs[4], refs[5:]
    out_ref[...] = kernel_grad(parts, *scratch)


def late_grad_body(scale, share, *refs):
    parts, early_ref, out_ref, scratch, total_ref = refs[:4], refs[4], refs[5], refs[6:9], refs[9]
    total = (kernel_grad(parts, *scratch) + early_ref[...]) * scale
    for tap in range(TAPS):
        total_ref[tap * C : (tap + 1) * C, :] = total[:, tap * C : (tap + 1) * C].T
    for along in range(8):
        for place in range(4):
            start = share * (16 * (place // 2) + 2 * along + place % 2)
            out_ref[along, place * share : (place + 1) * share] = total_ref[start : start + share]


def grad_scratch():
    count = 4 * OWN * WD
    return [
        pltpu.VMEM((count, DEPTH), BF16),
        pltpu.VMEM((count, DEPTH), BF16),
        pltpu.VMEM((2 * C, count), BF16),
    ]


def fold_body(share, in_ref, *refs):
    outs, held = refs[:4], refs[4]
    total = in_ref[0]
    for along in range(1, 8):
        total = total + in_ref[along]
    for place in range(4):
        held[place] = total[place * share : (place + 1) * share]
    here = crossing(lax.axis_index("row"))
    for by, ref in enumerate(outs):
        ref[...] = held[(here + by) % 4]


def settle_body(*refs):
    parts, out_ref = refs[:4], refs[4]
    here = crossing(lax.axis_index("row"))
    for by, part in enumerate(parts):
        out_ref[(here + 4 - by) % 4] = part[...]


def per_device(fresh, target, carried, returning, weights, section_blocks):
    tick_count = fresh.shape[0]
    cells = (
        tick_count
        * fresh.shape[1]
        * lax.axis_size("dp")
        * fresh.shape[2]
        * lax.axis_size("row")
        * fresh.shape[3]
    )
    segments = lax.axis_size("segment")
    dp_count = lax.axis_size("dp")
    rungs = dp_count // 2
    share = DEPTH // (2 * dp_count)
    flat = OWN * WD
    fresh = fresh.reshape(2, flat, 2 * C)
    target = target.reshape(flat, 2 * C)
    carried = carried.reshape(flat, 2 * C)
    returning = returning.reshape(2, flat, 2 * C)
    weights = weights.reshape(4, DEPTH, C)
    swap = [(0, 1), (1, 0)]
    onward = [(i, i + 1) for i in range(segments - 1)]
    homeward = [(i + 1, i) for i in range(segments - 1)]

    def across(by):
        pairs = []
        for row in range(2):
            for rung in range(rungs):
                for low in range(2):
                    there = (2 * row + low + by) % 4
                    pairs.append(
                        (
                            row * dp_count + 2 * rung + low,
                            (there // 2) * dp_count + 2 * rung + there % 2,
                        )
                    )
        return pairs

    def deal(parts):
        return [parts[0]] + [
            lax.ppermute(parts[by], ("row", "dp"), across(by)) for by in range(1, 4)
        ]

    conv_flops = 6 * DEPTH * C
    other_pair = lax.ppermute(returning, "row", swap)
    (packed,) = call(
        pack_body, [(2 * flat, 2 * C)], [], (fresh, carried, target), 8, 1 << 20
    )
    other_pack = lax.ppermute(packed, "row", swap)
    plain, turned = prepare(weights)

    sent, *dealt = call(
        backward_full_body,
        [(2, WINDOW * WD, 2 * C)] + [(PACK, C)] * 4,
        backward_scratch(FULL * WD),
        (section_blocks, returning, other_pair, plain, turned),
        24,
        8 * conv_flops * FULL * WD,
        smem=(0,),
    )
    came_back = lax.ppermute(sent, "segment", homeward)
    early = deal(dealt)
    (made,) = call(
        forward_full_body,
        [(WINDOW * WD, 2 * C)],
        forward_scratch(FULL * WD),
        (section_blocks, packed[:flat], other_pack, plain),
        24,
        4 * conv_flops * FULL * WD,
        smem=(0,),
    )
    came_on = lax.ppermute(made, "segment", onward)
    back, *dealt = call(
        backward_window_body,
        [(2, flat, 2 * C)] + [(PACK, C)] * 4,
        backward_scratch(WINDOW * WD),
        (section_blocks, came_back, made, target, other_pack, plain, turned),
        24,
        8 * conv_flops * WINDOW * WD,
        smem=(0,),
    )
    late = deal(dealt)
    (early_grad,) = call(
        early_grad_body, [(C, DEPTH)], grad_scratch(), tuple(early), 24, 4 * conv_flops * flat
    )
    (produced,) = call(
        forward_window_body,
        [(flat, 2 * C)],
        forward_scratch(WINDOW * WD),
        (section_blocks, came_on, fresh, other_pack, plain),
        24,
        4 * conv_flops * WINDOW * WD,
        smem=(0,),
    )
    (partial_sums,) = call(
        functools.partial(late_grad_body, 1.0 / math.sqrt(cells), share),
        [(rungs, 4 * share, C)],
        grad_scratch() + [pltpu.VMEM((DEPTH, C), F32)],
        tuple(late) + (early_grad,),
        24,
        4 * conv_flops * flat,
    )
    columns = [
        [row * dp_count + 2 * rung + low for rung in range(rungs)]
        for row in range(2)
        for low in range(2)
    ]
    spread = lax.all_to_all(
        partial_sums, ("row", "dp"), 0, 0, axis_index_groups=columns, tiled=True
    )
    folded = call(
        functools.partial(fold_body, share),
        [(share, C)] * 4,
        [pltpu.VMEM((4, share, C), F32)],
        (spread,),
        8,
        1 << 20,
    )
    (grad_weights,) = call(settle_body, [(4, share, C)], [], tuple(deal(folded)), 8, 1 << 20)
    return (
        grad_weights.reshape(1, 2, 2, share, C),
        produced.reshape(1, 1, OWN, WD, 2 * C),
        back.reshape(1, 2, 1, OWN, WD, 2 * C),
    )


def solution(mesh):
    return jax.shard_map(
        per_device,
        mesh=mesh,
        in_specs=(
            P(None, "dp", "row", None, None),
            P(None, "dp", "row", None, None),
            P("segment", "dp", "row", None, None),
            P("segment", None, "dp", "row", None, None),
            P("segment", None, None, None, None),
            P("segment"),
        ),
        out_specs=(
            P("segment", None, None, ("row", "dp"), None),
            P("segment", "dp", "row", None, None),
            P("segment", None, "dp", "row", None, None),
        ),
        check_vma=False,
    )
```

```python
import functools
import math

import jax
import jax.numpy as jnp
from jax import lax
from jax.experimental import pallas as pl
from jax.experimental.pallas import tpu as pltpu
from jax.sharding import PartitionSpec as P


F32 = jnp.float32
BF16 = jnp.bfloat16
C = 128
TAPS = 9
DEPTH = TAPS * C
WD = 16
OWN = 8
HALF = 4
FULL = 16
WINDOW = 12
VIEW = OWN + 2
PACK = (VIEW + OWN) * WD
MEGA = 1 << 20


def params(mib):
    return pltpu.CompilerParams(vmem_limit_bytes=mib * MEGA)


def cost(flops, nbytes):
    return pl.CostEstimate(flops=flops, bytes_accessed=nbytes, transcendentals=0)


def whole(memory_space=pltpu.VMEM):
    return pl.BlockSpec(memory_space=memory_space)


def call(body, out_shape, scratch, args, mib, flops, smem=()):
    in_specs = [whole(pltpu.SMEM if i in smem else pltpu.VMEM) for i in range(len(args))]
    outs = [jax.ShapeDtypeStruct(shape, F32) for shape in out_shape]
    nbytes = sum(4 * math.prod(shape) for shape in out_shape)
    return pl.pallas_call(
        body,
        out_shape=outs,
        in_specs=in_specs,
        out_specs=[whole() for _ in outs],
        scratch_shapes=scratch,
        compiler_params=params(mib),
        cost_estimate=cost(flops, nbytes),
    )(*args)


def rows(start, count):
    return pl.ds(pl.multiple_of(start * WD, HALF * WD), count * WD)


def hi_lo(value):
    high = value.astype(BF16)
    return high, (value - high.astype(F32)).astype(BF16)


def shifted(value):
    count = value.shape[0]
    column = lax.broadcasted_iota(jnp.int32, value.shape, 0) % WD
    left = jnp.where(column == 0, 0.0, pltpu.roll(value, 1, 0))
    right = jnp.where(column == WD - 1, 0.0, pltpu.roll(value, count - 1, 0))
    return left, value, right


def fill_patches(value, high_ref, low_ref):
    count = value.shape[0]
    for tap, moved in enumerate(shifted(value)):
        high, low = hi_lo(moved)
        high_ref[WD : WD + count, tap * C : (tap + 1) * C] = high
        low_ref[WD : WD + count, tap * C : (tap + 1) * C] = low


def clear_rim(ref, count):
    rim = jnp.zeros((WD,) + tuple(ref.shape[1:]), ref.dtype)
    ref[0:WD] = rim
    ref[WD + count : 2 * WD + count] = rim


def gathered(ref, count):
    return jnp.concatenate([ref[d * WD : d * WD + count, :] for d in range(3)], axis=1)


def conv(high_ref, low_ref, kernel_ref, slot, count):
    both = jnp.dot(gathered(high_ref, count), kernel_ref[slot], preferred_element_type=F32)
    rest = jnp.dot(
        gathered(low_ref, count), kernel_ref[slot, :, 0:C], preferred_element_type=F32
    )
    return both[:, :C] + (both[:, C:] + rest)


def logistic(value):
    return 1.0 / (1.0 + jnp.exp(-value))


def prepare_body(weight_ref, plain_ref, turned_ref):
    for tap in range(TAPS):
        block = weight_ref[0, tap * C : (tap + 1) * C, :]
        high, low = hi_lo(block)
        plain_ref[0, tap * C : (tap + 1) * C, 0:C] = high
        plain_ref[0, tap * C : (tap + 1) * C, C:] = low
        high, low = hi_lo(block.T)
        back = TAPS - 1 - tap
        turned_ref[0, back * C : (back + 1) * C, 0:C] = high
        turned_ref[0, back * C : (back + 1) * C, C:] = low


def prepare(weights):
    slots = weights.shape[0]
    shape = jax.ShapeDtypeStruct((slots, DEPTH, 2 * C), BF16)
    return pl.pallas_call(
        prepare_body,
        out_shape=[shape, shape],
        grid=(slots,),
        in_specs=[pl.BlockSpec((1, DEPTH, C), lambda i: (i, 0, 0))],
        out_specs=[pl.BlockSpec((1, DEPTH, 2 * C), lambda i: (i, 0, 0))] * 2,
        compiler_params=params(16),
        cost_estimate=cost(slots * DEPTH * C * 8, slots * DEPTH * C * 12),
    )(weights)


def pack_body(fresh_ref, carried_ref, target_ref, out_ref):
    first = lax.axis_index("segment") == 0
    start = HALF * (1 - lax.axis_index("row"))

    @pl.when(first)
    def _():
        out_ref[0 : OWN * WD] = fresh_ref[0]

    @pl.when(jnp.logical_not(first))
    def _():
        out_ref[0 : OWN * WD] = carried_ref[...]

    out_ref[OWN * WD : WINDOW * WD] = target_ref[rows(start, HALF)]
    out_ref[WINDOW * WD :] = fresh_ref[1, rows(start, HALF)]


def put_halves(ref, where, value):
    ref[0, where] = value[:, :C]
    ref[1, where] = value[:, C:]


def forward_loop(state_ref, high_ref, low_ref, kernel_ref, blocks_ref, count):
    clear_rim(high_ref, count)
    clear_rim(low_ref, count)

    def step(slot, carry):
        half = slot % 2
        source = state_ref[1 - half]
        fill_patches(source * logistic(source), high_ref, low_ref)
        state_ref[half] = state_ref[half] + conv(high_ref, low_ref, kernel_ref, slot, count)
        return carry

    lax.fori_loop(0, 2 * blocks_ref[0], step, 0)


def forward_full_body(blocks_ref, own_ref, other_ref, kernel_ref, out_ref, state, high, low):
    row = lax.axis_index("row")
    put_halves(state, rows(OWN * row, OWN), own_ref[...])
    put_halves(state, rows(OWN * (1 - row), OWN), other_ref[0 : OWN * WD])
    forward_loop(state, high, low, kernel_ref, blocks_ref, FULL * WD)
    part = rows(HALF * row, WINDOW)
    out_ref[:, :C] = state[0, part]
    out_ref[:, C:] = state[1, part]


def forward_window_body(
    blocks_ref, came_ref, fresh_ref, other_ref, kernel_ref, out_ref, state, high, low
):
    row = lax.axis_index("row")
    first = lax.axis_index("segment") == 0

    @pl.when(first)
    def _():
        put_halves(state, rows(HALF * row, OWN), fresh_ref[1])
        put_halves(state, rows(OWN * (1 - row), HALF), other_ref[WINDOW * WD :])

    @pl.when(jnp.logical_not(first))
    def _():
        put_halves(state, pl.ds(0, WINDOW * WD), came_ref[...])

    forward_loop(state, high, low, kernel_ref, blocks_ref, WINDOW * WD)
    part = rows(HALF * row, OWN)
    out_ref[:, :C] = state[0, part]
    out_ref[:, C:] = state[1, part]


def clear_picked(picked, blocks_ref):
    @pl.when(blocks_ref[0] < 2)
    def _():
        picked[2] = jnp.zeros((PACK, C), F32)
        picked[3] = jnp.zeros((PACK, C), F32)


def pick(picked, slot, source_pad, grads, half, own):
    picked[slot, 0 : VIEW * WD] = source_pad[rows(own, VIEW)]
    picked[slot, VIEW * WD :] = grads[half, rows(own, OWN)]


def backward_step(slot, half, state, grads, plain_ref, turned_ref, pads, count, picked, own):
    source_high, source_low, grad_high, grad_low = pads[:4]
    source = state[1 - half]
    grad = grads[half]
    gate = logistic(source)
    field = source * gate
    fill_patches(field, source_high, source_low)
    fill_patches(grad, grad_high, grad_low)
    if picked is not None:
        pads[4][WD : WD + count] = field
        pick(picked, slot, pads[4], grads, half, own)
    state[half] = state[half] - conv(source_high, source_low, plain_ref, slot, count)
    slope = gate * (1.0 + source * (1.0 - gate))
    grads[1 - half] = grads[1 - half] + slope * conv(
        grad_high, grad_low, turned_ref, slot, count
    )


def backward_loop(
    state, grads, plain_ref, turned_ref, blocks_ref, pads, picked, own, count, lowest
):
    for ref in pads:
        clear_rim(ref, count)
    clear_picked(picked, blocks_ref)
    top = 2 * blocks_ref[0] - 1

    def step(turn, carry):
        slot = top - turn
        backward_step(
            slot, slot % 2, state, grads, plain_ref, turned_ref, pads, count, picked, own
        )
        return carry

    lax.fori_loop(0, top + 1 - lowest, step, 0)


def crossing(row):
    return 2 * row + lax.axis_index("dp") % 2


def hand_out(picked, refs):
    place = crossing(lax.axis_index("row"))
    for by, ref in enumerate(refs):
        ref[...] = picked[(place + by) % 4]


def backward_full_body(
    blocks_ref, own_ref, other_ref, plain_ref, turned_ref, out_ref, *rest
):
    outs, (state, grads, picked), pads = rest[:4], rest[4:7], rest[7:]
    row = lax.axis_index("row")
    for ref, index in ((state, 0), (grads, 1)):
        put_halves(ref, rows(OWN * row, OWN), own_ref[index])
        put_halves(ref, rows(OWN * (1 - row), OWN), other_ref[index])
    backward_loop(
        state, grads, plain_ref, turned_ref, blocks_ref, pads, picked, OWN * row, FULL * WD, 0
    )
    part = rows(HALF * row, WINDOW)
    for ref, index in ((state, 0), (grads, 1)):
        out_ref[index, :, :C] = ref[0, part]
        out_ref[index, :, C:] = ref[1, part]
    hand_out(picked, outs)


def backward_window_body(
    blocks_ref,
    came_ref,
    made_ref,
    target_ref,
    other_ref,
    plain_ref,
    turned_ref,
    mid_ref,
    *rest,
):
    outs, (state, grads, picked), pads = rest[:4], rest[4:7], rest[7:]
    row = lax.axis_index("row")
    final = lax.axis_index("segment") == lax.axis_size("segment") - 1

    @pl.when(final)
    def _():
        put_halves(grads, rows(HALF * row, OWN), target_ref[...])
        put_halves(grads, rows(OWN * (1 - row), HALF), other_ref[OWN * WD : WINDOW * WD])
        for half in range(2):
            made = made_ref[:, half * C : (half + 1) * C]
            state[half] = made
            grads[half] = made - grads[half]

    @pl.when(jnp.logical_not(final))
    def _():
        put_halves(state, pl.ds(0, WINDOW * WD), came_ref[0])
        put_halves(grads, pl.ds(0, WINDOW * WD), came_ref[1])

    count = WINDOW * WD
    own = HALF * row
    backward_loop(
        state, grads, plain_ref, turned_ref, blocks_ref, pads, picked, own, count, 1
    )
    source = state[1]
    pads[4][WD : WD + count] = source * logistic(source)
    pick(picked, 0, pads[4], grads, 0, own)
    hand_out(picked, outs)
    mid_ref[0] = state[...]
    mid_ref[1] = grads[...]


def backward_tail_body(mid_ref, plain_ref, turned_ref, out_ref, state, grads, *pads):
    state[...] = mid_ref[0]
    grads[...] = mid_ref[1]
    for ref in pads:
        clear_rim(ref, WINDOW * WD)
    backward_step(
        0, 0, state, grads, plain_ref, turned_ref, pads, WINDOW * WD, None, None
    )
    part = rows(HALF * lax.axis_index("row"), OWN)
    for ref, index in ((state, 0), (grads, 1)):
        out_ref[index, :, :C] = ref[0, part]
        out_ref[index, :, C:] = ref[1, part]


def forward_scratch(count):
    return [
        pltpu.VMEM((2, count, C), F32),
        pltpu.VMEM((count + 2 * WD, 3 * C), BF16),
        pltpu.VMEM((count + 2 * WD, 3 * C), BF16),
    ]


def backward_scratch(count):
    padded = pltpu.VMEM((count + 2 * WD, 3 * C), BF16)
    return [
        pltpu.VMEM((2, count, C), F32),
        pltpu.VMEM((2, count, C), F32),
        pltpu.VMEM((4, PACK, C), F32),
        padded,
        padded,
        padded,
        padded,
        pltpu.VMEM((count + 2 * WD, C), F32),
    ]


def kernel_grad(parts, high_ref, low_ref, turned_ref):
    for index, part in enumerate(parts):
        at = slice(index * OWN * WD, (index + 1) * OWN * WD)
        for tap, moved in enumerate(shifted(part[0 : VIEW * WD])):
            high, low = hi_lo(moved)
            for drop in range(3):
                lanes = slice((3 * drop + tap) * C, (3 * drop + tap + 1) * C)
                high_ref[at, lanes] = high[drop * WD : (drop + OWN) * WD]
                low_ref[at, lanes] = low[drop * WD : (drop + OWN) * WD]
        high, low = hi_lo(part[VIEW * WD :].T)
        turned_ref[0:C, at] = high
        turned_ref[C:, at] = low
    both = jnp.dot(turned_ref[...], high_ref[...], preferred_element_type=F32)
    rest = jnp.dot(turned_ref[0:C], low_ref[...], preferred_element_type=F32)
    return both[:C] + (both[C:] + rest)


def early_grad_body(*refs):
    parts, out_ref, scratch = refs[:4], refs[4], refs[5:]
    out_ref[...] = kernel_grad(parts, *scratch)


def late_grad_body(scale, share, *refs):
    parts, early_ref, out_ref, scratch, total_ref = refs[:4], refs[4], refs[5], refs[6:9], refs[9]
    total = (kernel_grad(parts, *scratch) + early_ref[...]) * scale
    for tap in range(TAPS):
        total_ref[tap * C : (tap + 1) * C, :] = total[:, tap * C : (tap + 1) * C].T
    for along in range(8):
        for place in range(4):
            start = share * (16 * (place // 2) + 2 * along + place % 2)
            out_ref[along, place * share : (place + 1) * share] = total_ref[start : start + share]


def grad_scratch():
    count = 4 * OWN * WD
    return [
        pltpu.VMEM((count, DEPTH), BF16),
        pltpu.VMEM((count, DEPTH), BF16),
        pltpu.VMEM((2 * C, count), BF16),
    ]


def fold_body(share, in_ref, *refs):
    outs, held = refs[:4], refs[4]
    total = in_ref[0]
    for along in range(1, 8):
        total = total + in_ref[along]
    for place in range(4):
        held[place] = total[place * share : (place + 1) * share]
    here = crossing(lax.axis_index("row"))
    for by, ref in enumerate(outs):
        ref[...] = held[(here + by) % 4]


def settle_body(*refs):
    parts, out_ref = refs[:4], refs[4]
    here = crossing(lax.axis_index("row"))
    for by, part in enumerate(parts):
        out_ref[(here + 4 - by) % 4] = part[...]


def per_device(fresh, target, carried, returning, weights, section_blocks):
    tick_count = fresh.shape[0]
    cells = (
        tick_count
        * fresh.shape[1]
        * lax.axis_size("dp")
        * fresh.shape[2]
        * lax.axis_size("row")
        * fresh.shape[3]
    )
    segments = lax.axis_size("segment")
    dp_count = lax.axis_size("dp")
    rungs = dp_count // 2
    share = DEPTH // (2 * dp_count)
    flat = OWN * WD
    fresh = fresh.reshape(2, flat, 2 * C)
    target = target.reshape(flat, 2 * C)
    carried = carried.reshape(flat, 2 * C)
    returning = returning.reshape(2, flat, 2 * C)
    weights = weights.reshape(4, DEPTH, C)
    swap = [(0, 1), (1, 0)]
    onward = [(i, i + 1) for i in range(segments - 1)]
    homeward = [(i + 1, i) for i in range(segments - 1)]

    def across(by):
        pairs = []
        for row in range(2):
            for rung in range(rungs):
                for low in range(2):
                    there = (2 * row + low + by) % 4
                    pairs.append(
                        (
                            row * dp_count + 2 * rung + low,
                            (there // 2) * dp_count + 2 * rung + there % 2,
                        )
                    )
        return pairs

    def deal(parts):
        dealt = [parts[0]]
        for by in range(1, 4):
            dealt.append(lax.ppermute(parts[by], ("row", "dp"), across(by)))
        return dealt

    conv_flops = 6 * DEPTH * C
    other_pair = lax.ppermute(returning, "row", swap)
    (packed,) = call(
        pack_body, [(2 * flat, 2 * C)], [], (fresh, carried, target), 8, 1 << 20
    )
    other_pack = lax.ppermute(packed, "row", swap)
    plain, turned = prepare(weights)

    sent, *dealt = call(
        backward_full_body,
        [(2, WINDOW * WD, 2 * C)] + [(PACK, C)] * 4,
        backward_scratch(FULL * WD),
        (section_blocks, returning, other_pair, plain, turned),
        24,
        8 * conv_flops * FULL * WD,
        smem=(0,),
    )
    came_back = lax.ppermute(sent, "segment", homeward)
    early = deal(dealt)
    (made,) = call(
        forward_full_body,
        [(WINDOW * WD, 2 * C)],
        forward_scratch(FULL * WD),
        (section_blocks, packed[:flat], other_pack, plain),
        24,
        4 * conv_flops * FULL * WD,
        smem=(0,),
    )
    came_on = lax.ppermute(made, "segment", onward)
    mid, *dealt = call(
        backward_window_body,
        [(2, 2, WINDOW * WD, C)] + [(PACK, C)] * 4,
        backward_scratch(WINDOW * WD),
        (section_blocks, came_back, made, target, other_pack, plain, turned),
        24,
        8 * conv_flops * WINDOW * WD,
        smem=(0,),
    )
    late = deal(dealt)
    (back,) = call(
        backward_tail_body,
        [(2, flat, 2 * C)],
        backward_scratch(WINDOW * WD)[:2] + backward_scratch(WINDOW * WD)[3:7],
        (mid, plain, turned),
        24,
        2 * conv_flops * WINDOW * WD,
    )
    (produced,) = call(
        forward_window_body,
        [(flat, 2 * C)],
        forward_scratch(WINDOW * WD),
        (section_blocks, came_on, fresh, other_pack, plain),
        24,
        4 * conv_flops * WINDOW * WD,
        smem=(0,),
    )
    (early_grad,) = call(
        early_grad_body, [(C, DEPTH)], grad_scratch(), tuple(early), 24, 4 * conv_flops * flat
    )
    (partial_sums,) = call(
        functools.partial(late_grad_body, 1.0 / math.sqrt(cells), share),
        [(rungs, 4 * share, C)],
        grad_scratch() + [pltpu.VMEM((DEPTH, C), F32)],
        tuple(late) + (early_grad,),
        24,
        4 * conv_flops * flat,
    )
    columns = [
        [row * dp_count + 2 * rung + low for rung in range(rungs)]
        for row in range(2)
        for low in range(2)
    ]
    spread = lax.all_to_all(
        partial_sums, ("row", "dp"), 0, 0, axis_index_groups=columns, tiled=True
    )
    folded = call(
        functools.partial(fold_body, share),
        [(share, C)] * 4,
        [pltpu.VMEM((4, share, C), F32)],
        (spread,),
        8,
        1 << 20,
    )
    settled = deal(folded)
    (grad_weights,) = call(settle_body, [(4, share, C)], [], tuple(settled), 8, 1 << 20)
    return (
        grad_weights.reshape(1, 2, 2, share, C),
        produced.reshape(1, 1, OWN, WD, 2 * C),
        back.reshape(1, 2, 1, OWN, WD, 2 * C),
    )


def solution(mesh):
    return jax.shard_map(
        per_device,
        mesh=mesh,
        in_specs=(
            P(None, "dp", "row", None, None),
            P(None, "dp", "row", None, None),
            P("segment", "dp", "row", None, None),
            P("segment", None, "dp", "row", None, None),
            P("segment", None, None, None, None),
            P("segment"),
        ),
        out_specs=(
            P("segment", None, None, ("row", "dp"), None),
            P("segment", "dp", "row", None, None),
            P("segment", None, "dp", "row", None, None),
        ),
        check_vma=False,
    )
```

```python
import functools
import math

import jax
import jax.numpy as jnp
from jax import lax
from jax.experimental import pallas as pl
from jax.experimental.pallas import tpu as pltpu
from jax.sharding import PartitionSpec as P


F32 = jnp.float32
BF16 = jnp.bfloat16
C = 128
TAPS = 9
DEPTH = TAPS * C
WD = 16
OWN = 8
HALF = 4
FULL = 16
WINDOW = 12
VIEW = OWN + 2
PACK = (VIEW + OWN) * WD
MEGA = 1 << 20


def params(mib):
    return pltpu.CompilerParams(vmem_limit_bytes=mib * MEGA)


def cost(flops, nbytes):
    return pl.CostEstimate(flops=flops, bytes_accessed=nbytes, transcendentals=0)


def whole(memory_space=pltpu.VMEM):
    return pl.BlockSpec(memory_space=memory_space)


def call(body, out_shape, scratch, args, mib, flops, smem=(), space=pltpu.VMEM):
    in_specs = [whole(pltpu.SMEM if i in smem else space) for i in range(len(args))]
    outs = [jax.ShapeDtypeStruct(shape, F32) for shape in out_shape]
    nbytes = sum(4 * math.prod(shape) for shape in out_shape)
    return pl.pallas_call(
        body,
        out_shape=outs,
        in_specs=in_specs,
        out_specs=[whole() for _ in outs],
        scratch_shapes=scratch,
        compiler_params=params(mib),
        cost_estimate=cost(flops, nbytes),
    )(*args)


def in_hbm(value):
    return pltpu.with_memory_space_constraint(value, pltpu.HBM)


def rows(start, count):
    return pl.ds(pl.multiple_of(start * WD, HALF * WD), count * WD)


def hi_lo(value):
    high = value.astype(BF16)
    return high, (value - high.astype(F32)).astype(BF16)


def shifted(value):
    count = value.shape[0]
    column = lax.broadcasted_iota(jnp.int32, value.shape, 0) % WD
    left = jnp.where(column == 0, 0.0, pltpu.roll(value, 1, 0))
    right = jnp.where(column == WD - 1, 0.0, pltpu.roll(value, count - 1, 0))
    return left, value, right


def fill_patches(value, high_ref, low_ref):
    count = value.shape[0]
    for tap, moved in enumerate(shifted(value)):
        high, low = hi_lo(moved)
        high_ref[WD : WD + count, tap * C : (tap + 1) * C] = high
        low_ref[WD : WD + count, tap * C : (tap + 1) * C] = low


def clear_rim(ref, count):
    rim = jnp.zeros((WD,) + tuple(ref.shape[1:]), ref.dtype)
    ref[0:WD] = rim
    ref[WD + count : 2 * WD + count] = rim


def gathered(ref, count):
    return jnp.concatenate([ref[d * WD : d * WD + count, :] for d in range(3)], axis=1)


def conv(high_ref, low_ref, kernel_ref, slot, count):
    both = jnp.dot(gathered(high_ref, count), kernel_ref[slot], preferred_element_type=F32)
    rest = jnp.dot(
        gathered(low_ref, count), kernel_ref[slot, :, 0:C], preferred_element_type=F32
    )
    return both[:, :C] + (both[:, C:] + rest)


def logistic(value):
    return 1.0 / (1.0 + jnp.exp(-value))


def prepare_body(weight_ref, plain_ref, turned_ref, held, sems):
    slots = weight_ref.shape[0]
    for slot in range(slots):
        pltpu.make_async_copy(weight_ref.at[slot], held.at[slot], sems.at[slot]).start()

    def step(slot, carry):
        pltpu.make_async_copy(weight_ref.at[slot], held.at[slot], sems.at[slot]).wait()
        for tap in range(TAPS):
            block = held[slot, tap * C : (tap + 1) * C, :]
            high, low = hi_lo(block)
            plain_ref[slot, tap * C : (tap + 1) * C, 0:C] = high
            plain_ref[slot, tap * C : (tap + 1) * C, C:] = low
            high, low = hi_lo(block.T)
            back = TAPS - 1 - tap
            turned_ref[slot, back * C : (back + 1) * C, 0:C] = high
            turned_ref[slot, back * C : (back + 1) * C, C:] = low
        return carry

    lax.fori_loop(0, slots, step, 0)


def prepare(weights):
    slots = weights.shape[0]
    shape = jax.ShapeDtypeStruct((slots, DEPTH, 2 * C), BF16)
    return pl.pallas_call(
        prepare_body,
        out_shape=[shape, shape],
        in_specs=[whole(pltpu.HBM)],
        out_specs=[whole(), whole()],
        scratch_shapes=[
            pltpu.VMEM((slots, DEPTH, C), F32),
            pltpu.SemaphoreType.DMA((slots,)),
        ],
        compiler_params=params(16),
        cost_estimate=cost(slots * DEPTH * C * 8, slots * DEPTH * C * 12),
    )(in_hbm(weights))


def pack_body(fresh_ref, carried_ref, target_ref, out_ref, sems):
    first = lax.axis_index("segment") == 0
    start = HALF * (1 - lax.axis_index("row"))
    top = out_ref.at[0 : OWN * WD]
    from_fresh = pltpu.make_async_copy(fresh_ref.at[0], top, sems.at[0])
    from_carried = pltpu.make_async_copy(carried_ref, top, sems.at[0])
    others = (
        pltpu.make_async_copy(
            target_ref.at[rows(start, HALF)], out_ref.at[OWN * WD : WINDOW * WD], sems.at[1]
        ),
        pltpu.make_async_copy(
            fresh_ref.at[1, rows(start, HALF)], out_ref.at[WINDOW * WD :], sems.at[2]
        ),
    )

    @pl.when(first)
    def _():
        from_fresh.start()

    @pl.when(jnp.logical_not(first))
    def _():
        from_carried.start()

    for copy in others:
        copy.start()

    @pl.when(first)
    def _():
        from_fresh.wait()

    @pl.when(jnp.logical_not(first))
    def _():
        from_carried.wait()

    for copy in others:
        copy.wait()


def put_halves(ref, where, value):
    ref[0, where] = value[:, :C]
    ref[1, where] = value[:, C:]


def forward_loop(state_ref, high_ref, low_ref, kernel_ref, blocks_ref, count):
    clear_rim(high_ref, count)
    clear_rim(low_ref, count)

    def step(slot, carry):
        half = slot % 2
        source = state_ref[1 - half]
        fill_patches(source * logistic(source), high_ref, low_ref)
        state_ref[half] = state_ref[half] + conv(high_ref, low_ref, kernel_ref, slot, count)
        return carry

    lax.fori_loop(0, 2 * blocks_ref[0], step, 0)


def forward_full_body(blocks_ref, own_ref, other_ref, kernel_ref, out_ref, state, high, low):
    row = lax.axis_index("row")
    put_halves(state, rows(OWN * row, OWN), own_ref[...])
    put_halves(state, rows(OWN * (1 - row), OWN), other_ref[0 : OWN * WD])
    forward_loop(state, high, low, kernel_ref, blocks_ref, FULL * WD)
    part = rows(HALF * row, WINDOW)
    out_ref[:, :C] = state[0, part]
    out_ref[:, C:] = state[1, part]


def forward_window_body(
    blocks_ref, came_ref, fresh_ref, other_ref, kernel_ref, out_ref, state, high, low
):
    row = lax.axis_index("row")
    first = lax.axis_index("segment") == 0

    @pl.when(first)
    def _():
        put_halves(state, rows(HALF * row, OWN), fresh_ref[1])
        put_halves(state, rows(OWN * (1 - row), HALF), other_ref[WINDOW * WD :])

    @pl.when(jnp.logical_not(first))
    def _():
        put_halves(state, pl.ds(0, WINDOW * WD), came_ref[...])

    forward_loop(state, high, low, kernel_ref, blocks_ref, WINDOW * WD)
    part = rows(HALF * row, OWN)
    out_ref[:, :C] = state[0, part]
    out_ref[:, C:] = state[1, part]


def clear_picked(picked, blocks_ref):
    @pl.when(blocks_ref[0] < 2)
    def _():
        picked[2] = jnp.zeros((PACK, C), F32)
        picked[3] = jnp.zeros((PACK, C), F32)


def pick(picked, slot, source_pad, grads, half, own):
    picked[slot, 0 : VIEW * WD] = source_pad[rows(own, VIEW)]
    picked[slot, VIEW * WD :] = grads[half, rows(own, OWN)]


def backward_step(slot, half, state, grads, plain_ref, turned_ref, pads, count, picked, own):
    source_high, source_low, grad_high, grad_low = pads[:4]
    source = state[1 - half]
    grad = grads[half]
    gate = logistic(source)
    field = source * gate
    fill_patches(field, source_high, source_low)
    fill_patches(grad, grad_high, grad_low)
    if picked is not None:
        pads[4][WD : WD + count] = field
        pick(picked, slot, pads[4], grads, half, own)
    state[half] = state[half] - conv(source_high, source_low, plain_ref, slot, count)
    slope = gate * (1.0 + source * (1.0 - gate))
    grads[1 - half] = grads[1 - half] + slope * conv(
        grad_high, grad_low, turned_ref, slot, count
    )


def backward_loop(
    state, grads, plain_ref, turned_ref, blocks_ref, pads, picked, own, count, lowest
):
    for ref in pads:
        clear_rim(ref, count)
    clear_picked(picked, blocks_ref)
    top = 2 * blocks_ref[0] - 1

    def step(turn, carry):
        slot = top - turn
        backward_step(
            slot, slot % 2, state, grads, plain_ref, turned_ref, pads, count, picked, own
        )
        return carry

    lax.fori_loop(0, top + 1 - lowest, step, 0)


def crossing(row):
    return 2 * row + lax.axis_index("dp") % 2


def hand_out(picked, refs):
    place = crossing(lax.axis_index("row"))
    for by, ref in enumerate(refs):
        ref[...] = picked[(place + by) % 4]


def backward_full_body(
    blocks_ref, own_ref, other_ref, plain_ref, turned_ref, out_ref, *rest
):
    outs, (state, grads, picked), pads = rest[:4], rest[4:7], rest[7:]
    row = lax.axis_index("row")
    for ref, index in ((state, 0), (grads, 1)):
        put_halves(ref, rows(OWN * row, OWN), own_ref[index])
        put_halves(ref, rows(OWN * (1 - row), OWN), other_ref[index])
    backward_loop(
        state, grads, plain_ref, turned_ref, blocks_ref, pads, picked, OWN * row, FULL * WD, 0
    )
    part = rows(HALF * row, WINDOW)
    for ref, index in ((state, 0), (grads, 1)):
        out_ref[index, :, :C] = ref[0, part]
        out_ref[index, :, C:] = ref[1, part]
    hand_out(picked, outs)


def backward_window_body(
    blocks_ref,
    came_ref,
    made_ref,
    target_ref,
    other_ref,
    plain_ref,
    turned_ref,
    mid_ref,
    *rest,
):
    outs, (state, grads, picked), pads = rest[:4], rest[4:7], rest[7:]
    row = lax.axis_index("row")
    final = lax.axis_index("segment") == lax.axis_size("segment") - 1

    @pl.when(final)
    def _():
        put_halves(grads, rows(HALF * row, OWN), target_ref[...])
        put_halves(grads, rows(OWN * (1 - row), HALF), other_ref[OWN * WD : WINDOW * WD])
        for half in range(2):
            made = made_ref[:, half * C : (half + 1) * C]
            state[half] = made
            grads[half] = made - grads[half]

    @pl.when(jnp.logical_not(final))
    def _():
        put_halves(state, pl.ds(0, WINDOW * WD), came_ref[0])
        put_halves(grads, pl.ds(0, WINDOW * WD), came_ref[1])

    count = WINDOW * WD
    own = HALF * row
    backward_loop(
        state, grads, plain_ref, turned_ref, blocks_ref, pads, picked, own, count, 1
    )
    source = state[1]
    pads[4][WD : WD + count] = source * logistic(source)
    pick(picked, 0, pads[4], grads, 0, own)
    hand_out(picked, outs)
    mid_ref[0] = state[...]
    mid_ref[1] = grads[...]


def backward_tail_body(mid_ref, plain_ref, turned_ref, out_ref, state, grads, *pads):
    state[...] = mid_ref[0]
    grads[...] = mid_ref[1]
    for ref in pads:
        clear_rim(ref, WINDOW * WD)
    backward_step(
        0, 0, state, grads, plain_ref, turned_ref, pads, WINDOW * WD, None, None
    )
    part = rows(HALF * lax.axis_index("row"), OWN)
    for ref, index in ((state, 0), (grads, 1)):
        out_ref[index, :, :C] = ref[0, part]
        out_ref[index, :, C:] = ref[1, part]


def forward_scratch(count):
    return [
        pltpu.VMEM((2, count, C), F32),
        pltpu.VMEM((count + 2 * WD, 3 * C), BF16),
        pltpu.VMEM((count + 2 * WD, 3 * C), BF16),
    ]


def backward_scratch(count):
    padded = pltpu.VMEM((count + 2 * WD, 3 * C), BF16)
    return [
        pltpu.VMEM((2, count, C), F32),
        pltpu.VMEM((2, count, C), F32),
        pltpu.VMEM((4, PACK, C), F32),
        padded,
        padded,
        padded,
        padded,
        pltpu.VMEM((count + 2 * WD, C), F32),
    ]


def kernel_grad(parts, high_ref, low_ref, turned_ref):
    for index, part in enumerate(parts):
        at = slice(index * OWN * WD, (index + 1) * OWN * WD)
        for tap, moved in enumerate(shifted(part[0 : VIEW * WD])):
            high, low = hi_lo(moved)
            for drop in range(3):
                lanes = slice((3 * drop + tap) * C, (3 * drop + tap + 1) * C)
                high_ref[at, lanes] = high[drop * WD : (drop + OWN) * WD]
                low_ref[at, lanes] = low[drop * WD : (drop + OWN) * WD]
        high, low = hi_lo(part[VIEW * WD :].T)
        turned_ref[0:C, at] = high
        turned_ref[C:, at] = low
    both = jnp.dot(turned_ref[...], high_ref[...], preferred_element_type=F32)
    rest = jnp.dot(turned_ref[0:C], low_ref[...], preferred_element_type=F32)
    return both[:C] + (both[C:] + rest)


def early_grad_body(*refs):
    parts, out_ref, scratch = refs[:4], refs[4], refs[5:]
    out_ref[...] = kernel_grad(parts, *scratch)


def late_grad_body(scale, share, *refs):
    parts, early_ref, outs, scratch = refs[:4], refs[4], refs[5:13], refs[13:16]
    total_ref, held = refs[16:]
    total = (kernel_grad(parts, *scratch) + early_ref[...]) * scale
    for tap in range(TAPS):
        total_ref[tap * C : (tap + 1) * C, :] = total[:, tap * C : (tap + 1) * C].T
    for along in range(8):
        for place in range(4):
            start = share * (16 * (place // 2) + 2 * along + place % 2)
            held[along, place * share : (place + 1) * share] = total_ref[start : start + share]
    here = lax.axis_index("dp") // 2
    for by, ref in enumerate(outs):
        ref[...] = held[(here + by) % 8]


def grad_scratch():
    count = 4 * OWN * WD
    return [
        pltpu.VMEM((count, DEPTH), BF16),
        pltpu.VMEM((count, DEPTH), BF16),
        pltpu.VMEM((2 * C, count), BF16),
    ]


def fold_body(share, *refs):
    parts, outs, held = refs[:8], refs[8:12], refs[12]
    total = parts[0][...]
    for part in parts[1:]:
        total = total + part[...]
    for place in range(4):
        held[place] = total[place * share : (place + 1) * share]
    here = crossing(lax.axis_index("row"))
    for by, ref in enumerate(outs):
        ref[...] = held[(here + by) % 4]


def settle_body(*refs):
    parts, out_ref, held = refs[:4], refs[4], refs[5]
    here = crossing(lax.axis_index("row"))
    for by, part in enumerate(parts):
        held[(here + 4 - by) % 4] = part[...]
    for slot in range(4):
        out_ref[slot // 2, :, slot % 2, :] = held[slot]


def per_device(fresh, target, carried, returning, weights, section_blocks):
    tick_count = fresh.shape[0]
    cells = (
        tick_count
        * fresh.shape[1]
        * lax.axis_size("dp")
        * fresh.shape[2]
        * lax.axis_size("row")
        * fresh.shape[3]
    )
    segments = lax.axis_size("segment")
    dp_count = lax.axis_size("dp")
    rungs = dp_count // 2
    share = DEPTH // (2 * dp_count)
    flat = OWN * WD
    fresh = fresh.reshape(2, flat, 2 * C)
    target = target.reshape(flat, 2 * C)
    carried = carried.reshape(flat, 2 * C)
    returning = returning.reshape(2, flat, 2 * C)
    weights = weights.reshape(4, DEPTH, C)
    swap = [(0, 1), (1, 0)]
    onward = [(i, i + 1) for i in range(segments - 1)]
    homeward = [(i + 1, i) for i in range(segments - 1)]

    def across(by):
        pairs = []
        for row in range(2):
            for rung in range(rungs):
                for low in range(2):
                    there = (2 * row + low + by) % 4
                    pairs.append(
                        (
                            row * dp_count + 2 * rung + low,
                            (there // 2) * dp_count + 2 * rung + there % 2,
                        )
                    )
        return pairs

    def deal(parts):
        dealt = [parts[0]]
        for by in range(1, 4):
            dealt.append(lax.ppermute(parts[by], ("row", "dp"), across(by)))
        return dealt

    conv_flops = 6 * DEPTH * C
    other_pair = lax.ppermute(returning, "row", swap)
    (packed,) = call(
        pack_body,
        [(2 * flat, 2 * C)],
        [pltpu.SemaphoreType.DMA((3,))],
        tuple(in_hbm(value) for value in (fresh, carried, target)),
        8,
        1 << 20,
        space=pltpu.HBM,
    )
    other_pack = lax.ppermute(packed, "row", swap)
    plain, turned = prepare(weights)

    sent, *dealt = call(
        backward_full_body,
        [(2, WINDOW * WD, 2 * C)] + [(PACK, C)] * 4,
        backward_scratch(FULL * WD),
        (section_blocks, returning, other_pair, plain, turned),
        24,
        8 * conv_flops * FULL * WD,
        smem=(0,),
    )
    came_back = lax.ppermute(sent, "segment", homeward)
    early = deal(dealt)
    (made,) = call(
        forward_full_body,
        [(WINDOW * WD, 2 * C)],
        forward_scratch(FULL * WD),
        (section_blocks, packed[:flat], other_pack, plain),
        24,
        4 * conv_flops * FULL * WD,
        smem=(0,),
    )
    came_on = lax.ppermute(made, "segment", onward)
    mid, *dealt = call(
        backward_window_body,
        [(2, 2, WINDOW * WD, C)] + [(PACK, C)] * 4,
        backward_scratch(WINDOW * WD),
        (section_blocks, came_back, made, target, other_pack, plain, turned),
        24,
        8 * conv_flops * WINDOW * WD,
        smem=(0,),
    )
    late = deal(dealt)
    (back,) = call(
        backward_tail_body,
        [(2, flat, 2 * C)],
        backward_scratch(WINDOW * WD)[:2] + backward_scratch(WINDOW * WD)[3:7],
        (mid, plain, turned),
        24,
        2 * conv_flops * WINDOW * WD,
    )
    (early_grad,) = call(
        early_grad_body, [(C, DEPTH)], grad_scratch(), tuple(early), 24, 4 * conv_flops * flat
    )
    partial_sums = call(
        functools.partial(late_grad_body, 1.0 / math.sqrt(cells), share),
        [(4 * share, C)] * rungs,
        grad_scratch()
        + [pltpu.VMEM((DEPTH, C), F32), pltpu.VMEM((rungs, 4 * share, C), F32)],
        tuple(late) + (early_grad,),
        24,
        4 * conv_flops * flat,
    )
    spread = [partial_sums[0]]
    for by in FARTHEST:
        climbs = [
            (2 * rung + low, 2 * ((rung + by) % rungs) + low)
            for rung in range(rungs)
            for low in range(2)
        ]
        spread.append(lax.ppermute(partial_sums[by], "dp", climbs))
    (produced,) = call(
        forward_window_body,
        [(flat, 2 * C)],
        forward_scratch(WINDOW * WD),
        (section_blocks, came_on, fresh, other_pack, plain),
        24,
        4 * conv_flops * WINDOW * WD,
        smem=(0,),
    )
    folded = call(
        functools.partial(fold_body, share),
        [(share, C)] * 4,
        [pltpu.VMEM((4, share, C), F32)],
        tuple(spread),
        8,
        1 << 20,
    )
    settled = deal(folded)
    (grad_weights,) = call(
        settle_body,
        [(2, share, 2, C)],
        [pltpu.VMEM((4, share, C), F32)],
        tuple(settled),
        8,
        1 << 20,
    )
    return (
        grad_weights.transpose(0, 2, 1, 3)[None],
        produced.reshape(1, 1, OWN, WD, 2 * C),
        back.reshape(1, 2, 1, OWN, WD, 2 * C),
    )


FARTHEST = (4, 3, 5, 2, 6, 1, 7)


def solution(mesh):
    return jax.shard_map(
        per_device,
        mesh=mesh,
        in_specs=(
            P(None, "dp", "row", None, None),
            P(None, "dp", "row", None, None),
            P("segment", "dp", "row", None, None),
            P("segment", None, "dp", "row", None, None),
            P("segment", None, None, None, None),
            P("segment"),
        ),
        out_specs=(
            P("segment", None, None, ("row", "dp"), None),
            P("segment", "dp", "row", None, None),
            P("segment", None, "dp", "row", None, None),
        ),
        check_vma=False,
    )
```

```python
import functools
import math

import jax
import jax.numpy as jnp
from jax import lax
from jax.experimental import pallas as pl
from jax.experimental.pallas import tpu as pltpu
from jax.sharding import PartitionSpec as P


F32 = jnp.float32
BF16 = jnp.bfloat16
C = 128
TAPS = 9
DEPTH = TAPS * C
WD = 16
OWN = 8
HALF = 4
FULL = 16
WINDOW = 12
VIEW = OWN + 2
PACK = (VIEW + OWN) * WD
MEGA = 1 << 20


def params(mib):
    return pltpu.CompilerParams(vmem_limit_bytes=mib * MEGA)


def cost(flops, nbytes):
    return pl.CostEstimate(flops=flops, bytes_accessed=nbytes, transcendentals=0)


def whole(memory_space=pltpu.VMEM):
    return pl.BlockSpec(memory_space=memory_space)


def call(body, out_shape, scratch, args, mib, flops, smem=(), space=pltpu.VMEM, out_space=pltpu.VMEM):
    in_specs = [whole(pltpu.SMEM if i in smem else space) for i in range(len(args))]
    outs = [jax.ShapeDtypeStruct(shape, F32) for shape in out_shape]
    nbytes = sum(4 * math.prod(shape) for shape in out_shape)
    return pl.pallas_call(
        body,
        out_shape=outs,
        in_specs=in_specs,
        out_specs=[whole(out_space) for _ in outs],
        scratch_shapes=scratch,
        compiler_params=params(mib),
        cost_estimate=cost(flops, nbytes),
    )(*args)


def in_hbm(value):
    return pltpu.with_memory_space_constraint(value, pltpu.HBM)


def rows(start, count):
    return pl.ds(pl.multiple_of(start * WD, HALF * WD), count * WD)


def hi_lo(value):
    high = value.astype(BF16)
    return high, (value - high.astype(F32)).astype(BF16)


def shifted(value):
    count = value.shape[0]
    column = lax.broadcasted_iota(jnp.int32, value.shape, 0) % WD
    left = jnp.where(column == 0, 0.0, pltpu.roll(value, 1, 0))
    right = jnp.where(column == WD - 1, 0.0, pltpu.roll(value, count - 1, 0))
    return left, value, right


def fill_patches(value, high_ref, low_ref):
    count = value.shape[0]
    for tap, moved in enumerate(shifted(value)):
        high, low = hi_lo(moved)
        high_ref[WD : WD + count, tap * C : (tap + 1) * C] = high
        low_ref[WD : WD + count, tap * C : (tap + 1) * C] = low


def clear_rim(ref, count):
    rim = jnp.zeros((WD,) + tuple(ref.shape[1:]), ref.dtype)
    ref[0:WD] = rim
    ref[WD + count : 2 * WD + count] = rim


def gathered(ref, count):
    return jnp.concatenate([ref[d * WD : d * WD + count, :] for d in range(3)], axis=1)


def conv(high_ref, low_ref, kernel_ref, slot, count):
    both = jnp.dot(gathered(high_ref, count), kernel_ref[slot], preferred_element_type=F32)
    rest = jnp.dot(
        gathered(low_ref, count), kernel_ref[slot, :, 0:C], preferred_element_type=F32
    )
    return both[:, :C] + (both[:, C:] + rest)


def logistic(value):
    return 1.0 / (1.0 + jnp.exp(-value))


def prepare_body(weight_ref, plain_ref, turned_ref, held, sems):
    slots = weight_ref.shape[0]
    for slot in range(slots):
        pltpu.make_async_copy(weight_ref.at[slot], held.at[slot], sems.at[slot]).start()

    def step(slot, carry):
        pltpu.make_async_copy(weight_ref.at[slot], held.at[slot], sems.at[slot]).wait()
        for tap in range(TAPS):
            block = held[slot, tap * C : (tap + 1) * C, :]
            high, low = hi_lo(block)
            plain_ref[slot, tap * C : (tap + 1) * C, 0:C] = high
            plain_ref[slot, tap * C : (tap + 1) * C, C:] = low
            high, low = hi_lo(block.T)
            back = TAPS - 1 - tap
            turned_ref[slot, back * C : (back + 1) * C, 0:C] = high
            turned_ref[slot, back * C : (back + 1) * C, C:] = low
        return carry

    lax.fori_loop(0, slots, step, 0)


def prepare(weights):
    slots = weights.shape[0]
    shape = jax.ShapeDtypeStruct((slots, DEPTH, 2 * C), BF16)
    return pl.pallas_call(
        prepare_body,
        out_shape=[shape, shape],
        in_specs=[whole(pltpu.HBM)],
        out_specs=[whole(), whole()],
        scratch_shapes=[
            pltpu.VMEM((slots, DEPTH, C), F32),
            pltpu.SemaphoreType.DMA((slots,)),
        ],
        compiler_params=params(16),
        cost_estimate=cost(slots * DEPTH * C * 8, slots * DEPTH * C * 12),
    )(in_hbm(weights))


def pack_body(fresh_ref, carried_ref, target_ref, out_ref, sems):
    first = lax.axis_index("segment") == 0
    start = HALF * (1 - lax.axis_index("row"))
    top = out_ref.at[0 : OWN * WD]
    from_fresh = pltpu.make_async_copy(fresh_ref.at[0], top, sems.at[0])
    from_carried = pltpu.make_async_copy(carried_ref, top, sems.at[0])
    others = (
        pltpu.make_async_copy(
            target_ref.at[rows(start, HALF)], out_ref.at[OWN * WD : WINDOW * WD], sems.at[1]
        ),
        pltpu.make_async_copy(
            fresh_ref.at[1, rows(start, HALF)], out_ref.at[WINDOW * WD :], sems.at[2]
        ),
    )

    @pl.when(first)
    def _():
        from_fresh.start()

    @pl.when(jnp.logical_not(first))
    def _():
        from_carried.start()

    for copy in others:
        copy.start()

    @pl.when(first)
    def _():
        from_fresh.wait()

    @pl.when(jnp.logical_not(first))
    def _():
        from_carried.wait()

    for copy in others:
        copy.wait()


def put_halves(ref, where, value):
    ref[0, where] = value[:, :C]
    ref[1, where] = value[:, C:]


def forward_loop(state_ref, high_ref, low_ref, kernel_ref, blocks_ref, count):
    clear_rim(high_ref, count)
    clear_rim(low_ref, count)

    def step(slot, carry):
        half = slot % 2
        source = state_ref[1 - half]
        fill_patches(source * logistic(source), high_ref, low_ref)
        state_ref[half] = state_ref[half] + conv(high_ref, low_ref, kernel_ref, slot, count)
        return carry

    lax.fori_loop(0, 2 * blocks_ref[0], step, 0)


def forward_full_body(blocks_ref, own_ref, other_ref, kernel_ref, out_ref, state, high, low):
    row = lax.axis_index("row")
    put_halves(state, rows(OWN * row, OWN), own_ref[...])
    put_halves(state, rows(OWN * (1 - row), OWN), other_ref[0 : OWN * WD])
    forward_loop(state, high, low, kernel_ref, blocks_ref, FULL * WD)
    part = rows(HALF * row, WINDOW)
    out_ref[:, :C] = state[0, part]
    out_ref[:, C:] = state[1, part]


def forward_window_body(
    blocks_ref, came_ref, fresh_ref, other_ref, kernel_ref, out_ref, state, high, low
):
    row = lax.axis_index("row")
    first = lax.axis_index("segment") == 0

    @pl.when(first)
    def _():
        put_halves(state, rows(HALF * row, OWN), fresh_ref[1])
        put_halves(state, rows(OWN * (1 - row), HALF), other_ref[WINDOW * WD :])

    @pl.when(jnp.logical_not(first))
    def _():
        put_halves(state, pl.ds(0, WINDOW * WD), came_ref[...])

    forward_loop(state, high, low, kernel_ref, blocks_ref, WINDOW * WD)
    part = rows(HALF * row, OWN)
    out_ref[:, :C] = state[0, part]
    out_ref[:, C:] = state[1, part]


def clear_picked(picked, blocks_ref):
    @pl.when(blocks_ref[0] < 2)
    def _():
        picked[2] = jnp.zeros((PACK, C), F32)
        picked[3] = jnp.zeros((PACK, C), F32)


def pick(picked, slot, source_pad, grads, half, own):
    picked[slot, 0 : VIEW * WD] = source_pad[rows(own, VIEW)]
    picked[slot, VIEW * WD :] = grads[half, rows(own, OWN)]


def backward_step(slot, half, state, grads, plain_ref, turned_ref, pads, count, picked, own):
    source_high, source_low, grad_high, grad_low = pads[:4]
    source = state[1 - half]
    grad = grads[half]
    gate = logistic(source)
    field = source * gate
    fill_patches(field, source_high, source_low)
    fill_patches(grad, grad_high, grad_low)
    if picked is not None:
        pads[4][WD : WD + count] = field
        pick(picked, slot, pads[4], grads, half, own)
    state[half] = state[half] - conv(source_high, source_low, plain_ref, slot, count)
    slope = gate * (1.0 + source * (1.0 - gate))
    grads[1 - half] = grads[1 - half] + slope * conv(
        grad_high, grad_low, turned_ref, slot, count
    )


def backward_loop(
    state, grads, plain_ref, turned_ref, blocks_ref, pads, picked, own, count, lowest
):
    for ref in pads:
        clear_rim(ref, count)
    clear_picked(picked, blocks_ref)
    top = 2 * blocks_ref[0] - 1

    def step(turn, carry):
        slot = top - turn
        backward_step(
            slot, slot % 2, state, grads, plain_ref, turned_ref, pads, count, picked, own
        )
        return carry

    lax.fori_loop(0, top + 1 - lowest, step, 0)


def crossing(row):
    return 2 * row + lax.axis_index("dp") % 2


def hand_out(picked, refs):
    place = crossing(lax.axis_index("row"))
    for by, ref in enumerate(refs):
        ref[...] = picked[(place + by) % 4]


def backward_full_body(
    blocks_ref, own_ref, other_ref, plain_ref, turned_ref, out_ref, *rest
):
    outs, (state, grads, picked), pads = rest[:4], rest[4:7], rest[7:]
    row = lax.axis_index("row")
    for ref, index in ((state, 0), (grads, 1)):
        put_halves(ref, rows(OWN * row, OWN), own_ref[index])
        put_halves(ref, rows(OWN * (1 - row), OWN), other_ref[index])
    backward_loop(
        state, grads, plain_ref, turned_ref, blocks_ref, pads, picked, OWN * row, FULL * WD, 0
    )
    part = rows(HALF * row, WINDOW)
    for ref, index in ((state, 0), (grads, 1)):
        out_ref[index, :, :C] = ref[0, part]
        out_ref[index, :, C:] = ref[1, part]
    hand_out(picked, outs)


def backward_window_body(
    blocks_ref,
    came_ref,
    made_ref,
    target_ref,
    other_ref,
    plain_ref,
    turned_ref,
    mid_ref,
    *rest,
):
    outs, (state, grads, picked), pads = rest[:4], rest[4:7], rest[7:]
    row = lax.axis_index("row")
    final = lax.axis_index("segment") == lax.axis_size("segment") - 1

    @pl.when(final)
    def _():
        put_halves(grads, rows(HALF * row, OWN), target_ref[...])
        put_halves(grads, rows(OWN * (1 - row), HALF), other_ref[OWN * WD : WINDOW * WD])
        for half in range(2):
            made = made_ref[:, half * C : (half + 1) * C]
            state[half] = made
            grads[half] = made - grads[half]

    @pl.when(jnp.logical_not(final))
    def _():
        put_halves(state, pl.ds(0, WINDOW * WD), came_ref[0])
        put_halves(grads, pl.ds(0, WINDOW * WD), came_ref[1])

    count = WINDOW * WD
    own = HALF * row
    backward_loop(
        state, grads, plain_ref, turned_ref, blocks_ref, pads, picked, own, count, 1
    )
    source = state[1]
    pads[4][WD : WD + count] = source * logistic(source)
    pick(picked, 0, pads[4], grads, 0, own)
    hand_out(picked, outs)
    mid_ref[0] = state[...]
    mid_ref[1] = grads[...]


def backward_tail_body(mid_ref, plain_ref, turned_ref, out_ref, state, grads, *pads):
    state[...] = mid_ref[0]
    grads[...] = mid_ref[1]
    for ref in pads:
        clear_rim(ref, WINDOW * WD)
    backward_step(
        0, 0, state, grads, plain_ref, turned_ref, pads, WINDOW * WD, None, None
    )
    part = rows(HALF * lax.axis_index("row"), OWN)
    for ref, index in ((state, 0), (grads, 1)):
        out_ref[index, :, :C] = ref[0, part]
        out_ref[index, :, C:] = ref[1, part]


def forward_scratch(count):
    return [
        pltpu.VMEM((2, count, C), F32),
        pltpu.VMEM((count + 2 * WD, 3 * C), BF16),
        pltpu.VMEM((count + 2 * WD, 3 * C), BF16),
    ]


def backward_scratch(count):
    padded = pltpu.VMEM((count + 2 * WD, 3 * C), BF16)
    return [
        pltpu.VMEM((2, count, C), F32),
        pltpu.VMEM((2, count, C), F32),
        pltpu.VMEM((4, PACK, C), F32),
        padded,
        padded,
        padded,
        padded,
        pltpu.VMEM((count + 2 * WD, C), F32),
    ]


def kernel_grad(parts, high_ref, low_ref, turned_ref):
    for index, part in enumerate(parts):
        at = slice(index * OWN * WD, (index + 1) * OWN * WD)
        for tap, moved in enumerate(shifted(part[0 : VIEW * WD])):
            high, low = hi_lo(moved)
            for drop in range(3):
                lanes = slice((3 * drop + tap) * C, (3 * drop + tap + 1) * C)
                high_ref[at, lanes] = high[drop * WD : (drop + OWN) * WD]
                low_ref[at, lanes] = low[drop * WD : (drop + OWN) * WD]
        high, low = hi_lo(part[VIEW * WD :].T)
        turned_ref[0:C, at] = high
        turned_ref[C:, at] = low
    both = jnp.dot(turned_ref[...], high_ref[...], preferred_element_type=F32)
    rest = jnp.dot(turned_ref[0:C], low_ref[...], preferred_element_type=F32)
    return both[:C] + (both[C:] + rest)


def early_grad_body(*refs):
    parts, out_ref, scratch = refs[:4], refs[4], refs[5:]
    out_ref[...] = kernel_grad(parts, *scratch)


def late_grad_body(scale, share, *refs):
    parts, early_ref, out_ref, scratch = refs[:4], refs[4], refs[5], refs[6:9]
    total_ref, held, sem = refs[9:]
    total = (kernel_grad(parts, *scratch) + early_ref[...]) * scale
    for tap in range(TAPS):
        total_ref[tap * C : (tap + 1) * C, :] = total[:, tap * C : (tap + 1) * C].T
    for owner in range(held.shape[0]):
        held[owner] = total_ref[owner * share : (owner + 1) * share]
    copy = pltpu.make_async_copy(held, out_ref, sem)
    copy.start()
    copy.wait()


def grad_scratch():
    count = 4 * OWN * WD
    return [
        pltpu.VMEM((count, DEPTH), BF16),
        pltpu.VMEM((count, DEPTH), BF16),
        pltpu.VMEM((2 * C, count), BF16),
    ]


def settle_body(in_ref, out_ref):
    rungs = in_ref.shape[0] // 4
    for slot in range(4):
        first = (slot // 2) * 2 * rungs + slot % 2
        total = in_ref[first]
        for rung in range(1, rungs):
            total = total + in_ref[first + 2 * rung]
        out_ref[slot // 2, :, slot % 2, :] = total


def per_device(fresh, target, carried, returning, weights, section_blocks):
    tick_count = fresh.shape[0]
    cells = (
        tick_count
        * fresh.shape[1]
        * lax.axis_size("dp")
        * fresh.shape[2]
        * lax.axis_size("row")
        * fresh.shape[3]
    )
    segments = lax.axis_size("segment")
    dp_count = lax.axis_size("dp")
    rungs = dp_count // 2
    share = DEPTH // (2 * dp_count)
    flat = OWN * WD
    fresh = fresh.reshape(2, flat, 2 * C)
    target = target.reshape(flat, 2 * C)
    carried = carried.reshape(flat, 2 * C)
    returning = returning.reshape(2, flat, 2 * C)
    weights = weights.reshape(4, DEPTH, C)
    swap = [(0, 1), (1, 0)]
    onward = [(i, i + 1) for i in range(segments - 1)]
    homeward = [(i + 1, i) for i in range(segments - 1)]

    def across(by):
        pairs = []
        for row in range(2):
            for rung in range(rungs):
                for low in range(2):
                    there = (2 * row + low + by) % 4
                    pairs.append(
                        (
                            row * dp_count + 2 * rung + low,
                            (there // 2) * dp_count + 2 * rung + there % 2,
                        )
                    )
        return pairs

    def deal(parts):
        dealt = [parts[0]]
        for by in range(1, 4):
            dealt.append(lax.ppermute(parts[by], ("row", "dp"), across(by)))
        return dealt

    conv_flops = 6 * DEPTH * C
    other_pair = lax.ppermute(returning, "row", swap)
    (packed,) = call(
        pack_body,
        [(2 * flat, 2 * C)],
        [pltpu.SemaphoreType.DMA((3,))],
        tuple(in_hbm(value) for value in (fresh, carried, target)),
        8,
        1 << 20,
        space=pltpu.HBM,
    )
    other_pack = lax.ppermute(packed, "row", swap)
    plain, turned = prepare(weights)

    sent, *dealt = call(
        backward_full_body,
        [(2, WINDOW * WD, 2 * C)] + [(PACK, C)] * 4,
        backward_scratch(FULL * WD),
        (section_blocks, returning, other_pair, plain, turned),
        24,
        8 * conv_flops * FULL * WD,
        smem=(0,),
    )
    came_back = lax.ppermute(sent, "segment", homeward)
    early = deal(dealt)
    (made,) = call(
        forward_full_body,
        [(WINDOW * WD, 2 * C)],
        forward_scratch(FULL * WD),
        (section_blocks, packed[:flat], other_pack, plain),
        24,
        4 * conv_flops * FULL * WD,
        smem=(0,),
    )
    came_on = lax.ppermute(made, "segment", onward)
    mid, *dealt = call(
        backward_window_body,
        [(2, 2, WINDOW * WD, C)] + [(PACK, C)] * 4,
        backward_scratch(WINDOW * WD),
        (section_blocks, came_back, made, target, other_pack, plain, turned),
        24,
        8 * conv_flops * WINDOW * WD,
        smem=(0,),
    )
    late = deal(dealt)
    (back,) = call(
        backward_tail_body,
        [(2, flat, 2 * C)],
        backward_scratch(WINDOW * WD)[:2] + backward_scratch(WINDOW * WD)[3:7],
        (mid, plain, turned),
        24,
        2 * conv_flops * WINDOW * WD,
    )
    (early_grad,) = call(
        early_grad_body, [(C, DEPTH)], grad_scratch(), tuple(early), 24, 4 * conv_flops * flat
    )
    owners = 2 * dp_count
    (partial_sums,) = call(
        functools.partial(late_grad_body, 1.0 / math.sqrt(cells), share),
        [(owners, share, C)],
        grad_scratch()
        + [
            pltpu.VMEM((DEPTH, C), F32),
            pltpu.VMEM((owners, share, C), F32),
            pltpu.SemaphoreType.DMA,
        ],
        tuple(late) + (early_grad,),
        24,
        4 * conv_flops * flat,
        out_space=pltpu.HBM,
    )
    spread = lax.all_to_all(partial_sums, ("row", "dp"), 0, 0, tiled=True)
    (produced,) = call(
        forward_window_body,
        [(flat, 2 * C)],
        forward_scratch(WINDOW * WD),
        (section_blocks, came_on, fresh, other_pack, plain),
        24,
        4 * conv_flops * WINDOW * WD,
        smem=(0,),
    )
    (grad_weights,) = call(settle_body, [(2, share, 2, C)], [], (spread,), 8, 1 << 20)
    return (
        grad_weights.transpose(0, 2, 1, 3)[None],
        produced.reshape(1, 1, OWN, WD, 2 * C),
        back.reshape(1, 2, 1, OWN, WD, 2 * C),
    )


def solution(mesh):
    return jax.shard_map(
        per_device,
        mesh=mesh,
        in_specs=(
            P(None, "dp", "row", None, None),
            P(None, "dp", "row", None, None),
            P("segment", "dp", "row", None, None),
            P("segment", None, "dp", "row", None, None),
            P("segment", None, None, None, None),
            P("segment"),
        ),
        out_specs=(
            P("segment", None, None, ("row", "dp"), None),
            P("segment", "dp", "row", None, None),
            P("segment", None, "dp", "row", None, None),
        ),
        check_vma=False,
    )
```

```python
import functools
import math

import jax
import jax.numpy as jnp
from jax import lax
from jax.experimental import pallas as pl
from jax.experimental.pallas import tpu as pltpu
from jax.sharding import PartitionSpec as P


F32 = jnp.float32
BF16 = jnp.bfloat16
C = 128
TAPS = 9
DEPTH = TAPS * C
WD = 16
OWN = 8
HALF = 4
FULL = 16
WINDOW = 12
VIEW = OWN + 2
PACK = (VIEW + OWN) * WD
MEGA = 1 << 20


def params(mib):
    return pltpu.CompilerParams(vmem_limit_bytes=mib * MEGA)


def cost(flops, nbytes):
    return pl.CostEstimate(flops=flops, bytes_accessed=nbytes, transcendentals=0)


def whole(memory_space=pltpu.VMEM):
    return pl.BlockSpec(memory_space=memory_space)


def call(body, out_shape, scratch, args, mib, flops, smem=(), space=pltpu.VMEM):
    in_specs = [whole(pltpu.SMEM if i in smem else space) for i in range(len(args))]
    outs = [jax.ShapeDtypeStruct(shape, F32) for shape in out_shape]
    nbytes = sum(4 * math.prod(shape) for shape in out_shape)
    return pl.pallas_call(
        body,
        out_shape=outs,
        in_specs=in_specs,
        out_specs=[whole() for _ in outs],
        scratch_shapes=scratch,
        compiler_params=params(mib),
        cost_estimate=cost(flops, nbytes),
    )(*args)


def in_hbm(value):
    return pltpu.with_memory_space_constraint(value, pltpu.HBM)


def rows(start, count):
    return pl.ds(pl.multiple_of(start * WD, HALF * WD), count * WD)


def hi_lo(value):
    high = value.astype(BF16)
    return high, (value - high.astype(F32)).astype(BF16)


def shifted(value):
    count = value.shape[0]
    column = lax.broadcasted_iota(jnp.int32, value.shape, 0) % WD
    left = jnp.where(column == 0, 0.0, pltpu.roll(value, 1, 0))
    right = jnp.where(column == WD - 1, 0.0, pltpu.roll(value, count - 1, 0))
    return left, value, right


def fill_patches(value, high_ref, low_ref):
    count = value.shape[0]
    for tap, moved in enumerate(shifted(value)):
        high, low = hi_lo(moved)
        high_ref[WD : WD + count, tap * C : (tap + 1) * C] = high
        low_ref[WD : WD + count, tap * C : (tap + 1) * C] = low


def clear_rim(ref, count):
    rim = jnp.zeros((WD,) + tuple(ref.shape[1:]), ref.dtype)
    ref[0:WD] = rim
    ref[WD + count : 2 * WD + count] = rim


def gathered(ref, count):
    return jnp.concatenate([ref[d * WD : d * WD + count, :] for d in range(3)], axis=1)


def conv(high_ref, low_ref, kernel_ref, slot, count):
    both = jnp.dot(gathered(high_ref, count), kernel_ref[slot], preferred_element_type=F32)
    rest = jnp.dot(
        gathered(low_ref, count), kernel_ref[slot, :, 0:C], preferred_element_type=F32
    )
    return both[:, :C] + (both[:, C:] + rest)


def logistic(value):
    return 1.0 / (1.0 + jnp.exp(-value))


def prepare_body(weight_ref, plain_ref, turned_ref, held, sems):
    slots = weight_ref.shape[0]
    for slot in range(slots):
        pltpu.make_async_copy(weight_ref.at[slot], held.at[slot], sems.at[slot]).start()

    def step(slot, carry):
        pltpu.make_async_copy(weight_ref.at[slot], held.at[slot], sems.at[slot]).wait()
        for tap in range(TAPS):
            block = held[slot, tap * C : (tap + 1) * C, :]
            high, low = hi_lo(block)
            plain_ref[slot, tap * C : (tap + 1) * C, 0:C] = high
            plain_ref[slot, tap * C : (tap + 1) * C, C:] = low
            high, low = hi_lo(block.T)
            back = TAPS - 1 - tap
            turned_ref[slot, back * C : (back + 1) * C, 0:C] = high
            turned_ref[slot, back * C : (back + 1) * C, C:] = low
        return carry

    lax.fori_loop(0, slots, step, 0)


def prepare(weights):
    slots = weights.shape[0]
    shape = jax.ShapeDtypeStruct((slots, DEPTH, 2 * C), BF16)
    return pl.pallas_call(
        prepare_body,
        out_shape=[shape, shape],
        in_specs=[whole(pltpu.HBM)],
        out_specs=[whole(), whole()],
        scratch_shapes=[
            pltpu.VMEM((slots, DEPTH, C), F32),
            pltpu.SemaphoreType.DMA((slots,)),
        ],
        compiler_params=params(16),
        cost_estimate=cost(slots * DEPTH * C * 8, slots * DEPTH * C * 12),
    )(in_hbm(weights))


def pack_body(fresh_ref, carried_ref, target_ref, out_ref, sems):
    first = lax.axis_index("segment") == 0
    start = HALF * (1 - lax.axis_index("row"))
    top = out_ref.at[0 : OWN * WD]
    from_fresh = pltpu.make_async_copy(fresh_ref.at[0], top, sems.at[0])
    from_carried = pltpu.make_async_copy(carried_ref, top, sems.at[0])
    others = (
        pltpu.make_async_copy(
            target_ref.at[rows(start, HALF)], out_ref.at[OWN * WD : WINDOW * WD], sems.at[1]
        ),
        pltpu.make_async_copy(
            fresh_ref.at[1, rows(start, HALF)], out_ref.at[WINDOW * WD :], sems.at[2]
        ),
    )

    @pl.when(first)
    def _():
        from_fresh.start()

    @pl.when(jnp.logical_not(first))
    def _():
        from_carried.start()

    for copy in others:
        copy.start()

    @pl.when(first)
    def _():
        from_fresh.wait()

    @pl.when(jnp.logical_not(first))
    def _():
        from_carried.wait()

    for copy in others:
        copy.wait()


def put_halves(ref, where, value):
    ref[0, where] = value[:, :C]
    ref[1, where] = value[:, C:]


def forward_loop(state_ref, high_ref, low_ref, kernel_ref, blocks_ref, count):
    clear_rim(high_ref, count)
    clear_rim(low_ref, count)

    def step(slot, carry):
        half = slot % 2
        source = state_ref[1 - half]
        fill_patches(source * logistic(source), high_ref, low_ref)
        state_ref[half] = state_ref[half] + conv(high_ref, low_ref, kernel_ref, slot, count)
        return carry

    lax.fori_loop(0, 2 * blocks_ref[0], step, 0)


def forward_crop(blocks_ref, own_ref, other_ref, kernel_ref, state, high, low):
    row = lax.axis_index("row")
    put_halves(state, rows(OWN * row, OWN), own_ref[0 : OWN * WD])
    put_halves(state, rows(OWN * (1 - row), OWN), other_ref[0 : OWN * WD])
    forward_loop(state, high, low, kernel_ref, blocks_ref, FULL * WD)
    return rows(HALF * row, WINDOW)


def is_final():
    return lax.axis_index("segment") == lax.axis_size("segment") - 1


def forward_full_body(blocks_ref, own_ref, other_ref, kernel_ref, out_ref, state, high, low):
    @pl.when(jnp.logical_not(is_final()))
    def _():
        part = forward_crop(blocks_ref, own_ref, other_ref, kernel_ref, state, high, low)
        out_ref[:, :C] = state[0, part]
        out_ref[:, C:] = state[1, part]


def forward_window_body(
    blocks_ref, came_ref, fresh_ref, other_ref, kernel_ref, out_ref, state, high, low
):
    row = lax.axis_index("row")
    first = lax.axis_index("segment") == 0

    @pl.when(first)
    def _():
        put_halves(state, rows(HALF * row, OWN), fresh_ref[1])
        put_halves(state, rows(OWN * (1 - row), HALF), other_ref[WINDOW * WD :])

    @pl.when(jnp.logical_not(first))
    def _():
        put_halves(state, pl.ds(0, WINDOW * WD), came_ref[...])

    forward_loop(state, high, low, kernel_ref, blocks_ref, WINDOW * WD)
    part = rows(HALF * row, OWN)
    out_ref[:, :C] = state[0, part]
    out_ref[:, C:] = state[1, part]


def clear_picked(picked, blocks_ref):
    @pl.when(blocks_ref[0] < 2)
    def _():
        picked[2] = jnp.zeros((PACK, C), F32)
        picked[3] = jnp.zeros((PACK, C), F32)


def pick(picked, slot, source_pad, grads, half, own):
    picked[slot, 0 : VIEW * WD] = source_pad[rows(own, VIEW)]
    picked[slot, VIEW * WD :] = grads[half, rows(own, OWN)]


def backward_step(slot, half, state, grads, plain_ref, turned_ref, pads, count, picked, own):
    source_high, source_low, grad_high, grad_low = pads[:4]
    source = state[1 - half]
    grad = grads[half]
    gate = logistic(source)
    field = source * gate
    fill_patches(field, source_high, source_low)
    fill_patches(grad, grad_high, grad_low)
    if picked is not None:
        pads[4][WD : WD + count] = field
        pick(picked, slot, pads[4], grads, half, own)
    state[half] = state[half] - conv(source_high, source_low, plain_ref, slot, count)
    slope = gate * (1.0 + source * (1.0 - gate))
    grads[1 - half] = grads[1 - half] + slope * conv(
        grad_high, grad_low, turned_ref, slot, count
    )


def backward_loop(
    state, grads, plain_ref, turned_ref, blocks_ref, pads, picked, own, count, lowest
):
    for ref in pads:
        clear_rim(ref, count)
    clear_picked(picked, blocks_ref)
    top = 2 * blocks_ref[0] - 1

    def step(turn, carry):
        slot = top - turn
        backward_step(
            slot, slot % 2, state, grads, plain_ref, turned_ref, pads, count, picked, own
        )
        return carry

    lax.fori_loop(0, top + 1 - lowest, step, 0)


def crossing(row):
    return 2 * row + lax.axis_index("dp") % 2


def hand_out(picked, refs):
    place = crossing(lax.axis_index("row"))
    for by, ref in enumerate(refs):
        ref[...] = picked[(place + by) % 4]


def backward_full_body(
    blocks_ref, own_ref, other_ref, plain_ref, turned_ref, out_ref, *rest
):
    outs, (state, grads, picked), pads = rest[:4], rest[4:7], rest[7:]
    row = lax.axis_index("row")
    for ref, index in ((state, 0), (grads, 1)):
        put_halves(ref, rows(OWN * row, OWN), own_ref[index])
        put_halves(ref, rows(OWN * (1 - row), OWN), other_ref[index])
    backward_loop(
        state, grads, plain_ref, turned_ref, blocks_ref, pads, picked, OWN * row, FULL * WD, 0
    )
    part = rows(HALF * row, WINDOW)
    for ref, index in ((state, 0), (grads, 1)):
        out_ref[index, :, :C] = ref[0, part]
        out_ref[index, :, C:] = ref[1, part]
    hand_out(picked, outs)


def backward_window_body(
    blocks_ref,
    came_ref,
    own_ref,
    target_ref,
    other_ref,
    plain_ref,
    turned_ref,
    mid_ref,
    *rest,
):
    outs, (state, grads, picked), pads = rest[:4], rest[4:7], rest[7:12]
    crop_state, crop_high, crop_low = rest[12:]
    row = lax.axis_index("row")
    final = is_final()

    @pl.when(final)
    def _():
        part = forward_crop(
            blocks_ref, own_ref, other_ref, plain_ref, crop_state, crop_high, crop_low
        )
        put_halves(grads, rows(HALF * row, OWN), target_ref[...])
        put_halves(grads, rows(OWN * (1 - row), HALF), other_ref[OWN * WD : WINDOW * WD])
        for half in range(2):
            made = crop_state[half, part]
            state[half] = made
            grads[half] = made - grads[half]

    @pl.when(jnp.logical_not(final))
    def _():
        put_halves(state, pl.ds(0, WINDOW * WD), came_ref[0])
        put_halves(grads, pl.ds(0, WINDOW * WD), came_ref[1])

    count = WINDOW * WD
    own = HALF * row
    backward_loop(
        state, grads, plain_ref, turned_ref, blocks_ref, pads, picked, own, count, 1
    )
    source = state[1]
    pads[4][WD : WD + count] = source * logistic(source)
    pick(picked, 0, pads[4], grads, 0, own)
    hand_out(picked, outs)
    mid_ref[0] = state[...]
    mid_ref[1] = grads[...]


def backward_tail_body(mid_ref, plain_ref, turned_ref, out_ref, state, grads, *pads):
    state[...] = mid_ref[0]
    grads[...] = mid_ref[1]
    for ref in pads:
        clear_rim(ref, WINDOW * WD)
    backward_step(
        0, 0, state, grads, plain_ref, turned_ref, pads, WINDOW * WD, None, None
    )
    part = rows(HALF * lax.axis_index("row"), OWN)
    for ref, index in ((state, 0), (grads, 1)):
        out_ref[index, :, :C] = ref[0, part]
        out_ref[index, :, C:] = ref[1, part]


def forward_scratch(count):
    return [
        pltpu.VMEM((2, count, C), F32),
        pltpu.VMEM((count + 2 * WD, 3 * C), BF16),
        pltpu.VMEM((count + 2 * WD, 3 * C), BF16),
    ]


def backward_scratch(count):
    padded = pltpu.VMEM((count + 2 * WD, 3 * C), BF16)
    return [
        pltpu.VMEM((2, count, C), F32),
        pltpu.VMEM((2, count, C), F32),
        pltpu.VMEM((4, PACK, C), F32),
        padded,
        padded,
        padded,
        padded,
        pltpu.VMEM((count + 2 * WD, C), F32),
    ]


def kernel_grad(parts, high_ref, low_ref, turned_ref):
    for index, part in enumerate(parts):
        at = slice(index * OWN * WD, (index + 1) * OWN * WD)
        for tap, moved in enumerate(shifted(part[0 : VIEW * WD])):
            high, low = hi_lo(moved)
            for drop in range(3):
                lanes = slice((3 * drop + tap) * C, (3 * drop + tap + 1) * C)
                high_ref[at, lanes] = high[drop * WD : (drop + OWN) * WD]
                low_ref[at, lanes] = low[drop * WD : (drop + OWN) * WD]
        high, low = hi_lo(part[VIEW * WD :].T)
        turned_ref[0:C, at] = high
        turned_ref[C:, at] = low
    both = jnp.dot(turned_ref[...], high_ref[...], preferred_element_type=F32)
    rest = jnp.dot(turned_ref[0:C], low_ref[...], preferred_element_type=F32)
    return both[:C] + (both[C:] + rest)


def early_grad_body(*refs):
    parts, out_ref, scratch = refs[:4], refs[4], refs[5:]
    out_ref[...] = kernel_grad(parts, *scratch)


def late_grad_body(scale, share, *refs):
    parts, early_ref, (keep_ref, up_ref, down_ref), scratch = refs[:4], refs[4], refs[5:8], refs[8:11]
    total_ref, held = refs[11:]
    total = (kernel_grad(parts, *scratch) + early_ref[...]) * scale
    for tap in range(TAPS):
        total_ref[tap * C : (tap + 1) * C, :] = total[:, tap * C : (tap + 1) * C].T
    for along in range(8):
        for place in range(4):
            start = share * (16 * (place // 2) + 2 * along + place % 2)
            held[along, place * share : (place + 1) * share] = total_ref[start : start + share]
    odd = (lax.axis_index("dp") // 2) % 2
    for pair in range(4):
        keep_ref[pair] = held[2 * pair + odd]
        up_ref[pair] = held[2 * pair + 1 - odd, 0 : 2 * share]
        down_ref[pair] = held[2 * pair + 1 - odd, 2 * share :]


def grad_scratch():
    count = 4 * OWN * WD
    return [
        pltpu.VMEM((count, DEPTH), BF16),
        pltpu.VMEM((count, DEPTH), BF16),
        pltpu.VMEM((2 * C, count), BF16),
    ]


def fold_pair_body(share, keep_ref, up_ref, down_ref, *outs):
    here = lax.axis_index("dp") // 4
    for by, ref in enumerate(outs):
        pair = (here + by) % 4
        ref[0 : 2 * share] = keep_ref[pair, 0 : 2 * share] + up_ref[pair]
        ref[2 * share :] = keep_ref[pair, 2 * share :] + down_ref[pair]


def fold_body(share, *refs):
    parts, out_ref = refs[:4], refs[4]
    total = (parts[0][...] + parts[1][...]) + (parts[2][...] + parts[3][...])
    for place in range(4):
        out_ref[place] = total[place * share : (place + 1) * share]


def settle_body(in_ref, out_ref):
    for slot in range(4):
        out_ref[slot // 2, :, slot % 2, :] = in_ref[slot]


def per_device(fresh, target, carried, returning, weights, section_blocks):
    tick_count = fresh.shape[0]
    cells = (
        tick_count
        * fresh.shape[1]
        * lax.axis_size("dp")
        * fresh.shape[2]
        * lax.axis_size("row")
        * fresh.shape[3]
    )
    segments = lax.axis_size("segment")
    dp_count = lax.axis_size("dp")
    rungs = dp_count // 2
    share = DEPTH // (2 * dp_count)
    flat = OWN * WD
    fresh = fresh.reshape(2, flat, 2 * C)
    target = target.reshape(flat, 2 * C)
    carried = carried.reshape(flat, 2 * C)
    returning = returning.reshape(2, flat, 2 * C)
    weights = weights.reshape(4, DEPTH, C)
    swap = [(0, 1), (1, 0)]
    onward = [(i, i + 1) for i in range(segments - 1)]
    homeward = [(i + 1, i) for i in range(segments - 1)]

    def across(by):
        pairs = []
        for row in range(2):
            for rung in range(rungs):
                for low in range(2):
                    there = (2 * row + low + by) % 4
                    pairs.append(
                        (
                            row * dp_count + 2 * rung + low,
                            (there // 2) * dp_count + 2 * rung + there % 2,
                        )
                    )
        return pairs

    def deal(parts):
        dealt = [parts[0]]
        for by in range(1, 4):
            dealt.append(lax.ppermute(parts[by], ("row", "dp"), across(by)))
        return dealt

    conv_flops = 6 * DEPTH * C
    other_pair = lax.ppermute(returning, "row", swap)
    (packed,) = call(
        pack_body,
        [(2 * flat, 2 * C)],
        [pltpu.SemaphoreType.DMA((3,))],
        tuple(in_hbm(value) for value in (fresh, carried, target)),
        8,
        1 << 20,
        space=pltpu.HBM,
    )
    other_pack = lax.ppermute(packed, "row", swap)
    plain, turned = prepare(weights)

    sent, *dealt = call(
        backward_full_body,
        [(2, WINDOW * WD, 2 * C)] + [(PACK, C)] * 4,
        backward_scratch(FULL * WD),
        (section_blocks, returning, other_pair, plain, turned),
        24,
        8 * conv_flops * FULL * WD,
        smem=(0,),
    )
    came_back = lax.ppermute(sent, "segment", homeward)
    early = deal(dealt)
    mid, *dealt = call(
        backward_window_body,
        [(2, 2, WINDOW * WD, C)] + [(PACK, C)] * 4,
        backward_scratch(WINDOW * WD) + forward_scratch(FULL * WD),
        (section_blocks, came_back, packed, target, other_pack, plain, turned),
        24,
        8 * conv_flops * WINDOW * WD,
        smem=(0,),
    )
    late = deal(dealt)
    (made,) = call(
        forward_full_body,
        [(WINDOW * WD, 2 * C)],
        forward_scratch(FULL * WD),
        (section_blocks, packed, other_pack, plain),
        24,
        4 * conv_flops * FULL * WD,
        smem=(0,),
    )
    came_on = lax.ppermute(made, "segment", onward)
    (early_grad,) = call(
        early_grad_body, [(C, DEPTH)], grad_scratch(), tuple(early), 24, 4 * conv_flops * flat
    )
    keep, up, down = call(
        functools.partial(late_grad_body, 1.0 / math.sqrt(cells), share),
        [(4, 4 * share, C), (4, 2 * share, C), (4, 2 * share, C)],
        grad_scratch()
        + [pltpu.VMEM((DEPTH, C), F32), pltpu.VMEM((rungs, 4 * share, C), F32)],
        tuple(late) + (early_grad,),
        24,
        4 * conv_flops * flat,
    )

    def climb(goal):
        return [
            (2 * rung + low, 2 * (goal(rung) % rungs) + low)
            for rung in range(rungs)
            for low in range(2)
        ]

    up = lax.ppermute(up, "dp", climb(lambda rung: rung + 1 - 2 * (rung % 2)))
    down = lax.ppermute(down, "dp", climb(lambda rung: rung - 1 + 2 * (rung % 2)))
    (back,) = call(
        backward_tail_body,
        [(2, flat, 2 * C)],
        backward_scratch(WINDOW * WD)[:2] + backward_scratch(WINDOW * WD)[3:7],
        (mid, plain, turned),
        24,
        2 * conv_flops * WINDOW * WD,
    )
    paired = call(
        functools.partial(fold_pair_body, share),
        [(4 * share, C)] * 4,
        [],
        (keep, up, down),
        8,
        1 << 20,
    )
    spread = [paired[0]]
    for by in (2, 1, 3):
        spread.append(
            lax.ppermute(paired[by], "dp", climb(lambda rung, by=by: rung + 2 * by))
        )
    (produced,) = call(
        forward_window_body,
        [(flat, 2 * C)],
        forward_scratch(WINDOW * WD),
        (section_blocks, came_on, fresh, other_pack, plain),
        24,
        4 * conv_flops * WINDOW * WD,
        smem=(0,),
    )
    (folded,) = call(
        functools.partial(fold_body, share),
        [(4, share, C)],
        [],
        tuple(spread),
        8,
        1 << 20,
    )
    quads = [
        [row * dp_count + 2 * rung + low for row in range(2) for low in range(2)]
        for rung in range(rungs)
    ]
    settled = lax.all_to_all(
        folded, ("row", "dp"), 0, 0, axis_index_groups=quads, tiled=True
    )
    (grad_weights,) = call(settle_body, [(2, share, 2, C)], [], (settled,), 8, 1 << 20)
    return (
        grad_weights.transpose(0, 2, 1, 3)[None],
        produced.reshape(1, 1, OWN, WD, 2 * C),
        back.reshape(1, 2, 1, OWN, WD, 2 * C),
    )


def solution(mesh):
    return jax.shard_map(
        per_device,
        mesh=mesh,
        in_specs=(
            P(None, "dp", "row", None, None),
            P(None, "dp", "row", None, None),
            P("segment", "dp", "row", None, None),
            P("segment", None, "dp", "row", None, None),
            P("segment", None, None, None, None),
            P("segment"),
        ),
        out_specs=(
            P("segment", None, None, ("row", "dp"), None),
            P("segment", "dp", "row", None, None),
            P("segment", None, "dp", "row", None, None),
        ),
        check_vma=False,
    )
```

```python
import functools
import math

import jax
import jax.numpy as jnp
from jax import lax
from jax.experimental import pallas as pl
from jax.experimental.pallas import tpu as pltpu
from jax.sharding import PartitionSpec as P


F32 = jnp.float32
BF16 = jnp.bfloat16
C = 128
TAPS = 9
DEPTH = TAPS * C
WD = 16
OWN = 8
HALF = 4
FULL = 16
WINDOW = 12
VIEW = OWN + 2
PACK = (VIEW + OWN) * WD
MEGA = 1 << 20


def params(mib):
    return pltpu.CompilerParams(vmem_limit_bytes=mib * MEGA)


def cost(flops, nbytes):
    return pl.CostEstimate(flops=flops, bytes_accessed=nbytes, transcendentals=0)


def whole(memory_space=pltpu.VMEM):
    return pl.BlockSpec(memory_space=memory_space)


def call(body, out_shape, scratch, args, mib, flops, smem=(), space=pltpu.VMEM):
    in_specs = [whole(pltpu.SMEM if i in smem else space) for i in range(len(args))]
    outs = [jax.ShapeDtypeStruct(shape, F32) for shape in out_shape]
    nbytes = sum(4 * math.prod(shape) for shape in out_shape)
    return pl.pallas_call(
        body,
        out_shape=outs,
        in_specs=in_specs,
        out_specs=[whole() for _ in outs],
        scratch_shapes=scratch,
        compiler_params=params(mib),
        cost_estimate=cost(flops, nbytes),
    )(*args)


def in_hbm(value):
    return pltpu.with_memory_space_constraint(value, pltpu.HBM)


def rows(start, count):
    return pl.ds(pl.multiple_of(start * WD, HALF * WD), count * WD)


def hi_lo(value):
    high = value.astype(BF16)
    return high, (value - high.astype(F32)).astype(BF16)


def shifted(value):
    count = value.shape[0]
    column = lax.broadcasted_iota(jnp.int32, value.shape, 0) % WD
    left = jnp.where(column == 0, 0.0, pltpu.roll(value, 1, 0))
    right = jnp.where(column == WD - 1, 0.0, pltpu.roll(value, count - 1, 0))
    return left, value, right


def fill_patches(value, high_ref, low_ref):
    count = value.shape[0]
    for tap, moved in enumerate(shifted(value)):
        high, low = hi_lo(moved)
        high_ref[WD : WD + count, tap * C : (tap + 1) * C] = high
        low_ref[WD : WD + count, tap * C : (tap + 1) * C] = low


def clear_rim(ref, count):
    rim = jnp.zeros((WD,) + tuple(ref.shape[1:]), ref.dtype)
    ref[0:WD] = rim
    ref[WD + count : 2 * WD + count] = rim


def gathered(ref, count):
    return jnp.concatenate([ref[d * WD : d * WD + count, :] for d in range(3)], axis=1)


def conv(high_ref, low_ref, kernel_ref, slot, count):
    both = jnp.dot(gathered(high_ref, count), kernel_ref[slot], preferred_element_type=F32)
    rest = jnp.dot(
        gathered(low_ref, count), kernel_ref[slot, :, 0:C], preferred_element_type=F32
    )
    return both[:, :C] + (both[:, C:] + rest)


def logistic(value):
    return 1.0 / (1.0 + jnp.exp(-value))


def prepare_body(weight_ref, plain_ref, turned_ref, held, sems):
    slots = weight_ref.shape[0]
    for slot in range(slots):
        pltpu.make_async_copy(weight_ref.at[slot], held.at[slot], sems.at[slot]).start()

    def step(slot, carry):
        pltpu.make_async_copy(weight_ref.at[slot], held.at[slot], sems.at[slot]).wait()
        for tap in range(TAPS):
            block = held[slot, tap * C : (tap + 1) * C, :]
            high, low = hi_lo(block)
            plain_ref[slot, tap * C : (tap + 1) * C, 0:C] = high
            plain_ref[slot, tap * C : (tap + 1) * C, C:] = low
            high, low = hi_lo(block.T)
            back = TAPS - 1 - tap
            turned_ref[slot, back * C : (back + 1) * C, 0:C] = high
            turned_ref[slot, back * C : (back + 1) * C, C:] = low
        return carry

    lax.fori_loop(0, slots, step, 0)


def prepare(weights):
    slots = weights.shape[0]
    shape = jax.ShapeDtypeStruct((slots, DEPTH, 2 * C), BF16)
    return pl.pallas_call(
        prepare_body,
        out_shape=[shape, shape],
        in_specs=[whole(pltpu.HBM)],
        out_specs=[whole(), whole()],
        scratch_shapes=[
            pltpu.VMEM((slots, DEPTH, C), F32),
            pltpu.SemaphoreType.DMA((slots,)),
        ],
        compiler_params=params(16),
        cost_estimate=cost(slots * DEPTH * C * 8, slots * DEPTH * C * 12),
    )(in_hbm(weights))


def pack_body(fresh_ref, carried_ref, target_ref, out_ref, sems):
    first = lax.axis_index("segment") == 0
    start = HALF * (1 - lax.axis_index("row"))
    top = out_ref.at[0 : OWN * WD]
    from_fresh = pltpu.make_async_copy(fresh_ref.at[0], top, sems.at[0])
    from_carried = pltpu.make_async_copy(carried_ref, top, sems.at[0])
    others = (
        pltpu.make_async_copy(
            target_ref.at[rows(start, HALF)], out_ref.at[OWN * WD : WINDOW * WD], sems.at[1]
        ),
        pltpu.make_async_copy(
            fresh_ref.at[1, rows(start, HALF)], out_ref.at[WINDOW * WD :], sems.at[2]
        ),
    )

    @pl.when(first)
    def _():
        from_fresh.start()

    @pl.when(jnp.logical_not(first))
    def _():
        from_carried.start()

    for copy in others:
        copy.start()

    @pl.when(first)
    def _():
        from_fresh.wait()

    @pl.when(jnp.logical_not(first))
    def _():
        from_carried.wait()

    for copy in others:
        copy.wait()


def put_halves(ref, where, value):
    ref[0, where] = value[:, :C]
    ref[1, where] = value[:, C:]


def forward_loop(state_ref, high_ref, low_ref, kernel_ref, blocks_ref, count):
    clear_rim(high_ref, count)
    clear_rim(low_ref, count)

    def step(slot, carry):
        half = slot % 2
        source = state_ref[1 - half]
        fill_patches(source * logistic(source), high_ref, low_ref)
        state_ref[half] = state_ref[half] + conv(high_ref, low_ref, kernel_ref, slot, count)
        return carry

    lax.fori_loop(0, 2 * blocks_ref[0], step, 0)


def forward_crop(blocks_ref, own_ref, other_ref, kernel_ref, state, high, low):
    row = lax.axis_index("row")
    put_halves(state, rows(OWN * row, OWN), own_ref[0 : OWN * WD])
    put_halves(state, rows(OWN * (1 - row), OWN), other_ref[0 : OWN * WD])
    forward_loop(state, high, low, kernel_ref, blocks_ref, FULL * WD)
    return rows(HALF * row, WINDOW)


def is_final():
    return lax.axis_index("segment") == lax.axis_size("segment") - 1


def forward_full_body(blocks_ref, own_ref, other_ref, kernel_ref, out_ref, state, high, low):
    @pl.when(jnp.logical_not(is_final()))
    def _():
        part = forward_crop(blocks_ref, own_ref, other_ref, kernel_ref, state, high, low)
        out_ref[:, :C] = state[0, part]
        out_ref[:, C:] = state[1, part]


def forward_window_body(
    blocks_ref, came_ref, fresh_ref, other_ref, kernel_ref, out_ref, state, high, low
):
    row = lax.axis_index("row")
    first = lax.axis_index("segment") == 0

    @pl.when(first)
    def _():
        put_halves(state, rows(HALF * row, OWN), fresh_ref[1])
        put_halves(state, rows(OWN * (1 - row), HALF), other_ref[WINDOW * WD :])

    @pl.when(jnp.logical_not(first))
    def _():
        put_halves(state, pl.ds(0, WINDOW * WD), came_ref[...])

    forward_loop(state, high, low, kernel_ref, blocks_ref, WINDOW * WD)
    part = rows(HALF * row, OWN)
    out_ref[:, :C] = state[0, part]
    out_ref[:, C:] = state[1, part]


def clear_picked(picked, blocks_ref):
    @pl.when(blocks_ref[0] < 2)
    def _():
        picked[2] = jnp.zeros((PACK, C), F32)
        picked[3] = jnp.zeros((PACK, C), F32)


def pick(picked, slot, source_pad, grads, half, own):
    picked[slot, 0 : VIEW * WD] = source_pad[rows(own, VIEW)]
    picked[slot, VIEW * WD :] = grads[half, rows(own, OWN)]


def backward_step(slot, half, state, grads, plain_ref, turned_ref, pads, count, picked, own):
    source_high, source_low, grad_high, grad_low = pads[:4]
    source = state[1 - half]
    grad = grads[half]
    gate = logistic(source)
    field = source * gate
    fill_patches(field, source_high, source_low)
    fill_patches(grad, grad_high, grad_low)
    if picked is not None:
        pads[4][WD : WD + count] = field
        pick(picked, slot, pads[4], grads, half, own)
    state[half] = state[half] - conv(source_high, source_low, plain_ref, slot, count)
    slope = gate * (1.0 + source * (1.0 - gate))
    grads[1 - half] = grads[1 - half] + slope * conv(
        grad_high, grad_low, turned_ref, slot, count
    )


def backward_loop(
    state, grads, plain_ref, turned_ref, blocks_ref, pads, picked, own, count, lowest
):
    for ref in pads:
        clear_rim(ref, count)
    clear_picked(picked, blocks_ref)
    top = 2 * blocks_ref[0] - 1

    def step(turn, carry):
        slot = top - turn
        backward_step(
            slot, slot % 2, state, grads, plain_ref, turned_ref, pads, count, picked, own
        )
        return carry

    lax.fori_loop(0, top + 1 - lowest, step, 0)


def crossing(row):
    return 2 * row + lax.axis_index("dp") % 2


def hand_out(picked, refs):
    place = crossing(lax.axis_index("row"))
    for by, ref in enumerate(refs):
        ref[...] = picked[(place + by) % 4]


def backward_full_body(
    blocks_ref, own_ref, other_ref, plain_ref, turned_ref, out_ref, *rest
):
    outs, (state, grads, picked), pads = rest[:4], rest[4:7], rest[7:]
    row = lax.axis_index("row")
    for ref, index in ((state, 0), (grads, 1)):
        put_halves(ref, rows(OWN * row, OWN), own_ref[index])
        put_halves(ref, rows(OWN * (1 - row), OWN), other_ref[index])
    backward_loop(
        state, grads, plain_ref, turned_ref, blocks_ref, pads, picked, OWN * row, FULL * WD, 0
    )
    part = rows(HALF * row, WINDOW)
    for ref, index in ((state, 0), (grads, 1)):
        out_ref[index, :, :C] = ref[0, part]
        out_ref[index, :, C:] = ref[1, part]
    hand_out(picked, outs)


def backward_window_body(
    blocks_ref,
    came_ref,
    own_ref,
    target_ref,
    other_ref,
    plain_ref,
    turned_ref,
    mid_ref,
    *rest,
):
    outs, (state, grads, picked), pads = rest[:4], rest[4:7], rest[7:12]
    crop_state, crop_high, crop_low = rest[12:]
    row = lax.axis_index("row")
    final = is_final()

    @pl.when(final)
    def _():
        part = forward_crop(
            blocks_ref, own_ref, other_ref, plain_ref, crop_state, crop_high, crop_low
        )
        put_halves(grads, rows(HALF * row, OWN), target_ref[...])
        put_halves(grads, rows(OWN * (1 - row), HALF), other_ref[OWN * WD : WINDOW * WD])
        for half in range(2):
            made = crop_state[half, part]
            state[half] = made
            grads[half] = made - grads[half]

    @pl.when(jnp.logical_not(final))
    def _():
        put_halves(state, pl.ds(0, WINDOW * WD), came_ref[0])
        put_halves(grads, pl.ds(0, WINDOW * WD), came_ref[1])

    count = WINDOW * WD
    own = HALF * row
    backward_loop(
        state, grads, plain_ref, turned_ref, blocks_ref, pads, picked, own, count, 1
    )
    source = state[1]
    pads[4][WD : WD + count] = source * logistic(source)
    pick(picked, 0, pads[4], grads, 0, own)
    hand_out(picked, outs)
    mid_ref[0] = state[...]
    mid_ref[1] = grads[...]


def backward_tail_body(mid_ref, plain_ref, turned_ref, out_ref, state, grads, *pads):
    state[...] = mid_ref[0]
    grads[...] = mid_ref[1]
    for ref in pads:
        clear_rim(ref, WINDOW * WD)
    backward_step(
        0, 0, state, grads, plain_ref, turned_ref, pads, WINDOW * WD, None, None
    )
    part = rows(HALF * lax.axis_index("row"), OWN)
    for ref, index in ((state, 0), (grads, 1)):
        out_ref[index, :, :C] = ref[0, part]
        out_ref[index, :, C:] = ref[1, part]


def forward_scratch(count):
    return [
        pltpu.VMEM((2, count, C), F32),
        pltpu.VMEM((count + 2 * WD, 3 * C), BF16),
        pltpu.VMEM((count + 2 * WD, 3 * C), BF16),
    ]


def backward_scratch(count):
    padded = pltpu.VMEM((count + 2 * WD, 3 * C), BF16)
    return [
        pltpu.VMEM((2, count, C), F32),
        pltpu.VMEM((2, count, C), F32),
        pltpu.VMEM((4, PACK, C), F32),
        padded,
        padded,
        padded,
        padded,
        pltpu.VMEM((count + 2 * WD, C), F32),
    ]


def kernel_grad(parts, high_ref, low_ref, turned_ref):
    for index, part in enumerate(parts):
        at = slice(index * OWN * WD, (index + 1) * OWN * WD)
        for tap, moved in enumerate(shifted(part[0 : VIEW * WD])):
            high, low = hi_lo(moved)
            for drop in range(3):
                lanes = slice((3 * drop + tap) * C, (3 * drop + tap + 1) * C)
                high_ref[at, lanes] = high[drop * WD : (drop + OWN) * WD]
                low_ref[at, lanes] = low[drop * WD : (drop + OWN) * WD]
        high, low = hi_lo(part[VIEW * WD :].T)
        turned_ref[0:C, at] = high
        turned_ref[C:, at] = low
    both = jnp.dot(turned_ref[...], high_ref[...], preferred_element_type=F32)
    rest = jnp.dot(turned_ref[0:C], low_ref[...], preferred_element_type=F32)
    return both[:C] + (both[C:] + rest)


def early_grad_body(*refs):
    parts, out_ref, scratch = refs[:4], refs[4], refs[5:]
    out_ref[...] = kernel_grad(parts, *scratch)


def late_grad_body(scale, share, *refs):
    parts, early_ref, (keep_ref, up_ref, down_ref), scratch = refs[:4], refs[4], refs[5:8], refs[8:11]
    total_ref, held = refs[11:]
    total = (kernel_grad(parts, *scratch) + early_ref[...]) * scale
    for tap in range(TAPS):
        total_ref[tap * C : (tap + 1) * C, :] = total[:, tap * C : (tap + 1) * C].T
    for along in range(8):
        for place in range(4):
            start = share * (16 * (place // 2) + 2 * along + place % 2)
            held[along, place * share : (place + 1) * share] = total_ref[start : start + share]
    odd = (lax.axis_index("dp") // 2) % 2
    for pair in range(4):
        keep_ref[pair] = held[2 * pair + odd]
        up_ref[pair] = held[2 * pair + 1 - odd, 0 : 2 * share]
        down_ref[pair] = held[2 * pair + 1 - odd, 2 * share :]


def grad_scratch():
    count = 4 * OWN * WD
    return [
        pltpu.VMEM((count, DEPTH), BF16),
        pltpu.VMEM((count, DEPTH), BF16),
        pltpu.VMEM((2 * C, count), BF16),
    ]


def fold_pair_body(share, keep_ref, up_ref, down_ref, out_ref):
    for pair in range(4):
        for row, came_ref in enumerate((up_ref, down_ref)):
            at = slice(2 * row * share, 2 * (row + 1) * share)
            total = keep_ref[pair, at] + came_ref[pair]
            for low in range(2):
                out_ref[8 * row + 2 * pair + low] = total[low * share : (low + 1) * share]


def settle_body(in_ref, out_ref):
    for slot in range(4):
        first = 8 * (slot // 2) + slot % 2
        total = (in_ref[first] + in_ref[first + 2]) + (in_ref[first + 4] + in_ref[first + 6])
        out_ref[slot // 2, :, slot % 2, :] = total


def per_device(fresh, target, carried, returning, weights, section_blocks):
    tick_count = fresh.shape[0]
    cells = (
        tick_count
        * fresh.shape[1]
        * lax.axis_size("dp")
        * fresh.shape[2]
        * lax.axis_size("row")
        * fresh.shape[3]
    )
    segments = lax.axis_size("segment")
    dp_count = lax.axis_size("dp")
    rungs = dp_count // 2
    share = DEPTH // (2 * dp_count)
    flat = OWN * WD
    fresh = fresh.reshape(2, flat, 2 * C)
    target = target.reshape(flat, 2 * C)
    carried = carried.reshape(flat, 2 * C)
    returning = returning.reshape(2, flat, 2 * C)
    weights = weights.reshape(4, DEPTH, C)
    swap = [(0, 1), (1, 0)]
    onward = [(i, i + 1) for i in range(segments - 1)]
    homeward = [(i + 1, i) for i in range(segments - 1)]

    def across(by):
        pairs = []
        for row in range(2):
            for rung in range(rungs):
                for low in range(2):
                    there = (2 * row + low + by) % 4
                    pairs.append(
                        (
                            row * dp_count + 2 * rung + low,
                            (there // 2) * dp_count + 2 * rung + there % 2,
                        )
                    )
        return pairs

    def deal(parts):
        dealt = [parts[0]]
        for by in range(1, 4):
            dealt.append(lax.ppermute(parts[by], ("row", "dp"), across(by)))
        return dealt

    conv_flops = 6 * DEPTH * C
    other_pair = lax.ppermute(returning, "row", swap)
    (packed,) = call(
        pack_body,
        [(2 * flat, 2 * C)],
        [pltpu.SemaphoreType.DMA((3,))],
        tuple(in_hbm(value) for value in (fresh, carried, target)),
        8,
        1 << 20,
        space=pltpu.HBM,
    )
    other_pack = lax.ppermute(packed, "row", swap)
    plain, turned = prepare(weights)

    sent, *dealt = call(
        backward_full_body,
        [(2, WINDOW * WD, 2 * C)] + [(PACK, C)] * 4,
        backward_scratch(FULL * WD),
        (section_blocks, returning, other_pair, plain, turned),
        24,
        8 * conv_flops * FULL * WD,
        smem=(0,),
    )
    came_back = lax.ppermute(sent, "segment", homeward)
    early = deal(dealt)
    mid, *dealt = call(
        backward_window_body,
        [(2, 2, WINDOW * WD, C)] + [(PACK, C)] * 4,
        backward_scratch(WINDOW * WD) + forward_scratch(FULL * WD),
        (section_blocks, came_back, packed, target, other_pack, plain, turned),
        24,
        8 * conv_flops * WINDOW * WD,
        smem=(0,),
    )
    late = deal(dealt)
    (made,) = call(
        forward_full_body,
        [(WINDOW * WD, 2 * C)],
        forward_scratch(FULL * WD),
        (section_blocks, packed, other_pack, plain),
        24,
        4 * conv_flops * FULL * WD,
        smem=(0,),
    )
    (early_grad,) = call(
        early_grad_body, [(C, DEPTH)], grad_scratch(), tuple(early), 24, 4 * conv_flops * flat
    )
    keep, up, down = call(
        functools.partial(late_grad_body, 1.0 / math.sqrt(cells), share),
        [(4, 4 * share, C), (4, 2 * share, C), (4, 2 * share, C)],
        grad_scratch()
        + [pltpu.VMEM((DEPTH, C), F32), pltpu.VMEM((rungs, 4 * share, C), F32)],
        tuple(late) + (early_grad,),
        24,
        4 * conv_flops * flat,
    )

    def climb(goal):
        return [
            (2 * rung + low, 2 * (goal(rung) % rungs) + low)
            for rung in range(rungs)
            for low in range(2)
        ]

    up = lax.ppermute(up, "dp", climb(lambda rung: rung + 1 - 2 * (rung % 2)))
    down = lax.ppermute(down, "dp", climb(lambda rung: rung - 1 + 2 * (rung % 2)))
    came_on = lax.ppermute(made, "segment", onward)
    (back,) = call(
        backward_tail_body,
        [(2, flat, 2 * C)],
        backward_scratch(WINDOW * WD)[:2] + backward_scratch(WINDOW * WD)[3:7],
        (mid, plain, turned),
        24,
        2 * conv_flops * WINDOW * WD,
    )
    (produced,) = call(
        forward_window_body,
        [(flat, 2 * C)],
        forward_scratch(WINDOW * WD),
        (section_blocks, came_on, fresh, other_pack, plain),
        24,
        4 * conv_flops * WINDOW * WD,
        smem=(0,),
    )
    (paired,) = call(
        functools.partial(fold_pair_body, share),
        [(16, share, C)],
        [],
        (keep, up, down),
        8,
        1 << 20,
    )
    peers = [
        [
            row * dp_count + 2 * rung + low
            for row in range(2)
            for rung in range(odd, rungs, 2)
            for low in range(2)
        ]
        for odd in range(2)
    ]
    settled = lax.all_to_all(
        paired, ("row", "dp"), 0, 0, axis_index_groups=peers, tiled=True
    )
    (grad_weights,) = call(settle_body, [(2, share, 2, C)], [], (settled,), 8, 1 << 20)
    return (
        grad_weights.transpose(0, 2, 1, 3)[None],
        produced.reshape(1, 1, OWN, WD, 2 * C),
        back.reshape(1, 2, 1, OWN, WD, 2 * C),
    )


def solution(mesh):
    return jax.shard_map(
        per_device,
        mesh=mesh,
        in_specs=(
            P(None, "dp", "row", None, None),
            P(None, "dp", "row", None, None),
            P("segment", "dp", "row", None, None),
            P("segment", None, "dp", "row", None, None),
            P("segment", None, None, None, None),
            P("segment"),
        ),
        out_specs=(
            P("segment", None, None, ("row", "dp"), None),
            P("segment", "dp", "row", None, None),
            P("segment", None, "dp", "row", None, None),
        ),
        check_vma=False,
    )
```

```python
import functools
import math

import jax
import jax.numpy as jnp
from jax import lax
from jax.experimental import pallas as pl
from jax.experimental.pallas import tpu as pltpu
from jax.sharding import PartitionSpec as P


F32 = jnp.float32
BF16 = jnp.bfloat16
C = 128
TAPS = 9
DEPTH = TAPS * C
WD = 16
OWN = 8
HALF = 4
FULL = 16
WINDOW = 12
PART = OWN * WD
PACK = 2 * PART
CROP = FULL * WD
MEGA = 1 << 20


def params(mib):
    return pltpu.CompilerParams(vmem_limit_bytes=mib * MEGA)


def cost(flops, nbytes):
    return pl.CostEstimate(flops=flops, bytes_accessed=nbytes, transcendentals=0)


def whole(memory_space=pltpu.VMEM):
    return pl.BlockSpec(memory_space=memory_space)


def call(body, out_shape, scratch, args, mib, flops, smem=(), space=pltpu.VMEM):
    in_specs = [whole(pltpu.SMEM if i in smem else space) for i in range(len(args))]
    outs = [jax.ShapeDtypeStruct(shape, F32) for shape in out_shape]
    nbytes = sum(4 * math.prod(shape) for shape in out_shape)
    return pl.pallas_call(
        body,
        out_shape=outs,
        in_specs=in_specs,
        out_specs=[whole() for _ in outs],
        scratch_shapes=scratch,
        compiler_params=params(mib),
        cost_estimate=cost(flops, nbytes),
    )(*args)


def in_hbm(value):
    return pltpu.with_memory_space_constraint(value, pltpu.HBM)


def rows(start, count):
    return pl.ds(pl.multiple_of(start * WD, HALF * WD), count * WD)


def hi_lo(value):
    high = value.astype(BF16)
    return high, (value - high.astype(F32)).astype(BF16)


def shifted(value):
    count = value.shape[0]
    column = lax.broadcasted_iota(jnp.int32, value.shape, 0) % WD
    left = jnp.where(column == 0, 0.0, pltpu.roll(value, 1, 0))
    right = jnp.where(column == WD - 1, 0.0, pltpu.roll(value, count - 1, 0))
    return left, value, right


def fill_patches(value, high_ref, low_ref):
    count = value.shape[0]
    for tap, moved in enumerate(shifted(value)):
        high, low = hi_lo(moved)
        high_ref[WD : WD + count, tap * C : (tap + 1) * C] = high
        low_ref[WD : WD + count, tap * C : (tap + 1) * C] = low


def clear_rim(ref, count):
    rim = jnp.zeros((WD,) + tuple(ref.shape[1:]), ref.dtype)
    ref[0:WD] = rim
    ref[WD + count : 2 * WD + count] = rim


def gathered(ref, count):
    return jnp.concatenate([ref[d * WD : d * WD + count, :] for d in range(3)], axis=1)


def conv(high_ref, low_ref, kernel_ref, slot, count):
    both = jnp.dot(gathered(high_ref, count), kernel_ref[slot], preferred_element_type=F32)
    rest = jnp.dot(
        gathered(low_ref, count), kernel_ref[slot, :, 0:C], preferred_element_type=F32
    )
    return both[:, :C] + (both[:, C:] + rest)


def logistic(value):
    return 1.0 / (1.0 + jnp.exp(-value))


def prepare_body(weight_ref, plain_ref, turned_ref, held, sems):
    slots = weight_ref.shape[0]
    for slot in range(slots):
        pltpu.make_async_copy(weight_ref.at[slot], held.at[slot], sems.at[slot]).start()

    def step(slot, carry):
        pltpu.make_async_copy(weight_ref.at[slot], held.at[slot], sems.at[slot]).wait()
        for tap in range(TAPS):
            block = held[slot, tap * C : (tap + 1) * C, :]
            high, low = hi_lo(block)
            plain_ref[slot, tap * C : (tap + 1) * C, 0:C] = high
            plain_ref[slot, tap * C : (tap + 1) * C, C:] = low
            high, low = hi_lo(block.T)
            back = TAPS - 1 - tap
            turned_ref[slot, back * C : (back + 1) * C, 0:C] = high
            turned_ref[slot, back * C : (back + 1) * C, C:] = low
        return carry

    lax.fori_loop(0, slots, step, 0)


def prepare(weights):
    slots = weights.shape[0]
    shape = jax.ShapeDtypeStruct((slots, DEPTH, 2 * C), BF16)
    return pl.pallas_call(
        prepare_body,
        out_shape=[shape, shape],
        in_specs=[whole(pltpu.HBM)],
        out_specs=[whole(), whole()],
        scratch_shapes=[
            pltpu.VMEM((slots, DEPTH, C), F32),
            pltpu.SemaphoreType.DMA((slots,)),
        ],
        compiler_params=params(16),
        cost_estimate=cost(slots * DEPTH * C * 8, slots * DEPTH * C * 12),
    )(in_hbm(weights))


def pack_body(fresh_ref, carried_ref, target_ref, out_ref, sems):
    first = lax.axis_index("segment") == 0
    start = HALF * (1 - lax.axis_index("row"))
    top = out_ref.at[0 : OWN * WD]
    from_fresh = pltpu.make_async_copy(fresh_ref.at[0], top, sems.at[0])
    from_carried = pltpu.make_async_copy(carried_ref, top, sems.at[0])
    others = (
        pltpu.make_async_copy(
            target_ref.at[rows(start, HALF)], out_ref.at[OWN * WD : WINDOW * WD], sems.at[1]
        ),
        pltpu.make_async_copy(
            fresh_ref.at[1, rows(start, HALF)], out_ref.at[WINDOW * WD :], sems.at[2]
        ),
    )

    @pl.when(first)
    def _():
        from_fresh.start()

    @pl.when(jnp.logical_not(first))
    def _():
        from_carried.start()

    for copy in others:
        copy.start()

    @pl.when(first)
    def _():
        from_fresh.wait()

    @pl.when(jnp.logical_not(first))
    def _():
        from_carried.wait()

    for copy in others:
        copy.wait()


def put_halves(ref, where, value):
    ref[0, where] = value[:, :C]
    ref[1, where] = value[:, C:]


def forward_loop(state_ref, high_ref, low_ref, kernel_ref, blocks_ref, count):
    clear_rim(high_ref, count)
    clear_rim(low_ref, count)

    def step(slot, carry):
        half = slot % 2
        source = state_ref[1 - half]
        fill_patches(source * logistic(source), high_ref, low_ref)
        state_ref[half] = state_ref[half] + conv(high_ref, low_ref, kernel_ref, slot, count)
        return carry

    lax.fori_loop(0, 2 * blocks_ref[0], step, 0)


def forward_crop(blocks_ref, own_ref, other_ref, kernel_ref, state, high, low):
    row = lax.axis_index("row")
    put_halves(state, rows(OWN * row, OWN), own_ref[0 : OWN * WD])
    put_halves(state, rows(OWN * (1 - row), OWN), other_ref[0 : OWN * WD])
    forward_loop(state, high, low, kernel_ref, blocks_ref, FULL * WD)
    return rows(HALF * row, WINDOW)


def is_final():
    return lax.axis_index("segment") == lax.axis_size("segment") - 1


def forward_full_body(blocks_ref, own_ref, other_ref, kernel_ref, out_ref, state, high, low):
    @pl.when(jnp.logical_not(is_final()))
    def _():
        part = forward_crop(blocks_ref, own_ref, other_ref, kernel_ref, state, high, low)
        out_ref[:, :C] = state[0, part]
        out_ref[:, C:] = state[1, part]


def forward_window_body(
    blocks_ref, came_ref, fresh_ref, other_ref, kernel_ref, out_ref, state, high, low
):
    row = lax.axis_index("row")
    first = lax.axis_index("segment") == 0

    @pl.when(first)
    def _():
        put_halves(state, rows(HALF * row, OWN), fresh_ref[1])
        put_halves(state, rows(OWN * (1 - row), HALF), other_ref[WINDOW * WD :])

    @pl.when(jnp.logical_not(first))
    def _():
        put_halves(state, pl.ds(0, WINDOW * WD), came_ref[...])

    forward_loop(state, high, low, kernel_ref, blocks_ref, WINDOW * WD)
    part = rows(HALF * row, OWN)
    out_ref[:, :C] = state[0, part]
    out_ref[:, C:] = state[1, part]


def clear_picked(picked, blocks_ref):
    @pl.when(blocks_ref[0] < 2)
    def _():
        picked[2] = jnp.zeros((PACK, C), F32)
        picked[3] = jnp.zeros((PACK, C), F32)


def pick(picked, slot, field_ref, grads, half, own):
    picked[slot, 0:PART] = field_ref[rows(own, OWN)]
    picked[slot, PART:] = grads[half, rows(own, OWN)]


def backward_step(slot, half, state, grads, plain_ref, turned_ref, pads, count, picked, own):
    source_high, source_low, grad_high, grad_low = pads[:4]
    source = state[1 - half]
    grad = grads[half]
    gate = logistic(source)
    field = source * gate
    fill_patches(field, source_high, source_low)
    fill_patches(grad, grad_high, grad_low)
    if picked is not None:
        pads[4][...] = field
        pick(picked, slot, pads[4], grads, half, own)
    state[half] = state[half] - conv(source_high, source_low, plain_ref, slot, count)
    slope = gate * (1.0 + source * (1.0 - gate))
    grads[1 - half] = grads[1 - half] + slope * conv(
        grad_high, grad_low, turned_ref, slot, count
    )


def backward_loop(
    state, grads, plain_ref, turned_ref, blocks_ref, pads, picked, own, count, lowest
):
    for ref in pads[:4]:
        clear_rim(ref, count)
    clear_picked(picked, blocks_ref)
    top = 2 * blocks_ref[0] - 1

    def step(turn, carry):
        slot = top - turn
        backward_step(
            slot, slot % 2, state, grads, plain_ref, turned_ref, pads, count, picked, own
        )
        return carry

    lax.fori_loop(0, top + 1 - lowest, step, 0)


def crossing(row):
    return 2 * row + lax.axis_index("dp") % 2


def hand_out(picked, refs):
    place = crossing(lax.axis_index("row"))
    for by, ref in enumerate(refs):
        ref[...] = picked[(place + by) % 4]


def backward_full_body(
    blocks_ref, own_ref, other_ref, plain_ref, turned_ref, out_ref, *rest
):
    outs, (state, grads, picked), pads = rest[:4], rest[4:7], rest[7:]
    row = lax.axis_index("row")
    for ref, index in ((state, 0), (grads, 1)):
        put_halves(ref, rows(OWN * row, OWN), own_ref[index])
        put_halves(ref, rows(OWN * (1 - row), OWN), other_ref[index])
    backward_loop(
        state, grads, plain_ref, turned_ref, blocks_ref, pads, picked, OWN * row, FULL * WD, 0
    )
    part = rows(HALF * row, WINDOW)
    for ref, index in ((state, 0), (grads, 1)):
        out_ref[index, :, :C] = ref[0, part]
        out_ref[index, :, C:] = ref[1, part]
    hand_out(picked, outs)


def backward_window_body(
    blocks_ref,
    came_ref,
    own_ref,
    target_ref,
    other_ref,
    plain_ref,
    turned_ref,
    mid_ref,
    *rest,
):
    outs, (state, grads, picked), pads = rest[:4], rest[4:7], rest[7:12]
    crop_state, crop_high, crop_low = rest[12:]
    row = lax.axis_index("row")
    final = is_final()

    @pl.when(final)
    def _():
        part = forward_crop(
            blocks_ref, own_ref, other_ref, plain_ref, crop_state, crop_high, crop_low
        )
        put_halves(grads, rows(HALF * row, OWN), target_ref[...])
        put_halves(grads, rows(OWN * (1 - row), HALF), other_ref[OWN * WD : WINDOW * WD])
        for half in range(2):
            made = crop_state[half, part]
            state[half] = made
            grads[half] = made - grads[half]

    @pl.when(jnp.logical_not(final))
    def _():
        put_halves(state, pl.ds(0, WINDOW * WD), came_ref[0])
        put_halves(grads, pl.ds(0, WINDOW * WD), came_ref[1])

    count = WINDOW * WD
    own = HALF * row
    backward_loop(
        state, grads, plain_ref, turned_ref, blocks_ref, pads, picked, own, count, 1
    )
    source = state[1]
    pads[4][...] = source * logistic(source)
    pick(picked, 0, pads[4], grads, 0, own)
    hand_out(picked, outs)
    mid_ref[0] = state[...]
    mid_ref[1] = grads[...]


def backward_tail_body(mid_ref, plain_ref, turned_ref, out_ref, state, grads, *pads):
    state[...] = mid_ref[0]
    grads[...] = mid_ref[1]
    for ref in pads:
        clear_rim(ref, WINDOW * WD)
    backward_step(
        0, 0, state, grads, plain_ref, turned_ref, pads, WINDOW * WD, None, None
    )
    part = rows(HALF * lax.axis_index("row"), OWN)
    for ref, index in ((state, 0), (grads, 1)):
        out_ref[index, :, :C] = ref[0, part]
        out_ref[index, :, C:] = ref[1, part]


def forward_scratch(count):
    return [
        pltpu.VMEM((2, count, C), F32),
        pltpu.VMEM((count + 2 * WD, 3 * C), BF16),
        pltpu.VMEM((count + 2 * WD, 3 * C), BF16),
    ]


def backward_scratch(count):
    padded = pltpu.VMEM((count + 2 * WD, 3 * C), BF16)
    return [
        pltpu.VMEM((2, count, C), F32),
        pltpu.VMEM((2, count, C), F32),
        pltpu.VMEM((4, PACK, C), F32),
        padded,
        padded,
        padded,
        padded,
        pltpu.VMEM((count, C), F32),
    ]


def kernel_grad(parts, field_ref, grad_ref, high_ref, low_ref):
    here = crossing(lax.axis_index("row"))
    for by, part in enumerate(parts):
        at = rows(OWN * (((here + 4 - by) % 4) // 2), OWN)
        field_ref[by % 2, at] = part[0:PART]
        grad_ref[by % 2, at] = part[PART:]
    clear_rim(high_ref, CROP)
    clear_rim(low_ref, CROP)
    total = None
    for crop in range(2):
        fill_patches(field_ref[crop], high_ref, low_ref)
        high, low = hi_lo(grad_ref[crop].T)
        both = jnp.dot(
            jnp.concatenate([high, low], axis=0),
            gathered(high_ref, CROP),
            preferred_element_type=F32,
        )
        rest = jnp.dot(high, gathered(low_ref, CROP), preferred_element_type=F32)
        piece = both[:C] + (both[C:] + rest)
        total = piece if total is None else total + piece
    return total


def early_grad_body(*refs):
    parts, out_ref, scratch = refs[:4], refs[4], refs[5:]
    out_ref[...] = kernel_grad(parts, *scratch)


def late_grad_body(scale, share, *refs):
    parts, early_ref, (keep_ref, up_ref, down_ref), scratch = refs[:4], refs[4], refs[5:8], refs[8:12]
    total_ref, held = refs[12:]
    total = (kernel_grad(parts, *scratch) + early_ref[...]) * scale
    for tap in range(TAPS):
        total_ref[tap * C : (tap + 1) * C, :] = total[:, tap * C : (tap + 1) * C].T
    for along in range(8):
        for place in range(4):
            start = share * (16 * (place // 2) + 2 * along + place % 2)
            held[along, place * share : (place + 1) * share] = total_ref[start : start + share]
    odd = (lax.axis_index("dp") // 2) % 2
    for pair in range(4):
        keep_ref[pair] = held[2 * pair + odd]
        up_ref[pair] = held[2 * pair + 1 - odd, 0 : 2 * share]
        down_ref[pair] = held[2 * pair + 1 - odd, 2 * share :]


def grad_scratch():
    return [
        pltpu.VMEM((2, CROP, C), F32),
        pltpu.VMEM((2, CROP, C), F32),
        pltpu.VMEM((CROP + 2 * WD, 3 * C), BF16),
        pltpu.VMEM((CROP + 2 * WD, 3 * C), BF16),
    ]


def fold_pair_body(share, keep_ref, up_ref, down_ref, *outs):
    here = lax.axis_index("dp") // 4
    for by, ref in enumerate(outs):
        pair = (here + by) % 4
        ref[0 : 2 * share] = keep_ref[pair, 0 : 2 * share] + up_ref[pair]
        ref[2 * share :] = keep_ref[pair, 2 * share :] + down_ref[pair]


def fold_body(share, *refs):
    parts, outs, held = refs[:4], refs[4:8], refs[8]
    total = (parts[0][...] + parts[1][...]) + (parts[2][...] + parts[3][...])
    for place in range(4):
        held[place] = total[place * share : (place + 1) * share]
    here = crossing(lax.axis_index("row"))
    for by, ref in enumerate(outs):
        ref[...] = held[(here + by) % 4]


def settle_body(*refs):
    parts, out_ref, held = refs[:4], refs[4], refs[5]
    here = crossing(lax.axis_index("row"))
    for by, part in enumerate(parts):
        held[(here + 4 - by) % 4] = part[...]
    for slot in range(4):
        out_ref[slot // 2, :, slot % 2, :] = held[slot]


def per_device(fresh, target, carried, returning, weights, section_blocks):
    tick_count = fresh.shape[0]
    cells = (
        tick_count
        * fresh.shape[1]
        * lax.axis_size("dp")
        * fresh.shape[2]
        * lax.axis_size("row")
        * fresh.shape[3]
    )
    segments = lax.axis_size("segment")
    dp_count = lax.axis_size("dp")
    rungs = dp_count // 2
    share = DEPTH // (2 * dp_count)
    flat = OWN * WD
    fresh = fresh.reshape(2, flat, 2 * C)
    target = target.reshape(flat, 2 * C)
    carried = carried.reshape(flat, 2 * C)
    returning = returning.reshape(2, flat, 2 * C)
    weights = weights.reshape(4, DEPTH, C)
    swap = [(0, 1), (1, 0)]
    onward = [(i, i + 1) for i in range(segments - 1)]
    homeward = [(i + 1, i) for i in range(segments - 1)]

    def across(by):
        pairs = []
        for row in range(2):
            for rung in range(rungs):
                for low in range(2):
                    there = (2 * row + low + by) % 4
                    pairs.append(
                        (
                            row * dp_count + 2 * rung + low,
                            (there // 2) * dp_count + 2 * rung + there % 2,
                        )
                    )
        return pairs

    def deal(parts):
        dealt = [parts[0]]
        for by in range(1, 4):
            dealt.append(lax.ppermute(parts[by], ("row", "dp"), across(by)))
        return dealt

    conv_flops = 6 * DEPTH * C
    other_pair = lax.ppermute(returning, "row", swap)
    (packed,) = call(
        pack_body,
        [(2 * flat, 2 * C)],
        [pltpu.SemaphoreType.DMA((3,))],
        tuple(in_hbm(value) for value in (fresh, carried, target)),
        8,
        1 << 20,
        space=pltpu.HBM,
    )
    other_pack = lax.ppermute(packed, "row", swap)
    plain, turned = prepare(weights)

    sent, *dealt = call(
        backward_full_body,
        [(2, WINDOW * WD, 2 * C)] + [(PACK, C)] * 4,
        backward_scratch(FULL * WD),
        (section_blocks, returning, other_pair, plain, turned),
        24,
        8 * conv_flops * FULL * WD,
        smem=(0,),
    )
    came_back = lax.ppermute(sent, "segment", homeward)
    early = deal(dealt)
    mid, *dealt = call(
        backward_window_body,
        [(2, 2, WINDOW * WD, C)] + [(PACK, C)] * 4,
        backward_scratch(WINDOW * WD) + forward_scratch(FULL * WD),
        (section_blocks, came_back, packed, target, other_pack, plain, turned),
        24,
        8 * conv_flops * WINDOW * WD,
        smem=(0,),
    )
    late = deal(dealt)
    (made,) = call(
        forward_full_body,
        [(WINDOW * WD, 2 * C)],
        forward_scratch(FULL * WD),
        (section_blocks, packed, other_pack, plain),
        24,
        4 * conv_flops * FULL * WD,
        smem=(0,),
    )
    (early_grad,) = call(
        early_grad_body, [(C, DEPTH)], grad_scratch(), tuple(early), 24, 4 * conv_flops * flat
    )
    keep, up, down = call(
        functools.partial(late_grad_body, 1.0 / math.sqrt(cells), share),
        [(4, 4 * share, C), (4, 2 * share, C), (4, 2 * share, C)],
        grad_scratch()
        + [pltpu.VMEM((DEPTH, C), F32), pltpu.VMEM((rungs, 4 * share, C), F32)],
        tuple(late) + (early_grad,),
        24,
        4 * conv_flops * flat,
    )

    def climb(goal):
        return [
            (2 * rung + low, 2 * (goal(rung) % rungs) + low)
            for rung in range(rungs)
            for low in range(2)
        ]

    up = lax.ppermute(up, "dp", climb(lambda rung: rung + 1 - 2 * (rung % 2)))
    down = lax.ppermute(down, "dp", climb(lambda rung: rung - 1 + 2 * (rung % 2)))
    came_on = lax.ppermute(made, "segment", onward)
    (back,) = call(
        backward_tail_body,
        [(2, flat, 2 * C)],
        backward_scratch(WINDOW * WD)[:2] + backward_scratch(WINDOW * WD)[3:7],
        (mid, plain, turned),
        24,
        2 * conv_flops * WINDOW * WD,
    )
    paired = call(
        functools.partial(fold_pair_body, share),
        [(4 * share, C)] * 4,
        [],
        (keep, up, down),
        8,
        1 << 20,
    )
    spread = [paired[0]]
    for by in (2, 1, 3):
        spread.append(
            lax.ppermute(paired[by], "dp", climb(lambda rung, by=by: rung + 2 * by))
        )
    (produced,) = call(
        forward_window_body,
        [(flat, 2 * C)],
        forward_scratch(WINDOW * WD),
        (section_blocks, came_on, fresh, other_pack, plain),
        24,
        4 * conv_flops * WINDOW * WD,
        smem=(0,),
    )
    folded = call(
        functools.partial(fold_body, share),
        [(share, C)] * 4,
        [pltpu.VMEM((4, share, C), F32)],
        tuple(spread),
        8,
        1 << 20,
    )
    settled = deal(folded)
    (grad_weights,) = call(
        settle_body,
        [(2, share, 2, C)],
        [pltpu.VMEM((4, share, C), F32)],
        tuple(settled),
        8,
        1 << 20,
    )
    return (
        grad_weights.transpose(0, 2, 1, 3)[None],
        produced.reshape(1, 1, OWN, WD, 2 * C),
        back.reshape(1, 2, 1, OWN, WD, 2 * C),
    )


def solution(mesh):
    return jax.shard_map(
        per_device,
        mesh=mesh,
        in_specs=(
            P(None, "dp", "row", None, None),
            P(None, "dp", "row", None, None),
            P("segment", "dp", "row", None, None),
            P("segment", None, "dp", "row", None, None),
            P("segment", None, None, None, None),
            P("segment"),
        ),
        out_specs=(
            P("segment", None, None, ("row", "dp"), None),
            P("segment", "dp", "row", None, None),
            P("segment", None, "dp", "row", None, None),
        ),
        check_vma=False,
    )
```

```python
import functools
import math

import jax
import jax.numpy as jnp
from jax import lax
from jax.experimental import pallas as pl
from jax.experimental.pallas import tpu as pltpu
from jax.sharding import PartitionSpec as P


F32 = jnp.float32
BF16 = jnp.bfloat16
C = 128
TAPS = 9
DEPTH = TAPS * C
WD = 16
OWN = 8
HALF = 4
FULL = 16
WINDOW = 12
PART = OWN * WD
PACK = 2 * PART
CROP = FULL * WD
MEGA = 1 << 20


def params(mib):
    return pltpu.CompilerParams(vmem_limit_bytes=mib * MEGA)


def cost(flops, nbytes):
    return pl.CostEstimate(flops=flops, bytes_accessed=nbytes, transcendentals=0)


def whole(memory_space=pltpu.VMEM):
    return pl.BlockSpec(memory_space=memory_space)


def call(body, out_shape, scratch, args, mib, flops, smem=(), space=pltpu.VMEM):
    in_specs = [whole(pltpu.SMEM if i in smem else space) for i in range(len(args))]
    outs = [jax.ShapeDtypeStruct(shape, F32) for shape in out_shape]
    nbytes = sum(4 * math.prod(shape) for shape in out_shape)
    return pl.pallas_call(
        body,
        out_shape=outs,
        in_specs=in_specs,
        out_specs=[whole() for _ in outs],
        scratch_shapes=scratch,
        compiler_params=params(mib),
        cost_estimate=cost(flops, nbytes),
    )(*args)


def in_hbm(value):
    return pltpu.with_memory_space_constraint(value, pltpu.HBM)


def rows(start, count):
    return pl.ds(pl.multiple_of(start * WD, HALF * WD), count * WD)


def hi_lo(value):
    high = value.astype(BF16)
    return high, (value - high.astype(F32)).astype(BF16)


def shifted(value):
    count = value.shape[0]
    column = lax.broadcasted_iota(jnp.int32, value.shape, 0) % WD
    left = jnp.where(column == 0, 0.0, pltpu.roll(value, 1, 0))
    right = jnp.where(column == WD - 1, 0.0, pltpu.roll(value, count - 1, 0))
    return left, value, right


def fill_patches(value, high_ref, low_ref):
    count = value.shape[0]
    for tap, moved in enumerate(shifted(value)):
        high, low = hi_lo(moved)
        high_ref[WD : WD + count, tap * C : (tap + 1) * C] = high
        low_ref[WD : WD + count, tap * C : (tap + 1) * C] = low


def clear_rim(ref, count):
    rim = jnp.zeros((WD,) + tuple(ref.shape[1:]), ref.dtype)
    ref[0:WD] = rim
    ref[WD + count : 2 * WD + count] = rim


def gathered(ref, count):
    return jnp.concatenate([ref[d * WD : d * WD + count, :] for d in range(3)], axis=1)


def conv(high_ref, low_ref, kernel_ref, slot, count):
    both = jnp.dot(gathered(high_ref, count), kernel_ref[slot], preferred_element_type=F32)
    rest = jnp.dot(
        gathered(low_ref, count), kernel_ref[slot, :, 0:C], preferred_element_type=F32
    )
    return both[:, :C] + (both[:, C:] + rest)


def logistic(value):
    return 1.0 / (1.0 + jnp.exp(-value))


def prepare_body(weight_ref, plain_ref, turned_ref, held, sems):
    slots = weight_ref.shape[0]
    for slot in range(slots):
        pltpu.make_async_copy(weight_ref.at[slot], held.at[slot], sems.at[slot]).start()

    def step(slot, carry):
        pltpu.make_async_copy(weight_ref.at[slot], held.at[slot], sems.at[slot]).wait()
        for tap in range(TAPS):
            block = held[slot, tap * C : (tap + 1) * C, :]
            high, low = hi_lo(block)
            plain_ref[slot, tap * C : (tap + 1) * C, 0:C] = high
            plain_ref[slot, tap * C : (tap + 1) * C, C:] = low
            high, low = hi_lo(block.T)
            back = TAPS - 1 - tap
            turned_ref[slot, back * C : (back + 1) * C, 0:C] = high
            turned_ref[slot, back * C : (back + 1) * C, C:] = low
        return carry

    lax.fori_loop(0, slots, step, 0)


def prepare(weights):
    slots = weights.shape[0]
    shape = jax.ShapeDtypeStruct((slots, DEPTH, 2 * C), BF16)
    return pl.pallas_call(
        prepare_body,
        out_shape=[shape, shape],
        in_specs=[whole(pltpu.HBM)],
        out_specs=[whole(), whole()],
        scratch_shapes=[
            pltpu.VMEM((slots, DEPTH, C), F32),
            pltpu.SemaphoreType.DMA((slots,)),
        ],
        compiler_params=params(16),
        cost_estimate=cost(slots * DEPTH * C * 8, slots * DEPTH * C * 12),
    )(in_hbm(weights))


def pack_body(fresh_ref, carried_ref, target_ref, out_ref, sems):
    first = lax.axis_index("segment") == 0
    start = HALF * (1 - lax.axis_index("row"))
    top = out_ref.at[0:PART]
    from_fresh = pltpu.make_async_copy(fresh_ref.at[0], top, sems.at[0])
    from_carried = pltpu.make_async_copy(carried_ref, top, sems.at[0])
    others = (
        pltpu.make_async_copy(target_ref, out_ref.at[PART : 2 * PART], sems.at[1]),
        pltpu.make_async_copy(
            fresh_ref.at[1, rows(start, HALF)], out_ref.at[2 * PART :], sems.at[2]
        ),
    )

    @pl.when(first)
    def _():
        from_fresh.start()

    @pl.when(jnp.logical_not(first))
    def _():
        from_carried.start()

    for copy in others:
        copy.start()

    @pl.when(first)
    def _():
        from_fresh.wait()

    @pl.when(jnp.logical_not(first))
    def _():
        from_carried.wait()

    for copy in others:
        copy.wait()


def put_halves(ref, where, value):
    ref[0, where] = value[:, :C]
    ref[1, where] = value[:, C:]


def forward_loop(state_ref, high_ref, low_ref, kernel_ref, blocks_ref, count):
    clear_rim(high_ref, count)
    clear_rim(low_ref, count)

    def step(slot, carry):
        half = slot % 2
        source = state_ref[1 - half]
        fill_patches(source * logistic(source), high_ref, low_ref)
        state_ref[half] = state_ref[half] + conv(high_ref, low_ref, kernel_ref, slot, count)
        return carry

    lax.fori_loop(0, 2 * blocks_ref[0], step, 0)


def forward_crop(blocks_ref, own_ref, other_ref, kernel_ref, state, high, low):
    row = lax.axis_index("row")
    put_halves(state, rows(OWN * row, OWN), own_ref[0 : OWN * WD])
    put_halves(state, rows(OWN * (1 - row), OWN), other_ref[0 : OWN * WD])
    forward_loop(state, high, low, kernel_ref, blocks_ref, CROP)


def is_final():
    return lax.axis_index("segment") == lax.axis_size("segment") - 1


def forward_full_body(blocks_ref, own_ref, other_ref, kernel_ref, out_ref, state, high, low):
    @pl.when(jnp.logical_not(is_final()))
    def _():
        forward_crop(blocks_ref, own_ref, other_ref, kernel_ref, state, high, low)
        part = rows(HALF * lax.axis_index("row"), WINDOW)
        out_ref[:, :C] = state[0, part]
        out_ref[:, C:] = state[1, part]


def forward_window_body(
    blocks_ref, came_ref, fresh_ref, other_ref, kernel_ref, out_ref, state, high, low
):
    row = lax.axis_index("row")
    first = lax.axis_index("segment") == 0

    @pl.when(first)
    def _():
        put_halves(state, rows(HALF * row, OWN), fresh_ref[1])
        put_halves(state, rows(OWN * (1 - row), HALF), other_ref[2 * PART :])

    @pl.when(jnp.logical_not(first))
    def _():
        put_halves(state, pl.ds(0, WINDOW * WD), came_ref[...])

    forward_loop(state, high, low, kernel_ref, blocks_ref, WINDOW * WD)
    part = rows(HALF * row, OWN)
    out_ref[:, :C] = state[0, part]
    out_ref[:, C:] = state[1, part]


def clear_picked(picked, blocks_ref):
    @pl.when(blocks_ref[0] < 2)
    def _():
        picked[2] = jnp.zeros((2, CROP, C), F32)
        picked[3] = jnp.zeros((2, CROP, C), F32)


def backward_step(slot, half, state, grads, plain_ref, turned_ref, pads, picked):
    source_high, source_low, grad_high, grad_low = pads
    source = state[1 - half]
    grad = grads[half]
    gate = logistic(source)
    field = source * gate
    fill_patches(field, source_high, source_low)
    fill_patches(grad, grad_high, grad_low)
    if picked is not None:
        picked[slot, 0] = field
        picked[slot, 1] = grad
    state[half] = state[half] - conv(source_high, source_low, plain_ref, slot, CROP)
    slope = gate * (1.0 + source * (1.0 - gate))
    grads[1 - half] = grads[1 - half] + slope * conv(
        grad_high, grad_low, turned_ref, slot, CROP
    )


def backward_loop(state, grads, plain_ref, turned_ref, blocks_ref, pads, picked, lowest):
    for ref in pads:
        clear_rim(ref, CROP)
    clear_picked(picked, blocks_ref)
    top = 2 * blocks_ref[0] - 1

    def step(turn, carry):
        slot = top - turn
        backward_step(slot, slot % 2, state, grads, plain_ref, turned_ref, pads, picked)
        return carry

    lax.fori_loop(0, top + 1 - lowest, step, 0)


def crossing(row):
    return 2 * row + lax.axis_index("dp") % 2


def hand_out(picked, own_ref, next_ref, last_ref):
    row = lax.axis_index("row")
    place = crossing(row)
    part = rows(OWN * row, OWN)
    own_ref[...] = picked[place]
    for by, ref in ((1, next_ref), (3, last_ref)):
        slot = (place + by) % 4
        ref[0:PART] = picked[slot, 0, part]
        ref[PART:] = picked[slot, 1, part]


def backward_full_body(
    blocks_ref, own_ref, other_ref, plain_ref, turned_ref, out_ref, *rest
):
    outs, (state, grads, picked), pads = rest[:3], rest[3:6], rest[6:]
    row = lax.axis_index("row")
    for ref, index in ((state, 0), (grads, 1)):
        put_halves(ref, rows(OWN * row, OWN), own_ref[index])
        put_halves(ref, rows(OWN * (1 - row), OWN), other_ref[index])
    backward_loop(state, grads, plain_ref, turned_ref, blocks_ref, pads, picked, 0)
    for ref, index in ((state, 0), (grads, 1)):
        out_ref[index, :, :C] = ref[0]
        out_ref[index, :, C:] = ref[1]
    hand_out(picked, *outs)


def backward_near_body(
    blocks_ref,
    came_ref,
    own_ref,
    target_ref,
    other_ref,
    plain_ref,
    turned_ref,
    mid_ref,
    *rest,
):
    outs, (state, grads, picked), pads, crop_pads = rest[:3], rest[3:6], rest[6:10], rest[10:]
    row = lax.axis_index("row")
    final = is_final()

    @pl.when(final)
    def _():
        forward_crop(blocks_ref, own_ref, other_ref, plain_ref, state, *crop_pads)
        put_halves(grads, rows(OWN * row, OWN), target_ref[...])
        put_halves(grads, rows(OWN * (1 - row), OWN), other_ref[PART : 2 * PART])
        grads[...] = state[...] - grads[...]

    @pl.when(jnp.logical_not(final))
    def _():
        put_halves(state, pl.ds(0, CROP), came_ref[0])
        put_halves(grads, pl.ds(0, CROP), came_ref[1])

    backward_loop(state, grads, plain_ref, turned_ref, blocks_ref, pads, picked, 1)
    source = state[1]
    picked[0, 0] = source * logistic(source)
    picked[0, 1] = grads[0]
    hand_out(picked, *outs)
    mid_ref[0] = state[...]
    mid_ref[1] = grads[...]


def backward_tail_body(mid_ref, plain_ref, turned_ref, out_ref, state, grads, *pads):
    state[...] = mid_ref[0]
    grads[...] = mid_ref[1]
    for ref in pads:
        clear_rim(ref, CROP)
    backward_step(0, 0, state, grads, plain_ref, turned_ref, pads, None)
    part = rows(OWN * lax.axis_index("row"), OWN)
    for ref, index in ((state, 0), (grads, 1)):
        out_ref[index, :, :C] = ref[0, part]
        out_ref[index, :, C:] = ref[1, part]


def forward_scratch(count):
    return [
        pltpu.VMEM((2, count, C), F32),
        pltpu.VMEM((count + 2 * WD, 3 * C), BF16),
        pltpu.VMEM((count + 2 * WD, 3 * C), BF16),
    ]


def pad_scratch(number):
    return [pltpu.VMEM((CROP + 2 * WD, 3 * C), BF16)] * number


def backward_scratch():
    return [
        pltpu.VMEM((2, CROP, C), F32),
        pltpu.VMEM((2, CROP, C), F32),
        pltpu.VMEM((4, 2, CROP, C), F32),
    ] + pad_scratch(4)


def kernel_grad(parts, held_ref, high_ref, low_ref):
    own_ref, last_ref, next_ref = parts
    here = crossing(lax.axis_index("row"))
    for by, ref in ((1, last_ref), (3, next_ref)):
        at = rows(OWN * (((here + 4 - by) % 4) // 2), OWN)
        held_ref[0, at] = ref[0:PART]
        held_ref[1, at] = ref[PART:]
    clear_rim(high_ref, CROP)
    clear_rim(low_ref, CROP)
    total = None
    for crop_ref in (own_ref, held_ref):
        fill_patches(crop_ref[0], high_ref, low_ref)
        high, low = hi_lo(crop_ref[1].T)
        both = jnp.dot(
            jnp.concatenate([high, low], axis=0),
            gathered(high_ref, CROP),
            preferred_element_type=F32,
        )
        rest = jnp.dot(high, gathered(low_ref, CROP), preferred_element_type=F32)
        piece = both[:C] + (both[C:] + rest)
        total = piece if total is None else total + piece
    return total


def early_grad_body(*refs):
    parts, out_ref, scratch = refs[:3], refs[3], refs[4:]
    out_ref[...] = kernel_grad(parts, *scratch)


def late_grad_body(scale, share, *refs):
    parts, early_ref, (keep_ref, up_ref, down_ref) = refs[:3], refs[3], refs[4:7]
    scratch, (total_ref, held) = refs[7:10], refs[10:]
    total = (kernel_grad(parts, *scratch) + early_ref[...]) * scale
    for tap in range(TAPS):
        total_ref[tap * C : (tap + 1) * C, :] = total[:, tap * C : (tap + 1) * C].T
    for along in range(8):
        for place in range(4):
            start = share * (16 * (place // 2) + 2 * along + place % 2)
            held[along, place * share : (place + 1) * share] = total_ref[start : start + share]
    odd = (lax.axis_index("dp") // 2) % 2
    for pair in range(4):
        keep_ref[pair] = held[2 * pair + odd]
        up_ref[pair] = held[2 * pair + 1 - odd, 0 : 2 * share]
        down_ref[pair] = held[2 * pair + 1 - odd, 2 * share :]


def grad_scratch():
    return [pltpu.VMEM((2, CROP, C), F32)] + pad_scratch(2)


def fold_pair_body(share, keep_ref, up_ref, down_ref, *outs):
    here = lax.axis_index("dp") // 4
    for by, ref in enumerate(outs):
        pair = (here + by) % 4
        ref[0 : 2 * share] = keep_ref[pair, 0 : 2 * share] + up_ref[pair]
        ref[2 * share :] = keep_ref[pair, 2 * share :] + down_ref[pair]


def fold_body(share, *refs):
    parts, outs, held = refs[:4], refs[4:8], refs[8]
    total = (parts[0][...] + parts[1][...]) + (parts[2][...] + parts[3][...])
    for place in range(4):
        held[place] = total[place * share : (place + 1) * share]
    here = crossing(lax.axis_index("row"))
    for by, ref in enumerate(outs):
        ref[...] = held[(here + by) % 4]


def settle_body(*refs):
    parts, out_ref, held = refs[:4], refs[4], refs[5]
    here = crossing(lax.axis_index("row"))
    for by, part in enumerate(parts):
        held[(here + 4 - by) % 4] = part[...]
    for slot in range(4):
        out_ref[slot // 2, :, slot % 2, :] = held[slot]


def per_device(fresh, target, carried, returning, weights, section_blocks):
    tick_count = fresh.shape[0]
    cells = (
        tick_count
        * fresh.shape[1]
        * lax.axis_size("dp")
        * fresh.shape[2]
        * lax.axis_size("row")
        * fresh.shape[3]
    )
    segments = lax.axis_size("segment")
    dp_count = lax.axis_size("dp")
    rungs = dp_count // 2
    share = DEPTH // (2 * dp_count)
    flat = OWN * WD
    fresh = fresh.reshape(2, flat, 2 * C)
    target = target.reshape(flat, 2 * C)
    carried = carried.reshape(flat, 2 * C)
    returning = returning.reshape(2, flat, 2 * C)
    weights = weights.reshape(4, DEPTH, C)
    swap = [(0, 1), (1, 0)]
    onward = [(i, i + 1) for i in range(segments - 1)]
    homeward = [(i + 1, i) for i in range(segments - 1)]

    def across(by):
        pairs = []
        for row in range(2):
            for rung in range(rungs):
                for low in range(2):
                    there = (2 * row + low + by) % 4
                    pairs.append(
                        (
                            row * dp_count + 2 * rung + low,
                            (there // 2) * dp_count + 2 * rung + there % 2,
                        )
                    )
        return pairs

    def deal(parts, steps):
        dealt = [parts[0]]
        for by in steps:
            dealt.append(lax.ppermute(parts[len(dealt)], ("row", "dp"), across(by)))
        return dealt

    conv_flops = 6 * DEPTH * C
    other_pair = lax.ppermute(returning, "row", swap)
    (packed,) = call(
        pack_body,
        [((FULL + HALF) * WD, 2 * C)],
        [pltpu.SemaphoreType.DMA((3,))],
        tuple(in_hbm(value) for value in (fresh, carried, target)),
        8,
        1 << 20,
        space=pltpu.HBM,
    )
    other_pack = lax.ppermute(packed, "row", swap)
    plain, turned = prepare(weights)

    sent, *dealt = call(
        backward_full_body,
        [(2, CROP, 2 * C), (2, CROP, C), (PACK, C), (PACK, C)],
        backward_scratch(),
        (section_blocks, returning, other_pair, plain, turned),
        24,
        8 * conv_flops * FULL * WD,
        smem=(0,),
    )
    came_back = lax.ppermute(sent, "segment", homeward)
    early = deal(dealt, (1, 3))
    mid, *dealt = call(
        backward_near_body,
        [(2, 2, CROP, C), (2, CROP, C), (PACK, C), (PACK, C)],
        backward_scratch() + pad_scratch(2),
        (section_blocks, came_back, packed, target, other_pack, plain, turned),
        24,
        8 * conv_flops * WINDOW * WD,
        smem=(0,),
    )
    late = deal(dealt, (1, 3))
    (made,) = call(
        forward_full_body,
        [(WINDOW * WD, 2 * C)],
        forward_scratch(FULL * WD),
        (section_blocks, packed, other_pack, plain),
        24,
        4 * conv_flops * FULL * WD,
        smem=(0,),
    )
    (early_grad,) = call(
        early_grad_body, [(C, DEPTH)], grad_scratch(), tuple(early), 24, 4 * conv_flops * flat
    )
    keep, up, down = call(
        functools.partial(late_grad_body, 1.0 / math.sqrt(cells), share),
        [(4, 4 * share, C), (4, 2 * share, C), (4, 2 * share, C)],
        grad_scratch()
        + [pltpu.VMEM((DEPTH, C), F32), pltpu.VMEM((rungs, 4 * share, C), F32)],
        tuple(late) + (early_grad,),
        24,
        4 * conv_flops * flat,
    )

    def climb(goal):
        return [
            (2 * rung + low, 2 * (goal(rung) % rungs) + low)
            for rung in range(rungs)
            for low in range(2)
        ]

    up = lax.ppermute(up, "dp", climb(lambda rung: rung + 1 - 2 * (rung % 2)))
    down = lax.ppermute(down, "dp", climb(lambda rung: rung - 1 + 2 * (rung % 2)))
    came_on = lax.ppermute(made, "segment", onward)
    (back,) = call(
        backward_tail_body,
        [(2, flat, 2 * C)],
        backward_scratch()[:2] + pad_scratch(4),
        (mid, plain, turned),
        24,
        2 * conv_flops * WINDOW * WD,
    )
    paired = call(
        functools.partial(fold_pair_body, share),
        [(4 * share, C)] * 4,
        [],
        (keep, up, down),
        8,
        1 << 20,
    )
    spread = [paired[0]]
    for by in (2, 1, 3):
        spread.append(
            lax.ppermute(paired[by], "dp", climb(lambda rung, by=by: rung + 2 * by))
        )
    (produced,) = call(
        forward_window_body,
        [(flat, 2 * C)],
        forward_scratch(WINDOW * WD),
        (section_blocks, came_on, fresh, other_pack, plain),
        24,
        4 * conv_flops * WINDOW * WD,
        smem=(0,),
    )
    folded = call(
        functools.partial(fold_body, share),
        [(share, C)] * 4,
        [pltpu.VMEM((4, share, C), F32)],
        tuple(spread),
        8,
        1 << 20,
    )
    settled = deal(folded, (1, 2, 3))
    (grad_weights,) = call(
        settle_body,
        [(2, share, 2, C)],
        [pltpu.VMEM((4, share, C), F32)],
        tuple(settled),
        8,
        1 << 20,
    )
    return (
        grad_weights.transpose(0, 2, 1, 3)[None],
        produced.reshape(1, 1, OWN, WD, 2 * C),
        back.reshape(1, 2, 1, OWN, WD, 2 * C),
    )


def solution(mesh):
    return jax.shard_map(
        per_device,
        mesh=mesh,
        in_specs=(
            P(None, "dp", "row", None, None),
            P(None, "dp", "row", None, None),
            P("segment", "dp", "row", None, None),
            P("segment", None, "dp", "row", None, None),
            P("segment", None, None, None, None),
            P("segment"),
        ),
        out_specs=(
            P("segment", None, None, ("row", "dp"), None),
            P("segment", "dp", "row", None, None),
            P("segment", None, "dp", "row", None, None),
        ),
        check_vma=False,
    )
```

```python
import functools
import math

import jax
import jax.numpy as jnp
from jax import lax
from jax.experimental import pallas as pl
from jax.experimental.pallas import tpu as pltpu
from jax.sharding import PartitionSpec as P


F32 = jnp.float32
BF16 = jnp.bfloat16
C = 128
TAPS = 9
DEPTH = TAPS * C
WD = 16
OWN = 8
HALF = 4
FULL = 16
WINDOW = 12
PART = OWN * WD
CROP = FULL * WD
MEGA = 1 << 20


def params(mib):
    return pltpu.CompilerParams(vmem_limit_bytes=mib * MEGA)


def cost(flops, nbytes):
    return pl.CostEstimate(flops=flops, bytes_accessed=nbytes, transcendentals=0)


def whole(memory_space=pltpu.VMEM):
    return pl.BlockSpec(memory_space=memory_space)


def call(body, out_shape, scratch, args, mib, flops, smem=(), space=pltpu.VMEM):
    in_specs = [whole(pltpu.SMEM if i in smem else space) for i in range(len(args))]
    outs = [jax.ShapeDtypeStruct(shape, F32) for shape in out_shape]
    nbytes = sum(4 * math.prod(shape) for shape in out_shape)
    return pl.pallas_call(
        body,
        out_shape=outs,
        in_specs=in_specs,
        out_specs=[whole() for _ in outs],
        scratch_shapes=scratch,
        compiler_params=params(mib),
        cost_estimate=cost(flops, nbytes),
    )(*args)


def in_hbm(value):
    return pltpu.with_memory_space_constraint(value, pltpu.HBM)


def rows(start, count):
    return pl.ds(pl.multiple_of(start * WD, HALF * WD), count * WD)


def hi_lo(value):
    high = value.astype(BF16)
    return high, (value - high.astype(F32)).astype(BF16)


def shifted(value):
    count = value.shape[0]
    column = lax.broadcasted_iota(jnp.int32, value.shape, 0) % WD
    left = jnp.where(column == 0, 0.0, pltpu.roll(value, 1, 0))
    right = jnp.where(column == WD - 1, 0.0, pltpu.roll(value, count - 1, 0))
    return left, value, right


def fill_patches(value, high_ref, low_ref):
    count = value.shape[0]
    for tap, moved in enumerate(shifted(value)):
        high, low = hi_lo(moved)
        high_ref[WD : WD + count, tap * C : (tap + 1) * C] = high
        low_ref[WD : WD + count, tap * C : (tap + 1) * C] = low


def clear_rim(ref, count):
    rim = jnp.zeros((WD,) + tuple(ref.shape[1:]), ref.dtype)
    ref[0:WD] = rim
    ref[WD + count : 2 * WD + count] = rim


def gathered(ref, count):
    return jnp.concatenate([ref[d * WD : d * WD + count, :] for d in range(3)], axis=1)


def conv(high_ref, low_ref, kernel_ref, slot, count):
    both = jnp.dot(gathered(high_ref, count), kernel_ref[slot], preferred_element_type=F32)
    rest = jnp.dot(
        gathered(low_ref, count), kernel_ref[slot, :, 0:C], preferred_element_type=F32
    )
    return both[:, :C] + (both[:, C:] + rest)


def logistic(value):
    return 1.0 / (1.0 + jnp.exp(-value))


def prepare_body(weight_ref, plain_ref, turned_ref, held, sems):
    slots = weight_ref.shape[0]
    for slot in range(slots):
        pltpu.make_async_copy(weight_ref.at[slot], held.at[slot], sems.at[slot]).start()

    def step(slot, carry):
        pltpu.make_async_copy(weight_ref.at[slot], held.at[slot], sems.at[slot]).wait()
        for tap in range(TAPS):
            block = held[slot, tap * C : (tap + 1) * C, :]
            high, low = hi_lo(block)
            plain_ref[slot, tap * C : (tap + 1) * C, 0:C] = high
            plain_ref[slot, tap * C : (tap + 1) * C, C:] = low
            high, low = hi_lo(block.T)
            back = TAPS - 1 - tap
            turned_ref[slot, back * C : (back + 1) * C, 0:C] = high
            turned_ref[slot, back * C : (back + 1) * C, C:] = low
        return carry

    lax.fori_loop(0, slots, step, 0)


def prepare(weights):
    slots = weights.shape[0]
    shape = jax.ShapeDtypeStruct((slots, DEPTH, 2 * C), BF16)
    return pl.pallas_call(
        prepare_body,
        out_shape=[shape, shape],
        in_specs=[whole(pltpu.HBM)],
        out_specs=[whole(), whole()],
        scratch_shapes=[
            pltpu.VMEM((slots, DEPTH, C), F32),
            pltpu.SemaphoreType.DMA((slots,)),
        ],
        compiler_params=params(16),
        cost_estimate=cost(slots * DEPTH * C * 8, slots * DEPTH * C * 12),
    )(in_hbm(weights))


def pack_body(fresh_ref, carried_ref, target_ref, out_ref, sems):
    first = lax.axis_index("segment") == 0
    start = HALF * (1 - lax.axis_index("row"))
    top = out_ref.at[0:PART]
    from_fresh = pltpu.make_async_copy(fresh_ref.at[0], top, sems.at[0])
    from_carried = pltpu.make_async_copy(carried_ref, top, sems.at[0])
    others = (
        pltpu.make_async_copy(target_ref, out_ref.at[PART : 2 * PART], sems.at[1]),
        pltpu.make_async_copy(
            fresh_ref.at[1, rows(start, HALF)], out_ref.at[2 * PART :], sems.at[2]
        ),
    )

    @pl.when(first)
    def _():
        from_fresh.start()

    @pl.when(jnp.logical_not(first))
    def _():
        from_carried.start()

    for copy in others:
        copy.start()

    @pl.when(first)
    def _():
        from_fresh.wait()

    @pl.when(jnp.logical_not(first))
    def _():
        from_carried.wait()

    for copy in others:
        copy.wait()


def put_halves(ref, where, value):
    ref[0, where] = value[:, :C]
    ref[1, where] = value[:, C:]


def forward_loop(state_ref, high_ref, low_ref, kernel_ref, blocks_ref, count):
    clear_rim(high_ref, count)
    clear_rim(low_ref, count)

    def step(slot, carry):
        half = slot % 2
        source = state_ref[1 - half]
        fill_patches(source * logistic(source), high_ref, low_ref)
        state_ref[half] = state_ref[half] + conv(high_ref, low_ref, kernel_ref, slot, count)
        return carry

    lax.fori_loop(0, 2 * blocks_ref[0], step, 0)


def forward_crop(blocks_ref, own_ref, other_ref, kernel_ref, state, high, low):
    row = lax.axis_index("row")
    put_halves(state, rows(OWN * row, OWN), own_ref[0 : OWN * WD])
    put_halves(state, rows(OWN * (1 - row), OWN), other_ref[0 : OWN * WD])
    forward_loop(state, high, low, kernel_ref, blocks_ref, CROP)


def is_final():
    return lax.axis_index("segment") == lax.axis_size("segment") - 1


def forward_full_body(blocks_ref, own_ref, other_ref, kernel_ref, out_ref, state, high, low):
    @pl.when(jnp.logical_not(is_final()))
    def _():
        forward_crop(blocks_ref, own_ref, other_ref, kernel_ref, state, high, low)
        part = rows(HALF * lax.axis_index("row"), WINDOW)
        out_ref[:, :C] = state[0, part]
        out_ref[:, C:] = state[1, part]


def forward_window_body(
    blocks_ref, came_ref, fresh_ref, other_ref, kernel_ref, out_ref, state, high, low
):
    row = lax.axis_index("row")
    first = lax.axis_index("segment") == 0

    @pl.when(first)
    def _():
        put_halves(state, rows(HALF * row, OWN), fresh_ref[1])
        put_halves(state, rows(OWN * (1 - row), HALF), other_ref[2 * PART :])

    @pl.when(jnp.logical_not(first))
    def _():
        put_halves(state, pl.ds(0, WINDOW * WD), came_ref[...])

    forward_loop(state, high, low, kernel_ref, blocks_ref, WINDOW * WD)
    part = rows(HALF * row, OWN)
    out_ref[:, :C] = state[0, part]
    out_ref[:, C:] = state[1, part]


def clear_picked(picked, blocks_ref):
    @pl.when(blocks_ref[0] < 2)
    def _():
        picked[2] = jnp.zeros((2, CROP, C), F32)
        picked[3] = jnp.zeros((2, CROP, C), F32)


def backward_step(slot, half, state, grads, plain_ref, turned_ref, pads, picked):
    source_high, source_low, grad_high, grad_low = pads
    source = state[1 - half]
    grad = grads[half]
    gate = logistic(source)
    field = source * gate
    fill_patches(field, source_high, source_low)
    fill_patches(grad, grad_high, grad_low)
    if picked is not None:
        picked[slot, 0] = field
        picked[slot, 1] = grad
    state[half] = state[half] - conv(source_high, source_low, plain_ref, slot, CROP)
    slope = gate * (1.0 + source * (1.0 - gate))
    grads[1 - half] = grads[1 - half] + slope * conv(
        grad_high, grad_low, turned_ref, slot, CROP
    )


def backward_loop(state, grads, plain_ref, turned_ref, blocks_ref, pads, picked, lowest):
    for ref in pads:
        clear_rim(ref, CROP)
    clear_picked(picked, blocks_ref)
    top = 2 * blocks_ref[0] - 1

    def step(turn, carry):
        slot = top - turn
        backward_step(slot, slot % 2, state, grads, plain_ref, turned_ref, pads, picked)
        return carry

    lax.fori_loop(0, top + 1 - lowest, step, 0)


def crossing(row):
    return 2 * row + lax.axis_index("dp") % 2


def hand_out(picked, out_ref):
    place = crossing(lax.axis_index("row"))
    for turn in range(2):
        out_ref[turn] = picked[(place + turn) % 4]


def backward_full_body(
    blocks_ref, own_ref, other_ref, plain_ref, turned_ref, out_ref, *rest
):
    pair_ref, (state, grads, picked), pads = rest[0], rest[1:4], rest[4:]
    row = lax.axis_index("row")
    for ref, index in ((state, 0), (grads, 1)):
        put_halves(ref, rows(OWN * row, OWN), own_ref[index])
        put_halves(ref, rows(OWN * (1 - row), OWN), other_ref[index])
    backward_loop(state, grads, plain_ref, turned_ref, blocks_ref, pads, picked, 0)
    for ref, index in ((state, 0), (grads, 1)):
        out_ref[index, :, :C] = ref[0]
        out_ref[index, :, C:] = ref[1]
    hand_out(picked, pair_ref)


def backward_near_body(
    blocks_ref,
    came_ref,
    own_ref,
    target_ref,
    other_ref,
    plain_ref,
    turned_ref,
    mid_ref,
    *rest,
):
    pair_ref, (state, grads, picked) = rest[0], rest[1:4]
    pads, crop_pads = rest[4:8], rest[8:]
    row = lax.axis_index("row")
    final = is_final()

    @pl.when(final)
    def _():
        forward_crop(blocks_ref, own_ref, other_ref, plain_ref, state, *crop_pads)
        put_halves(grads, rows(OWN * row, OWN), target_ref[...])
        put_halves(grads, rows(OWN * (1 - row), OWN), other_ref[PART : 2 * PART])
        grads[...] = state[...] - grads[...]

    @pl.when(jnp.logical_not(final))
    def _():
        put_halves(state, pl.ds(0, CROP), came_ref[0])
        put_halves(grads, pl.ds(0, CROP), came_ref[1])

    backward_loop(state, grads, plain_ref, turned_ref, blocks_ref, pads, picked, 1)
    source = state[1]
    picked[0, 0] = source * logistic(source)
    picked[0, 1] = grads[0]
    hand_out(picked, pair_ref)
    mid_ref[0] = state[...]
    mid_ref[1] = grads[...]


def backward_tail_body(mid_ref, plain_ref, turned_ref, out_ref, state, grads, *pads):
    state[...] = mid_ref[0]
    grads[...] = mid_ref[1]
    for ref in pads:
        clear_rim(ref, CROP)
    backward_step(0, 0, state, grads, plain_ref, turned_ref, pads, None)
    part = rows(OWN * lax.axis_index("row"), OWN)
    for ref, index in ((state, 0), (grads, 1)):
        out_ref[index, :, :C] = ref[0, part]
        out_ref[index, :, C:] = ref[1, part]


def forward_scratch(count):
    return [
        pltpu.VMEM((2, count, C), F32),
        pltpu.VMEM((count + 2 * WD, 3 * C), BF16),
        pltpu.VMEM((count + 2 * WD, 3 * C), BF16),
    ]


def pad_scratch(number):
    return [pltpu.VMEM((CROP + 2 * WD, 3 * C), BF16)] * number


def backward_scratch():
    return [
        pltpu.VMEM((2, CROP, C), F32),
        pltpu.VMEM((2, CROP, C), F32),
        pltpu.VMEM((4, 2, CROP, C), F32),
    ] + pad_scratch(4)


def kernel_grad(crop_ref, turn, high_ref, low_ref):
    fill_patches(crop_ref[turn, 0], high_ref, low_ref)
    high, low = hi_lo(crop_ref[turn, 1].T)
    both = jnp.dot(
        jnp.concatenate([high, low], axis=0),
        gathered(high_ref, CROP),
        preferred_element_type=F32,
    )
    rest = jnp.dot(high, gathered(low_ref, CROP), preferred_element_type=F32)
    return both[:C] + (both[C:] + rest)


def early_grad_body(crop_ref, out_ref, *pads):
    for turn in range(2):
        for ref in pads[2 * turn : 2 * turn + 2]:
            clear_rim(ref, CROP)
        out_ref[turn] = kernel_grad(crop_ref, turn, *pads[2 * turn : 2 * turn + 2])


def late_grad_body(scale, share, crop_ref, early_ref, *refs):
    outs, pads, (total_ref, held) = refs[:8], refs[8:12], refs[12:]
    here = crossing(lax.axis_index("row"))
    odd = (lax.axis_index("dp") // 2) % 2
    for turn in range(2):
        keep_ref, side_ref, along_ref, slant_ref = outs[4 * turn : 4 * turn + 4]
        for ref in pads[2 * turn : 2 * turn + 2]:
            clear_rim(ref, CROP)
        total = kernel_grad(crop_ref, turn, *pads[2 * turn : 2 * turn + 2])
        total = (total + early_ref[turn]) * scale
        for tap in range(TAPS):
            total_ref[turn, tap * C : (tap + 1) * C, :] = total[:, tap * C : (tap + 1) * C].T
        for along in range(8):
            for place in range(4):
                start = share * (16 * (place // 2) + 2 * along + place % 2)
                held[turn, along, place] = total_ref[turn, start : start + share]
        step = 1 - 2 * turn
        mine = (here, (here + 4 + step) % 4)
        theirs = ((here + 4 - step) % 4, (here + 4 - 2 * step) % 4)
        for pair in range(4):
            for place in range(2):
                at = slice(place * share, (place + 1) * share)
                keep_ref[pair, at] = held[turn, 2 * pair + odd, mine[place]]
                side_ref[pair, at] = held[turn, 2 * pair + odd, theirs[place]]
                along_ref[pair, at] = held[turn, 2 * pair + 1 - odd, mine[place]]
                slant_ref[pair, at] = held[turn, 2 * pair + 1 - odd, theirs[place]]


def fold_pair_body(share, *refs):
    parts, outs = refs[:8], refs[8:]
    here = lax.axis_index("dp") // 4
    for by, ref in enumerate(outs):
        pair = (here + by) % 4
        for turn in range(2):
            keep, side, along, slant = (part[pair] for part in parts[4 * turn : 4 * turn + 4])
            ref[2 * turn * share : 2 * (turn + 1) * share] = (keep + side) + (along + slant)


def fold_body(share, *refs):
    parts, (keep_ref, up_ref, down_ref) = refs[:4], refs[4:]
    total = (parts[0][...] + parts[1][...]) + (parts[2][...] + parts[3][...])
    keep_ref[0] = total[0:share]
    up_ref[...] = total[share : 2 * share]
    keep_ref[1] = total[2 * share : 3 * share]
    down_ref[...] = total[3 * share :]


def settle_body(keep_ref, up_ref, down_ref, out_ref, held):
    here = crossing(lax.axis_index("row"))
    held[here] = keep_ref[0]
    held[(here + 1) % 4] = keep_ref[1]
    held[(here + 3) % 4] = up_ref[...]
    held[(here + 2) % 4] = down_ref[...]
    for slot in range(4):
        out_ref[slot // 2, :, slot % 2, :] = held[slot]


def per_device(fresh, target, carried, returning, weights, section_blocks):
    tick_count = fresh.shape[0]
    cells = (
        tick_count
        * fresh.shape[1]
        * lax.axis_size("dp")
        * fresh.shape[2]
        * lax.axis_size("row")
        * fresh.shape[3]
    )
    segments = lax.axis_size("segment")
    dp_count = lax.axis_size("dp")
    rungs = dp_count // 2
    share = DEPTH // (2 * dp_count)
    flat = OWN * WD
    fresh = fresh.reshape(2, flat, 2 * C)
    target = target.reshape(flat, 2 * C)
    carried = carried.reshape(flat, 2 * C)
    returning = returning.reshape(2, flat, 2 * C)
    weights = weights.reshape(4, DEPTH, C)
    swap = [(0, 1), (1, 0)]
    onward = [(i, i + 1) for i in range(segments - 1)]
    homeward = [(i + 1, i) for i in range(segments - 1)]

    def neighbour(rung, conv):
        step = 1 - 2 * ((rung + conv) % 2)
        return (rung + step) % rungs

    def route(goal):
        pairs = []
        for place in range(4):
            for rung in range(rungs):
                there, above = goal(place, rung)
                pairs.append(
                    tuple(
                        (spot % 4 // 2) * dp_count + 2 * (level % rungs) + spot % 2
                        for spot, level in ((place, rung), (there, above))
                    )
                )
        return pairs

    def send(value, goal):
        return lax.ppermute(value, ("row", "dp"), route(goal))

    conv_flops = 6 * DEPTH * C
    other_pair = lax.ppermute(returning, "row", swap)
    (packed,) = call(
        pack_body,
        [((FULL + HALF) * WD, 2 * C)],
        [pltpu.SemaphoreType.DMA((3,))],
        tuple(in_hbm(value) for value in (fresh, carried, target)),
        8,
        1 << 20,
        space=pltpu.HBM,
    )
    other_pack = lax.ppermute(packed, "row", swap)
    plain, turned = prepare(weights)

    sent, early_pair = call(
        backward_full_body,
        [(2, CROP, 2 * C), (2, 2, CROP, C)],
        backward_scratch(),
        (section_blocks, returning, other_pair, plain, turned),
        24,
        8 * conv_flops * CROP,
        smem=(0,),
    )
    came_back = lax.ppermute(sent, "segment", homeward)
    (early_grad,) = call(
        early_grad_body,
        [(2, C, DEPTH)],
        pad_scratch(4),
        (early_pair,),
        24,
        2 * conv_flops * CROP,
    )
    (made,) = call(
        forward_full_body,
        [(WINDOW * WD, 2 * C)],
        forward_scratch(CROP),
        (section_blocks, packed, other_pack, plain),
        24,
        4 * conv_flops * CROP,
        smem=(0,),
    )
    mid, late_pair = call(
        backward_near_body,
        [(2, 2, CROP, C), (2, 2, CROP, C)],
        backward_scratch() + pad_scratch(2),
        (section_blocks, came_back, packed, target, other_pack, plain, turned),
        24,
        6 * conv_flops * CROP,
        smem=(0,),
    )
    parts = call(
        functools.partial(late_grad_body, 1.0 / math.sqrt(cells), share),
        [(4, 2 * share, C)] * 8,
        pad_scratch(4)
        + [pltpu.VMEM((2, DEPTH, C), F32), pltpu.VMEM((2, rungs, 4, share, C), F32)],
        (late_pair, early_grad),
        24,
        2 * conv_flops * CROP,
    )
    parts = list(parts)
    came = [parts[0], None, None, None, parts[4], None, None, None]
    came[3] = send(parts[7], lambda x, z: (x + 1, neighbour(z, x + 1)))
    came[7] = send(parts[3], lambda x, z: (x - 1, neighbour(z, x)))
    came[1] = send(parts[5], lambda x, z: (x + 1, z))
    came[5] = send(parts[1], lambda x, z: (x - 1, z))
    came[2] = send(parts[2], lambda x, z: (x, neighbour(z, x)))
    came[6] = send(parts[6], lambda x, z: (x, neighbour(z, x + 1)))
    came_on = lax.ppermute(made, "segment", onward)
    (back,) = call(
        backward_tail_body,
        [(2, flat, 2 * C)],
        backward_scratch()[:2] + pad_scratch(4),
        (mid, plain, turned),
        24,
        2 * conv_flops * CROP,
    )
    paired = call(
        functools.partial(fold_pair_body, share),
        [(4 * share, C)] * 4,
        [],
        tuple(came),
        8,
        1 << 20,
    )
    spread = [paired[0]]
    for by in (2, 1, 3):
        spread.append(send(paired[by], lambda x, z, by=by: (x, z + 2 * by)))
    (produced,) = call(
        forward_window_body,
        [(flat, 2 * C)],
        forward_scratch(WINDOW * WD),
        (section_blocks, came_on, fresh, other_pack, plain),
        24,
        4 * conv_flops * WINDOW * WD,
        smem=(0,),
    )
    keep, up, down = call(
        functools.partial(fold_body, share),
        [(2, share, C), (share, C), (share, C)],
        [],
        tuple(spread),
        8,
        1 << 20,
    )
    up = send(up, lambda x, z: (x + 1, z))
    down = send(down, lambda x, z: (x - 1, z))
    (grad_weights,) = call(
        settle_body,
        [(2, share, 2, C)],
        [pltpu.VMEM((4, share, C), F32)],
        (keep, up, down),
        8,
        1 << 20,
    )
    return (
        grad_weights.transpose(0, 2, 1, 3)[None],
        produced.reshape(1, 1, OWN, WD, 2 * C),
        back.reshape(1, 2, 1, OWN, WD, 2 * C),
    )


def solution(mesh):
    return jax.shard_map(
        per_device,
        mesh=mesh,
        in_specs=(
            P(None, "dp", "row", None, None),
            P(None, "dp", "row", None, None),
            P("segment", "dp", "row", None, None),
            P("segment", None, "dp", "row", None, None),
            P("segment", None, None, None, None),
            P("segment"),
        ),
        out_specs=(
            P("segment", None, None, ("row", "dp"), None),
            P("segment", "dp", "row", None, None),
            P("segment", None, "dp", "row", None, None),
        ),
        check_vma=False,
    )
```

```python
import functools
import math

import jax
import jax.numpy as jnp
from jax import lax
from jax.experimental import pallas as pl
from jax.experimental.pallas import tpu as pltpu
from jax.sharding import PartitionSpec as P


F32 = jnp.float32
BF16 = jnp.bfloat16
C = 128
TAPS = 9
DEPTH = TAPS * C
WD = 16
OWN = 8
HALF = 4
FULL = 16
WINDOW = 12
PART = OWN * WD
CROP = FULL * WD
MEGA = 1 << 20


def params(mib):
    return pltpu.CompilerParams(vmem_limit_bytes=mib * MEGA)


def cost(flops, nbytes):
    return pl.CostEstimate(flops=flops, bytes_accessed=nbytes, transcendentals=0)


def whole(memory_space=pltpu.VMEM):
    return pl.BlockSpec(memory_space=memory_space)


def call(body, out_shape, scratch, args, mib, flops, smem=(), space=pltpu.VMEM):
    in_specs = [whole(pltpu.SMEM if i in smem else space) for i in range(len(args))]
    outs = [jax.ShapeDtypeStruct(shape, F32) for shape in out_shape]
    nbytes = sum(4 * math.prod(shape) for shape in out_shape)
    return pl.pallas_call(
        body,
        out_shape=outs,
        in_specs=in_specs,
        out_specs=[whole() for _ in outs],
        scratch_shapes=scratch,
        compiler_params=params(mib),
        cost_estimate=cost(flops, nbytes),
    )(*args)


def in_hbm(value):
    return pltpu.with_memory_space_constraint(value, pltpu.HBM)


def rows(start, count):
    return pl.ds(pl.multiple_of(start * WD, HALF * WD), count * WD)


def hi_lo(value):
    high = value.astype(BF16)
    return high, (value - high.astype(F32)).astype(BF16)


def shifted(value):
    count = value.shape[0]
    column = lax.broadcasted_iota(jnp.int32, value.shape, 0) % WD
    left = jnp.where(column == 0, 0.0, pltpu.roll(value, 1, 0))
    right = jnp.where(column == WD - 1, 0.0, pltpu.roll(value, count - 1, 0))
    return left, value, right


def fill_patches(value, high_ref, low_ref):
    count = value.shape[0]
    for tap, moved in enumerate(shifted(value)):
        high, low = hi_lo(moved)
        high_ref[WD : WD + count, tap * C : (tap + 1) * C] = high
        low_ref[WD : WD + count, tap * C : (tap + 1) * C] = low


def clear_rim(ref, count):
    rim = jnp.zeros((WD,) + tuple(ref.shape[1:]), ref.dtype)
    ref[0:WD] = rim
    ref[WD + count : 2 * WD + count] = rim


def gathered(ref, count):
    return jnp.concatenate([ref[d * WD : d * WD + count, :] for d in range(3)], axis=1)


def conv(high_ref, low_ref, kernel_ref, thin_ref, slot, count):
    both = jnp.dot(gathered(high_ref, count), kernel_ref[slot], preferred_element_type=F32)
    rest = jnp.dot(low_ref[...], thin_ref[slot], preferred_element_type=F32)
    total = both[:, :C] + both[:, C:]
    for drop in range(3):
        total = total + rest[drop * WD : drop * WD + count, drop * C : (drop + 1) * C]
    return total


def logistic(value):
    return 1.0 / (1.0 + jnp.exp(-value))


def prepare_body(weight_ref, plain_ref, turned_ref, plain_thin, turned_thin, held, sems):
    slots = weight_ref.shape[0]
    for slot in range(slots):
        pltpu.make_async_copy(weight_ref.at[slot], held.at[slot], sems.at[slot]).start()

    def step(slot, carry):
        pltpu.make_async_copy(weight_ref.at[slot], held.at[slot], sems.at[slot]).wait()
        for tap in range(TAPS):
            block = held[slot, tap * C : (tap + 1) * C, :]
            high, low = hi_lo(block)
            plain_ref[slot, tap * C : (tap + 1) * C, 0:C] = high
            plain_ref[slot, tap * C : (tap + 1) * C, C:] = low
            drop, shift = tap // 3 * C, tap % 3 * C
            plain_thin[slot, shift : shift + C, drop : drop + C] = high
            high, low = hi_lo(block.T)
            back = TAPS - 1 - tap
            turned_ref[slot, back * C : (back + 1) * C, 0:C] = high
            turned_ref[slot, back * C : (back + 1) * C, C:] = low
            drop, shift = back // 3 * C, back % 3 * C
            turned_thin[slot, shift : shift + C, drop : drop + C] = high
        return carry

    lax.fori_loop(0, slots, step, 0)


def prepare(weights):
    slots = weights.shape[0]
    shape = jax.ShapeDtypeStruct((slots, DEPTH, 2 * C), BF16)
    thin = jax.ShapeDtypeStruct((slots, 3 * C, 3 * C), BF16)
    return pl.pallas_call(
        prepare_body,
        out_shape=[shape, shape, thin, thin],
        in_specs=[whole(pltpu.HBM)],
        out_specs=[whole()] * 4,
        scratch_shapes=[
            pltpu.VMEM((slots, DEPTH, C), F32),
            pltpu.SemaphoreType.DMA((slots,)),
        ],
        compiler_params=params(16),
        cost_estimate=cost(slots * DEPTH * C * 8, slots * DEPTH * C * 12),
    )(in_hbm(weights))


def pack_body(fresh_ref, carried_ref, target_ref, out_ref, sems):
    first = lax.axis_index("segment") == 0
    start = HALF * (1 - lax.axis_index("row"))
    top = out_ref.at[0:PART]
    from_fresh = pltpu.make_async_copy(fresh_ref.at[0], top, sems.at[0])
    from_carried = pltpu.make_async_copy(carried_ref, top, sems.at[0])
    others = (
        pltpu.make_async_copy(target_ref, out_ref.at[PART : 2 * PART], sems.at[1]),
        pltpu.make_async_copy(
            fresh_ref.at[1, rows(start, HALF)], out_ref.at[2 * PART :], sems.at[2]
        ),
    )

    @pl.when(first)
    def _():
        from_fresh.start()

    @pl.when(jnp.logical_not(first))
    def _():
        from_carried.start()

    for copy in others:
        copy.start()

    @pl.when(first)
    def _():
        from_fresh.wait()

    @pl.when(jnp.logical_not(first))
    def _():
        from_carried.wait()

    for copy in others:
        copy.wait()


def put_halves(ref, where, value):
    ref[0, where] = value[:, :C]
    ref[1, where] = value[:, C:]


def forward_loop(state_ref, high_ref, low_ref, kernel_ref, thin_ref, blocks_ref, count):
    clear_rim(high_ref, count)
    clear_rim(low_ref, count)

    def step(slot, carry):
        half = slot % 2
        source = state_ref[1 - half]
        fill_patches(source * logistic(source), high_ref, low_ref)
        state_ref[half] = state_ref[half] + conv(high_ref, low_ref, kernel_ref, thin_ref, slot, count)
        return carry

    lax.fori_loop(0, 2 * blocks_ref[0], step, 0)


def forward_crop(blocks_ref, own_ref, other_ref, kernel_ref, thin_ref, state, high, low):
    row = lax.axis_index("row")
    put_halves(state, rows(OWN * row, OWN), own_ref[0 : OWN * WD])
    put_halves(state, rows(OWN * (1 - row), OWN), other_ref[0 : OWN * WD])
    forward_loop(state, high, low, kernel_ref, thin_ref, blocks_ref, CROP)


def is_final():
    return lax.axis_index("segment") == lax.axis_size("segment") - 1


def forward_full_body(
    blocks_ref, own_ref, other_ref, kernel_ref, thin_ref, out_ref, state, high, low
):
    @pl.when(jnp.logical_not(is_final()))
    def _():
        forward_crop(
            blocks_ref, own_ref, other_ref, kernel_ref, thin_ref, state, high, low
        )
        part = rows(HALF * lax.axis_index("row"), WINDOW)
        out_ref[:, :C] = state[0, part]
        out_ref[:, C:] = state[1, part]


def forward_window_body(
    blocks_ref, came_ref, fresh_ref, other_ref, kernel_ref, thin_ref, out_ref, state, high, low
):
    row = lax.axis_index("row")
    first = lax.axis_index("segment") == 0

    @pl.when(first)
    def _():
        put_halves(state, rows(HALF * row, OWN), fresh_ref[1])
        put_halves(state, rows(OWN * (1 - row), HALF), other_ref[2 * PART :])

    @pl.when(jnp.logical_not(first))
    def _():
        put_halves(state, pl.ds(0, WINDOW * WD), came_ref[...])

    forward_loop(state, high, low, kernel_ref, thin_ref, blocks_ref, WINDOW * WD)
    part = rows(HALF * row, OWN)
    out_ref[:, :C] = state[0, part]
    out_ref[:, C:] = state[1, part]


def clear_picked(picked, blocks_ref):
    @pl.when(blocks_ref[0] < 2)
    def _():
        picked[2] = jnp.zeros((2, CROP, C), F32)
        picked[3] = jnp.zeros((2, CROP, C), F32)


def backward_step(slot, half, state, grads, kernels, pads, picked):
    plain_ref, turned_ref, plain_thin, turned_thin = kernels
    source_high, source_low, grad_high, grad_low = pads
    source = state[1 - half]
    grad = grads[half]
    gate = logistic(source)
    field = source * gate
    fill_patches(field, source_high, source_low)
    fill_patches(grad, grad_high, grad_low)
    if picked is not None:
        picked[slot, 0] = field
        picked[slot, 1] = grad
    state[half] = state[half] - conv(
        source_high, source_low, plain_ref, plain_thin, slot, CROP
    )
    slope = gate * (1.0 + source * (1.0 - gate))
    grads[1 - half] = grads[1 - half] + slope * conv(
        grad_high, grad_low, turned_ref, turned_thin, slot, CROP
    )


def backward_loop(state, grads, kernels, blocks_ref, pads, picked, lowest):
    for ref in pads:
        clear_rim(ref, CROP)
    clear_picked(picked, blocks_ref)
    top = 2 * blocks_ref[0] - 1

    def step(turn, carry):
        slot = top - turn
        backward_step(slot, slot % 2, state, grads, kernels, pads, picked)
        return carry

    lax.fori_loop(0, top + 1 - lowest, step, 0)


def crossing(row):
    return 2 * row + lax.axis_index("dp") % 2


def hand_out(picked, out_ref):
    place = crossing(lax.axis_index("row"))
    for turn in range(2):
        out_ref[turn] = picked[(place + turn) % 4]


def backward_full_body(
    blocks_ref, own_ref, other_ref, plain, turned, plain_thin, turned_thin, out_ref, *rest
):
    kernels = (plain, turned, plain_thin, turned_thin)
    pair_ref, (state, grads, picked), pads = rest[0], rest[1:4], rest[4:]
    row = lax.axis_index("row")
    for ref, index in ((state, 0), (grads, 1)):
        put_halves(ref, rows(OWN * row, OWN), own_ref[index])
        put_halves(ref, rows(OWN * (1 - row), OWN), other_ref[index])
    backward_loop(state, grads, kernels, blocks_ref, pads, picked, 0)
    for ref, index in ((state, 0), (grads, 1)):
        out_ref[index, :, :C] = ref[0]
        out_ref[index, :, C:] = ref[1]
    hand_out(picked, pair_ref)


def backward_near_body(
    blocks_ref,
    came_ref,
    own_ref,
    target_ref,
    other_ref,
    plain,
    turned,
    plain_thin,
    turned_thin,
    mid_ref,
    *rest,
):
    kernels = (plain, turned, plain_thin, turned_thin)
    pair_ref, (state, grads, picked) = rest[0], rest[1:4]
    pads, crop_pads = rest[4:8], rest[8:]
    row = lax.axis_index("row")
    final = is_final()

    @pl.when(final)
    def _():
        forward_crop(blocks_ref, own_ref, other_ref, plain, plain_thin, state, *crop_pads)
        put_halves(grads, rows(OWN * row, OWN), target_ref[...])
        put_halves(grads, rows(OWN * (1 - row), OWN), other_ref[PART : 2 * PART])
        grads[...] = state[...] - grads[...]

    @pl.when(jnp.logical_not(final))
    def _():
        put_halves(state, pl.ds(0, CROP), came_ref[0])
        put_halves(grads, pl.ds(0, CROP), came_ref[1])

    backward_loop(state, grads, kernels, blocks_ref, pads, picked, 1)
    source = state[1]
    picked[0, 0] = source * logistic(source)
    picked[0, 1] = grads[0]
    hand_out(picked, pair_ref)
    mid_ref[0] = state[...]
    mid_ref[1] = grads[...]


def backward_tail_body(
    mid_ref, plain, turned, plain_thin, turned_thin, out_ref, state, grads, *pads
):
    kernels = (plain, turned, plain_thin, turned_thin)
    state[...] = mid_ref[0]
    grads[...] = mid_ref[1]
    for ref in pads:
        clear_rim(ref, CROP)
    backward_step(0, 0, state, grads, kernels, pads, None)
    part = rows(OWN * lax.axis_index("row"), OWN)
    for ref, index in ((state, 0), (grads, 1)):
        out_ref[index, :, :C] = ref[0, part]
        out_ref[index, :, C:] = ref[1, part]


def forward_scratch(count):
    return [
        pltpu.VMEM((2, count, C), F32),
        pltpu.VMEM((count + 2 * WD, 3 * C), BF16),
        pltpu.VMEM((count + 2 * WD, 3 * C), BF16),
    ]


def pad_scratch(number):
    return [pltpu.VMEM((CROP + 2 * WD, 3 * C), BF16)] * number


def backward_scratch():
    return [
        pltpu.VMEM((2, CROP, C), F32),
        pltpu.VMEM((2, CROP, C), F32),
        pltpu.VMEM((4, 2, CROP, C), F32),
    ] + pad_scratch(4)


def kernel_grad(crop_ref, turn, high_ref, low_ref):
    fill_patches(crop_ref[turn, 0], high_ref, low_ref)
    high, low = hi_lo(crop_ref[turn, 1].T)
    both = jnp.dot(
        jnp.concatenate([high, low], axis=0),
        gathered(high_ref, CROP),
        preferred_element_type=F32,
    )
    rest = jnp.dot(high, gathered(low_ref, CROP), preferred_element_type=F32)
    return both[:C] + (both[C:] + rest)


def early_grad_body(crop_ref, out_ref, *pads):
    for turn in range(2):
        for ref in pads[2 * turn : 2 * turn + 2]:
            clear_rim(ref, CROP)
        out_ref[turn] = kernel_grad(crop_ref, turn, *pads[2 * turn : 2 * turn + 2])


def late_grad_body(scale, share, crop_ref, early_ref, *refs):
    outs, pads, (total_ref, held) = refs[:8], refs[8:12], refs[12:]
    here = crossing(lax.axis_index("row"))
    odd = (lax.axis_index("dp") // 2) % 2
    for turn in range(2):
        keep_ref, side_ref, along_ref, slant_ref = outs[4 * turn : 4 * turn + 4]
        for ref in pads[2 * turn : 2 * turn + 2]:
            clear_rim(ref, CROP)
        total = kernel_grad(crop_ref, turn, *pads[2 * turn : 2 * turn + 2])
        total = (total + early_ref[turn]) * scale
        for tap in range(TAPS):
            total_ref[turn, tap * C : (tap + 1) * C, :] = total[:, tap * C : (tap + 1) * C].T
        for along in range(8):
            for place in range(4):
                start = share * (16 * (place // 2) + 2 * along + place % 2)
                held[turn, along, place] = total_ref[turn, start : start + share]
        step = 1 - 2 * turn
        mine = (here, (here + 4 + step) % 4)
        theirs = ((here + 4 - step) % 4, (here + 4 - 2 * step) % 4)
        for pair in range(4):
            for place in range(2):
                at = slice(place * share, (place + 1) * share)
                keep_ref[pair, at] = held[turn, 2 * pair + odd, mine[place]]
                side_ref[pair, at] = held[turn, 2 * pair + odd, theirs[place]]
                along_ref[pair, at] = held[turn, 2 * pair + 1 - odd, mine[place]]
                slant_ref[pair, at] = held[turn, 2 * pair + 1 - odd, theirs[place]]


def fold_pair_body(share, *refs):
    parts, outs = refs[:8], refs[8:]
    here = lax.axis_index("dp") // 4
    for by, ref in enumerate(outs):
        pair = (here + by) % 4
        for turn in range(2):
            keep, side, along, slant = (part[pair] for part in parts[4 * turn : 4 * turn + 4])
            ref[2 * turn * share : 2 * (turn + 1) * share] = (keep + side) + (along + slant)


def fold_body(share, *refs):
    parts, (keep_ref, up_ref, down_ref) = refs[:4], refs[4:]
    total = (parts[0][...] + parts[1][...]) + (parts[2][...] + parts[3][...])
    keep_ref[0] = total[0:share]
    up_ref[...] = total[share : 2 * share]
    keep_ref[1] = total[2 * share : 3 * share]
    down_ref[...] = total[3 * share :]


def settle_body(keep_ref, up_ref, down_ref, out_ref, held):
    here = crossing(lax.axis_index("row"))
    held[here] = keep_ref[0]
    held[(here + 1) % 4] = keep_ref[1]
    held[(here + 3) % 4] = up_ref[...]
    held[(here + 2) % 4] = down_ref[...]
    for slot in range(4):
        out_ref[slot // 2, :, slot % 2, :] = held[slot]


def per_device(fresh, target, carried, returning, weights, section_blocks):
    tick_count = fresh.shape[0]
    cells = (
        tick_count
        * fresh.shape[1]
        * lax.axis_size("dp")
        * fresh.shape[2]
        * lax.axis_size("row")
        * fresh.shape[3]
    )
    segments = lax.axis_size("segment")
    dp_count = lax.axis_size("dp")
    rungs = dp_count // 2
    share = DEPTH // (2 * dp_count)
    flat = OWN * WD
    fresh = fresh.reshape(2, flat, 2 * C)
    target = target.reshape(flat, 2 * C)
    carried = carried.reshape(flat, 2 * C)
    returning = returning.reshape(2, flat, 2 * C)
    weights = weights.reshape(4, DEPTH, C)
    swap = [(0, 1), (1, 0)]
    onward = [(i, i + 1) for i in range(segments - 1)]
    homeward = [(i + 1, i) for i in range(segments - 1)]

    def neighbour(rung, conv):
        step = 1 - 2 * ((rung + conv) % 2)
        return (rung + step) % rungs

    def route(goal):
        pairs = []
        for place in range(4):
            for rung in range(rungs):
                there, above = goal(place, rung)
                pairs.append(
                    tuple(
                        (spot % 4 // 2) * dp_count + 2 * (level % rungs) + spot % 2
                        for spot, level in ((place, rung), (there, above))
                    )
                )
        return pairs

    def send(value, goal):
        return lax.ppermute(value, ("row", "dp"), route(goal))

    conv_flops = 6 * DEPTH * C
    other_pair = lax.ppermute(returning, "row", swap)
    (packed,) = call(
        pack_body,
        [((FULL + HALF) * WD, 2 * C)],
        [pltpu.SemaphoreType.DMA((3,))],
        tuple(in_hbm(value) for value in (fresh, carried, target)),
        8,
        1 << 20,
        space=pltpu.HBM,
    )
    other_pack = lax.ppermute(packed, "row", swap)
    plain, turned, plain_thin, turned_thin = prepare(weights)
    forth, back_kernels = (plain, plain_thin), (plain, turned, plain_thin, turned_thin)

    sent, early_pair = call(
        backward_full_body,
        [(2, CROP, 2 * C), (2, 2, CROP, C)],
        backward_scratch(),
        (section_blocks, returning, other_pair, *back_kernels),
        24,
        8 * conv_flops * CROP,
        smem=(0,),
    )
    came_back = lax.ppermute(sent, "segment", homeward)
    (early_grad,) = call(
        early_grad_body,
        [(2, C, DEPTH)],
        pad_scratch(4),
        (early_pair,),
        24,
        2 * conv_flops * CROP,
    )
    (made,) = call(
        forward_full_body,
        [(WINDOW * WD, 2 * C)],
        forward_scratch(CROP),
        (section_blocks, packed, other_pack, *forth),
        24,
        4 * conv_flops * CROP,
        smem=(0,),
    )
    mid, late_pair = call(
        backward_near_body,
        [(2, 2, CROP, C), (2, 2, CROP, C)],
        backward_scratch() + pad_scratch(2),
        (section_blocks, came_back, packed, target, other_pack, *back_kernels),
        24,
        6 * conv_flops * CROP,
        smem=(0,),
    )
    parts = call(
        functools.partial(late_grad_body, 1.0 / math.sqrt(cells), share),
        [(4, 2 * share, C)] * 8,
        pad_scratch(4)
        + [pltpu.VMEM((2, DEPTH, C), F32), pltpu.VMEM((2, rungs, 4, share, C), F32)],
        (late_pair, early_grad),
        24,
        2 * conv_flops * CROP,
    )
    parts = list(parts)
    came = [parts[0], None, None, None, parts[4], None, None, None]
    came[3] = send(parts[7], lambda x, z: (x + 1, neighbour(z, x + 1)))
    came[7] = send(parts[3], lambda x, z: (x - 1, neighbour(z, x)))
    came[1] = send(parts[5], lambda x, z: (x + 1, z))
    came[5] = send(parts[1], lambda x, z: (x - 1, z))
    came[2] = send(parts[2], lambda x, z: (x, neighbour(z, x)))
    came[6] = send(parts[6], lambda x, z: (x, neighbour(z, x + 1)))
    came_on = lax.ppermute(made, "segment", onward)
    (back,) = call(
        backward_tail_body,
        [(2, flat, 2 * C)],
        backward_scratch()[:2] + pad_scratch(4),
        (mid, *back_kernels),
        24,
        2 * conv_flops * CROP,
    )
    paired = call(
        functools.partial(fold_pair_body, share),
        [(4 * share, C)] * 4,
        [],
        tuple(came),
        8,
        1 << 20,
    )
    spread = [paired[0]]
    for by in (2, 1, 3):
        spread.append(send(paired[by], lambda x, z, by=by: (x, z + 2 * by)))
    (produced,) = call(
        forward_window_body,
        [(flat, 2 * C)],
        forward_scratch(WINDOW * WD),
        (section_blocks, came_on, fresh, other_pack, *forth),
        24,
        4 * conv_flops * WINDOW * WD,
        smem=(0,),
    )
    keep, up, down = call(
        functools.partial(fold_body, share),
        [(2, share, C), (share, C), (share, C)],
        [],
        tuple(spread),
        8,
        1 << 20,
    )
    up = send(up, lambda x, z: (x + 1, z))
    down = send(down, lambda x, z: (x - 1, z))
    (grad_weights,) = call(
        settle_body,
        [(2, share, 2, C)],
        [pltpu.VMEM((4, share, C), F32)],
        (keep, up, down),
        8,
        1 << 20,
    )
    return (
        grad_weights.transpose(0, 2, 1, 3)[None],
        produced.reshape(1, 1, OWN, WD, 2 * C),
        back.reshape(1, 2, 1, OWN, WD, 2 * C),
    )


def solution(mesh):
    return jax.shard_map(
        per_device,
        mesh=mesh,
        in_specs=(
            P(None, "dp", "row", None, None),
            P(None, "dp", "row", None, None),
            P("segment", "dp", "row", None, None),
            P("segment", None, "dp", "row", None, None),
            P("segment", None, None, None, None),
            P("segment"),
        ),
        out_specs=(
            P("segment", None, None, ("row", "dp"), None),
            P("segment", "dp", "row", None, None),
            P("segment", None, "dp", "row", None, None),
        ),
        check_vma=False,
    )
```
